32 devices in a mesh: wide: 8 (over z, y), narrow: 4 (over x, core).
Axes of the slice: x: 2, y: 2, z: 4, core: 2. Of those that a mesh axis runs over, the one named last changes fastest.
Arguments:
- tokens: bfloat16 [4096, 1152], P(('wide', 'narrow'))
- norm_gain: float32 [1152], replicated, may hold values from 0.5 to 1.5
- w_in: bfloat16 [1152, 4608], P(None, ('wide', 'narrow')), may hold values from -0.1875 to 0.1875
- conv_w: bfloat16 [4, 2304], P(None, ('wide', 'narrow')), may hold values from -3 to 3
- conv_b: bfloat16 [2304], P(('wide', 'narrow')), may hold values from -4 to 4
- w_x: bfloat16 [2304, 104], P(('wide', 'narrow')), may hold values from -0.125 to 0.125
- w_dt: bfloat16 [72, 2304], P(None, ('wide', 'narrow')), may hold values from -0.75 to 0.75
- dt_bias: bfloat16 [2304], P(('wide', 'narrow')), may hold values from -6 to -2
- a_log: bfloat16 [2304, 16], P(('wide', 'narrow')), may hold values from 0 to 2.765625
- d_skip: bfloat16 [2304], P(('wide', 'narrow')), may hold values from 0.5 to 1.5
- w_out: bfloat16 [2304, 1152], P(('wide', 'narrow')), may hold values from -0.125 to 0.125
- moe_gain: float32 [1152], replicated, may hold values from 0.5 to 1.5
- w_router: bfloat16 [1152, 3], replicated, may hold values from -0.09375 to 0.09375
- w_up: bfloat16 [3, 1152, 3072], P(None, None, ('wide', 'narrow')), may hold values from -0.1875 to 0.1875
- w_down: bfloat16 [3, 3072, 1152], P(None, ('wide', 'narrow')), may hold values from -0.3125 to 0.3125
- seq_lengths: int32 [32, 2], P(('wide', 'narrow')), may hold values from 16 to 112, as said below
- valid_counts: int32 [32], P(('wide', 'narrow')), may hold values from 32 to 128, as said below
- expert_ids: int32 [4096], P(('wide', 'narrow')), may hold values from 0 to 2
- out_grad: bfloat16 [4096, 1152], P(('wide', 'narrow')), may hold values from -6 to 6
Outputs:
- layer_out: bfloat16 [4096, 1152], P(('wide', 'narrow'))
- grad_tokens: float32 [4096, 1152], P(('wide', 'narrow'))
- grad_norm_gain: float32 [1152], replicated
- grad_w_in: float32 [1152, 4608], P(None, ('wide', 'narrow'))
- grad_conv_w: float32 [4, 2304], P(None, ('wide', 'narrow'))
- grad_conv_b: float32 [2304], P(('wide', 'narrow'))
- grad_w_x: float32 [2304, 104], P(('wide', 'narrow'))
- grad_w_dt: float32 [72, 2304], P(None, ('wide', 'narrow'))
- grad_dt_bias: float32 [2304], P(('wide', 'narrow'))
- grad_a_log: float32 [2304, 16], P(('wide', 'narrow'))
- grad_d_skip: float32 [2304], P(('wide', 'narrow'))
- grad_w_out: float32 [2304, 1152], P(('wide', 'narrow'))
- grad_moe_gain: float32 [1152], replicated
- grad_w_router: float32 [1152, 3], replicated
- grad_w_up: float32 [3, 1152, 3072], P(None, None, ('wide', 'narrow'))
- grad_w_down: float32 [3, 3072, 1152], P(None, ('wide', 'narrow'))
- token_rms: float32 [3], replicated
The draws below stay inside these ranges and needn't reach their ends.
Inputs may be any that keep to these rules, and one draw needn't show every extreme that they name: `seq_lengths`: each device holds 2 sequences packed from its first slot, whose lengths sum to its valid count; on one device they are 112 and 16. `valid_counts`: each equals the sum of that device's sequence lengths; one device is full and one holds 32.
All inputs are finite; a program needn't handle non-finite values.
Results may differ from the reference program's by a relative error of at most 0.012.
Values may be sent and summed in bfloat16 or wider, within the bound.
A program may use at most 448 MiB of HBM per device.

```python
import jax
import jax.numpy as jnp
from jax import lax

D = 1152
DI = 2304
NS = 16
KC = 4
R = 72
FF = 3072
EXPERTS = 3
TOK_DEV = 128
LEN_MIN = 16
TOKENS = 4096
N_WIDE = 8
N_NARROW = 4


def packing(key):
    base_key = jax.random.fold_in(key, 11)
    first_key, second_key, third_key, fourth_key = jax.random.split(base_key, 4)
    devices = N_WIDE * N_NARROW
    counts = jax.random.randint(first_key, (devices,), TOK_DEV // 4, TOK_DEV + 1)
    full_device = jax.random.randint(second_key, (), 0, devices)
    short_device = (full_device + 1 + jax.random.randint(third_key, (), 0, devices - 1)) % devices
    places = jnp.arange(devices, dtype=jnp.int32)
    counts = jnp.where(places == full_device, TOK_DEV, jnp.where(places == short_device, TOK_DEV // 4, counts))
    leading = jax.random.randint(fourth_key, (devices,), LEN_MIN, counts - LEN_MIN + 1)
    leading = jnp.where(places == full_device, TOK_DEV - LEN_MIN, leading)
    lengths = jnp.stack([leading, counts - leading], axis=1)
    return (lengths.astype(jnp.int32), counts.astype(jnp.int32))


def draw_seq_lengths(key, part):
    return packing(key)[0]


def draw_valid_counts(key, part):
    return packing(key)[1]


def draw_tokens(key, part):
    all_rows = TOK_DEV * N_WIDE * N_NARROW
    position = jnp.arange(all_rows, dtype=jnp.float32)[:, None] / all_rows
    values = jax.random.normal(key, (all_rows, D), jnp.float32) * (1.0 + 2.0 * position)
    return values.astype(jnp.bfloat16)


def set_ends(array, own_key, smallest, high):
    place = [jax.random.randint(jax.random.fold_in(own_key, axis), (), 0, length) for axis, length in enumerate(array.shape)]
    widest = array.shape.index(max(array.shape))
    next_to = place[:widest] + [(place[widest] + 1) % array.shape[widest]] + place[widest + 1:]
    return array.at[tuple(place)].set(smallest).at[tuple(next_to)].set(high)


def level_of(key, dims, cuts, low, high):
    def one(dim, shards_of):
        steps = jax.random.uniform(jax.random.fold_in(jax.random.fold_in(key, 6), dim), (shards_of,), jnp.float32, low / len(cuts), high / len(cuts))
        return jnp.repeat(jnp.exp(steps), dims[dim] // shards_of).reshape((-1,) + (1,) * (len(dims) - dim - 1))

    loudness = one(*cuts[0])
    for cut in cuts[1:]:
        loudness = loudness * one(*cut)
    return loudness


def centred(rng, extent, deviation, reach, pieces=(), held_as=jnp.bfloat16):
    values = deviation * jax.random.normal(rng, extent, jnp.float32)
    if pieces:
        values = values * level_of(rng, extent, pieces, -0.22, 0.18)
    return jnp.clip(values, -reach, reach).astype(held_as)


def setup_inputs(seed: int = 0) -> dict:
    key_of = jax.random.split(jax.random.key(seed), 20)
    return {
        "tokens": draw_tokens(jax.random.fold_in(key_of[19], 71), 0),
        "norm_gain": jnp.clip(1.0 + 0.1 * jax.random.normal(key_of[1], (D,), jnp.float32), 0.5, 1.5),
        "w_in": centred(key_of[2], (D, 2 * DI), D ** -0.5, 0.1875, ((1, 32),)),
        "conv_w": centred(key_of[3], (KC, DI), KC ** -0.5, 3.0, ((1, 32),)),
        "conv_b": centred(key_of[4], (DI,), 0.3, 4.0, ((0, 32),)),
        "w_x": centred(key_of[5], (DI, R + 2 * NS), DI ** -0.5, 0.125, ((0, 32),)),
        "w_dt": centred(key_of[6], (R, DI), R ** -0.5, 0.75, ((1, 32),)),
        "dt_bias": jnp.clip(-6.0 + 4.0 * jax.random.uniform(key_of[7], (DI,), jnp.float32) ** level_of(key_of[7], (DI,), ((0, 32),), -0.2, 0.2), -6.0, -2.0).astype(jnp.bfloat16),
        "a_log": jnp.clip(2.765625 * jax.random.uniform(key_of[8], (DI, NS), jnp.float32) ** level_of(key_of[8], (DI, NS), ((0, 32),), -0.2, 0.2), 0.0, 2.765625).astype(jnp.bfloat16),
        "d_skip": jnp.clip(0.5 + 1.0 * jax.random.uniform(key_of[9], (DI,), jnp.float32) ** level_of(key_of[9], (DI,), ((0, 32),), -0.2, 0.2), 0.5, 1.5).astype(jnp.bfloat16),
        "w_out": centred(key_of[10], (DI, D), DI ** -0.5, 0.125, ((0, 32),)),
        "moe_gain": jnp.clip(1.0 + 0.1 * jax.random.normal(key_of[11], (D,), jnp.float32), 0.5, 1.5),
        "w_router": centred(key_of[12], (D, EXPERTS), (4 * D) ** -0.5, 0.09375),
        "w_up": centred(key_of[13], (EXPERTS, D, FF), D ** -0.5, 0.1875, ((2, 32),)),
        "w_down": centred(key_of[14], (EXPERTS, FF, D), (FF // 8) ** -0.5, 0.3125, ((1, 32),)),
        "seq_lengths": draw_seq_lengths(jax.random.fold_in(key_of[19], 71), 0),
        "valid_counts": draw_valid_counts(jax.random.fold_in(key_of[19], 71), 0),
        "expert_ids": set_ends(jax.random.randint(key_of[17], (TOKENS,), 0, EXPERTS), jax.random.fold_in(key_of[17], 1), 0, EXPERTS - 1).astype(jnp.int32),
        "out_grad": centred(key_of[18], (TOKENS, D), 1.0, 6.0, ((0, 32),)),
    }


EPS = 1e-05
PRECISE = lax.Precision.HIGHEST

@jax.custom_vjp
def low(v):
    return lax.optimization_barrier(v.astype(jnp.bfloat16)).astype(jnp.float32)

@jax.custom_vjp
def low_back(v):
    return v

def low_keep(v):
    return (low(v), None)

def low_pass(kept, grad):
    return (grad,)

def back_keep(v):
    return (v, None)

def back_low(kept, grad):
    return (low(grad),)
low.defvjp(low_keep, low_pass)
low_back.defvjp(back_keep, back_low)

def rms_norm(values, scale_gain):
    return values * lax.rsqrt(lax.optimization_barrier(jnp.mean(values * values, axis=-1, keepdims=True)) + EPS) * scale_gain

def matmul_high(left, right):
    return jnp.dot(left, right, precision=PRECISE)

def gelu_tanh(values):
    return jax.nn.gelu(values, approximate=True)

def conv_taps(signal, tap_weights, tap_bias, segment):
    total_sum = tap_bias + tap_weights[0] * signal
    for lag_index in range(1, tap_weights.shape[0]):
        shifted = jnp.concatenate([jnp.zeros((lag_index, signal.shape[1]), signal.dtype), signal[:-lag_index]], axis=0)
        earlier_seg = jnp.concatenate([jnp.full((lag_index,), -1, jnp.int32), segment[:-lag_index]], axis=0)
        same_seg = (earlier_seg == segment).astype(signal.dtype)[:, None]
        total_sum = total_sum + tap_weights[lag_index] * shifted * same_seg
    return total_sum

def device_scan(a_neg, inputs):
    delta, conved, input_b, output_c, keep_state = inputs

    def advance(state, position):
        rate_row, conved_row, b_row, c_row, keep_row = position
        state = state * keep_row * jnp.exp(rate_row[:, None] * a_neg) + (rate_row * conved_row)[:, None] * b_row[None, :]
        return (state, jnp.dot(state, c_row, precision=PRECISE))
    start_state = jnp.zeros(a_neg.shape, jnp.float32)
    _, scanned = lax.scan(advance, start_state, (delta, conved, input_b, output_c, keep_state))
    return scanned

def reference(tokens, norm_gain, w_in, conv_w, conv_b, w_x, w_dt, dt_bias, a_log, d_skip, w_out, moe_gain, w_router, w_up, w_down, seq_lengths, valid_counts, expert_ids, out_grad):
    blocks = N_WIDE * N_NARROW
    places = jnp.arange(TOK_DEV, dtype=jnp.int32)
    bounds = jnp.cumsum(seq_lengths, axis=1).astype(jnp.int32)
    segment = lax.optimization_barrier(jnp.sum((places[None, :, None] >= bounds[:, None, :]).astype(jnp.int32), axis=2))
    opening = (places[None, :] == 0) | jnp.any(places[None, :, None] == bounds[:, None, :], axis=2)
    keep_state = 1.0 - opening.astype(jnp.float32)
    valid_rows = (places[None, :] < valid_counts[:, None]).astype(jnp.float32).reshape(TOKENS, 1)
    onehot = (expert_ids[:, None] == jnp.arange(EXPERTS, dtype=jnp.int32)[None, :]).astype(jnp.float32)

    def forward(stream, gain_one, win, conv_taps_w, conv_bias, wx_full, wdt_full, dt_shift, alog_full, skip_full, wout_full, gain_two, router_full, up_full, down_full):
        normed = low(rms_norm(stream, gain_one))
        projected = low_back(matmul_high(normed, win))
        source = projected[:, :DI]
        gate_in = projected[:, DI:]
        conv_blocks = jax.vmap(conv_taps, in_axes=(0, None, None, 0))(source.reshape(blocks, TOK_DEV, DI), conv_taps_w, conv_bias, segment)
        conved = jax.nn.silu(conv_blocks).reshape(TOKENS, DI)
        conved_low = low(conved)
        expanded = low_back(matmul_high(conved_low, wx_full))
        rate_in = low(expanded[:, :R])
        input_b = expanded[:, R:R + NS]
        output_c = expanded[:, R + NS:]
        delta = jax.nn.softplus(low_back(matmul_high(rate_in, wdt_full)) + dt_shift)
        a_neg = -jnp.exp(alog_full)

        def one_block(inputs):
            return device_scan(a_neg, inputs)
        scanned = lax.map(jax.checkpoint(one_block), (delta.reshape(blocks, TOK_DEV, DI), conved.reshape(blocks, TOK_DEV, DI), input_b.reshape(blocks, TOK_DEV, NS), output_c.reshape(blocks, TOK_DEV, NS), keep_state))
        scanned = scanned.reshape(TOKENS, DI)
        gated = low((scanned + skip_full * conved) * jax.nn.silu(gate_in))
        branch_one = valid_rows * low_back(matmul_high(gated, wout_full))
        middle = stream + branch_one
        moe_in = low(rms_norm(middle, gain_two))
        router_probs = jax.nn.softmax(low_back(matmul_high(moe_in, router_full)), axis=-1)
        chosen = lax.optimization_barrier(jnp.sum(router_probs * onehot, axis=-1, keepdims=True))
        picked = jnp.zeros_like(stream)
        for expert_index in range(EXPERTS):
            hidden = low(gelu_tanh(low_back(matmul_high(moe_in, up_full[expert_index]))))
            picked = picked + onehot[:, expert_index:expert_index + 1] * low_back(matmul_high(hidden, down_full[expert_index]))
        branch_two = valid_rows * chosen * picked
        return (middle + branch_two, (branch_one, branch_two))
    floats = (tokens.astype(jnp.float32), norm_gain.astype(jnp.float32), w_in.astype(jnp.float32), conv_w.astype(jnp.float32), conv_b.astype(jnp.float32), w_x.astype(jnp.float32), w_dt.astype(jnp.float32), dt_bias.astype(jnp.float32), a_log.astype(jnp.float32), d_skip.astype(jnp.float32), w_out.astype(jnp.float32), moe_gain.astype(jnp.float32), w_router.astype(jnp.float32), w_up.astype(jnp.float32), w_down.astype(jnp.float32))
    result, pullback, branches = jax.vjp(forward, *floats, has_aux=True)
    gradients = pullback(out_grad.astype(jnp.float32))
    count_all = jnp.sum(valid_counts).astype(jnp.float32) * D
    token_rms = jnp.sqrt(jnp.stack([jnp.sum(valid_rows * result * result), jnp.sum(branches[0] * branches[0]), jnp.sum(branches[1] * branches[1])]) / count_all)
    return (result.astype(jnp.bfloat16), gradients[0], gradients[1], gradients[2], gradients[3], gradients[4], gradients[5], gradients[6], gradients[7], gradients[8], gradients[9], gradients[10], gradients[11], gradients[12], gradients[13], gradients[14], token_rms)
```

```python
from functools import partial

import jax
import jax.numpy as jnp
from jax import lax
from jax.experimental import pallas as pl
from jax.experimental.pallas import tpu as pltpu
from jax.sharding import PartitionSpec as P

EPS = 1e-05
LOW = jnp.bfloat16
F32 = jnp.float32
LANES = 128
CH = 384


def dot_nn(a, b):
    return lax.dot_general(a, b, (((1,), (0,)), ((), ())), preferred_element_type=F32)


def dot_nt(a, b):
    return lax.dot_general(a, b, (((1,), (1,)), ((), ())), preferred_element_type=F32)


def dot_tn(a, b):
    return lax.dot_general(a, b, (((0,), (0,)), ((), ())), preferred_element_type=F32)


def sigmoid(v):
    return 1.0 / (1.0 + jnp.exp(-v))


def softplus(v):
    return jnp.maximum(v, 0.0) + jnp.log1p(jnp.exp(-jnp.abs(v)))


class Small:
    def __init__(self, rank, states, taps):
        self.rank, self.states, self.taps = rank, states, taps
        self.alog = -(-rank // 8) * 8
        self.conv = self.alog + states
        self.bias = self.conv + taps
        self.rate = self.bias + 1
        self.skip = self.bias + 2
        self.end = self.bias + 3


def row_iota(shape):
    return lax.broadcasted_iota(jnp.int32, shape, 0)


def lane_iota(shape):
    return lax.broadcasted_iota(jnp.int32, shape, 1)


def segments(lens_ref, shape):
    first = lens_ref[0]
    second = first + lens_ref[1]
    t = row_iota(shape)
    seg = (t >= first).astype(jnp.int32) + (t >= second).astype(jnp.int32)
    opening = (t == 0) | (t == first) | (t == second)
    return t, seg, opening


def lag_masks(lens_ref, shape, taps):
    first = lens_ref[0]
    second = first + lens_ref[1]
    t = row_iota(shape)
    masks = [None]
    for lag in range(1, taps):
        e = t - lag
        same = ((t >= first) == (e >= first)) & ((t >= second) == (e >= second)) & (e >= 0)
        masks.append(same)
    return masks


def conv_pre(src, prm, sm, masks):
    taps = sm.taps
    total = prm[sm.bias : sm.bias + 1, :] + prm[sm.conv : sm.conv + 1, :] * src
    for lag in range(1, taps):
        moved = jnp.where(masks[lag], pltpu.roll(src, lag, 0), 0.0)
        total = total + prm[sm.conv + lag : sm.conv + lag + 1, :] * moved
    return total


def params_of(small_ref, k):
    blk = small_ref[pl.ds(pl.multiple_of(k * CH, CH), CH), LANES : 2 * LANES]
    return jnp.transpose(blk.astype(F32))


def lanes3(v):
    return jnp.concatenate([v] * (CH // LANES), axis=1)


def fold3(v):
    out = v[:, 0:LANES]
    for i in range(1, CH // LANES):
        out = out + v[:, i * LANES : (i + 1) * LANES]
    return out


def spread(expanded, start, states, out_ref):
    rows = expanded.shape[0]
    for s in range(states):
        col = jnp.broadcast_to(expanded[:, start + s : start + s + 1], (rows, LANES))
        out_ref[pl.ds(s, rows, stride=states), :] = col


def rows_sum8(ref, rows):
    planes = []
    for i in range(CH // LANES):
        out = ref[i, pl.ds(0, rows, stride=8), :]
        for j in range(1, 8):
            out = out + ref[i, pl.ds(j, rows, stride=8), :]
        planes.append(out)
    return jnp.concatenate(planes, axis=1)


def put_planes(ref, at, v):
    for i in range(CH // LANES):
        ref[i, at, :] = v[:, i * LANES : (i + 1) * LANES]


def lane_chunk(k, base=0):
    return pl.ds(pl.multiple_of(base + k * CH, LANES), CH)


def row_chunk(k, base=0):
    return pl.ds(pl.multiple_of(base + k * CH, LANES), CH)


def norm_of(x, gain):
    r = lax.rsqrt(jnp.mean(x * x, axis=-1, keepdims=True) + EPS)
    return x * r * gain


def forward_chunk_conv(k, sm, lens_ref, normed_ref, win_ref, small_ref, src_ref, gate_ref, exp_acc, inner):
    normed = normed_ref[...]
    src = dot_nt(normed, win_ref[row_chunk(k), :])
    src_ref[:, lane_chunk(k)] = src
    gate_ref[:, lane_chunk(k)] = dot_nt(normed, win_ref[row_chunk(k, inner), :])
    prm = params_of(small_ref, k)
    masks = lag_masks(lens_ref, src.shape, sm.taps)
    pre = conv_pre(src, prm, sm, masks)
    conved = pre * sigmoid(pre)
    exp_acc[...] += dot_nn(conved.astype(LOW), small_ref[row_chunk(k), 0:LANES])
    return conved


def scan_forward(rows, dl_ref, dx_ref, a, bb_ref, states, cc_ref=None, yp_ref=None, hist_ref=None, dec_ref=None):
    def block(tb, h):
        t0 = pl.multiple_of(tb * 8, 8)
        d8 = dl_ref[pl.ds(t0, 8), :]
        x8 = dx_ref[pl.ds(t0, 8), :]
        for j in range(8):
            d = jnp.broadcast_to(d8[j : j + 1, :], (states, CH))
            x = jnp.broadcast_to(x8[j : j + 1, :], (states, CH))
            dec = jnp.exp(d * a)
            at = pl.ds(pl.multiple_of(t0 * states, 8 * states) + j * states, states)
            h = h * dec + x * lanes3(bb_ref[at, :])
            if hist_ref is not None:
                hist_ref[at, :] = h
                dec_ref[at, :] = dec
            if yp_ref is not None:
                p = h * lanes3(cc_ref[at, :])
                ps = p[0:8]
                for i in range(1, states // 8):
                    ps = ps + p[8 * i : 8 * i + 8]
                put_planes(yp_ref, pl.ds(pl.multiple_of(t0 * 8, 64) + j * 8, 8), ps)
        return h

    lax.fori_loop(0, rows // 8, block, jnp.zeros((states, CH), F32))


def mixer_forward_kernel(
    sm, inner,
    lens_ref, count_ref, tok_ref, gain_ref, win_ref, small_ref, wout_ref, gain2_ref,
    normed_ref, src_ref, gate_ref, lin_ref, ym_ref, exp_ref, gated_ref, middle_ref, moe_ref,
    conved_s, dl_s, dx_s, bb_s, cc_s, yp_s, acc_s,
):
    rows = tok_ref.shape[0]
    states = sm.states
    chunks = inner // CH
    tok = tok_ref[...].astype(F32)
    normed_ref[...] = norm_of(tok, gain_ref[...]).astype(LOW)
    exp_ref[...] = jnp.zeros_like(exp_ref)

    @pl.loop(0, chunks)
    def _(k):
        conved_s[:, lane_chunk(k)] = forward_chunk_conv(
            k, sm, lens_ref, normed_ref, win_ref, small_ref, src_ref, gate_ref, exp_ref, inner
        )

    expanded = exp_ref[...]
    lane = lane_iota((rows, LANES))
    rate = jnp.where(lane < sm.rank, expanded, 0.0).astype(LOW)
    spread(expanded, sm.rank, states, bb_s)
    spread(expanded, sm.rank + states, states, cc_s)
    acc_s[...] = jnp.zeros_like(acc_s)

    @pl.loop(0, chunks)
    def _(k):
        prm = params_of(small_ref, k)
        lin = dot_nt(rate, small_ref[row_chunk(k), LANES : 2 * LANES]) + prm[sm.rate : sm.rate + 1, :]
        lin_ref[:, lane_chunk(k)] = lin
        delta = softplus(lin)
        conved = conved_s[:, lane_chunk(k)]
        _, _, opening = segments(lens_ref, lin.shape)
        dl_s[...] = jnp.where(opening, 1e30, delta)
        dx_s[...] = delta * conved
        a = -jnp.exp(prm[sm.alog : sm.alog + states, :])
        scan_forward(rows, dl_s, dx_s, a, bb_s, states, cc_s, yp_s)
        ym = rows_sum8(yp_s, rows) + prm[sm.skip : sm.skip + 1, :] * conved
        ym_ref[:, lane_chunk(k)] = ym
        gate = gate_ref[:, lane_chunk(k)]
        gated = (ym * (gate * sigmoid(gate))).astype(LOW)
        gated_ref[:, lane_chunk(k)] = gated
        acc_s[...] += dot_nn(gated, wout_ref[row_chunk(k), :])

    valid = row_iota((rows, 1)) < count_ref[0]
    middle = tok + jnp.where(valid, acc_s[...], 0.0)
    middle_ref[...] = middle
    moe_ref[...] = norm_of(middle, gain2_ref[...]).astype(LOW)


def silu_grad(v, s):
    return s * (1.0 + v * (1.0 - s))


def norm_back(x, gain, grad):
    r = lax.rsqrt(jnp.mean(x * x, axis=-1, keepdims=True) + EPS)
    n = x * r
    q = grad * gain
    return r * (q - n * jnp.mean(q * n, axis=-1, keepdims=True)), grad * n


def scan_backward(rows, states, a, gs_ref, dx_ref, dt_ref, bb_ref, cc_ref, hist_ref, dec_ref, gcp_ref, gbp_ref, lbp_ref, amp_ref):
    blocks = rows // 8

    def fold8(p):
        out = p[0:8]
        for i in range(1, states // 8):
            out = out + p[8 * i : 8 * i + 8]
        return out

    def block(i, carry):
        back, total = carry
        tb = blocks - 1 - i
        t0 = pl.multiple_of(tb * 8, 8)
        g8 = gs_ref[pl.ds(t0, 8), :]
        x8 = dx_ref[pl.ds(t0, 8), :]
        d8 = dt_ref[pl.ds(t0, 8), :]
        for j in range(7, -1, -1):
            base = pl.multiple_of(t0 * states, 8 * states) + j * states
            at = pl.ds(base + states, states)
            prev = pl.ds(base, states)
            here = pl.ds(base, states)
            g = jnp.broadcast_to(g8[j : j + 1, :], (states, CH))
            x = jnp.broadcast_to(x8[j : j + 1, :], (states, CH))
            d = jnp.broadcast_to(d8[j : j + 1, :], (states, CH))
            adj = g * lanes3(cc_ref[here, :]) + back
            gcp_ref[here, :] += fold3(hist_ref[at, :] * g)
            gbp_ref[here, :] += fold3(adj * x)
            out8 = pl.ds(pl.multiple_of(t0 * 8, 64) + j * 8, 8)
            put_planes(lbp_ref, out8, fold8(adj * lanes3(bb_ref[here, :])))
            back = adj * dec_ref[here, :]
            m = back * hist_ref[prev, :]
            put_planes(amp_ref, out8, fold8(m * a))
            total = total + m * d
        return back, total

    zero = jnp.zeros((states, CH), F32)
    _, total = lax.fori_loop(0, blocks, block, (zero, zero))
    return total * a


def mixer_backward_kernel(
    sm, inner,
    lens_ref, count_ref, tok_ref, gain_ref, win_ref, small_ref, wout_ref, gain2_ref,
    normed_ref, src_ref, gate_ref, lin_ref, ym_ref, exp_ref, gated_ref, middle_ref, gmoe_ref, gout_ref,
    gtok_ref, gwin_ref, gsmall_ref, gwout_ref, ggain_ref, ggain2_ref,
    gmid_s, gmix_s, ggate_s, gconv_s, dl_s, dx_s, dt_s, gs_s, bb_s, cc_s, hist_s, dec_s, gcp_s, gbp_s, lbp_s, amp_s, grate_s, gnorm_s,
):
    rows = tok_ref.shape[0]
    states = sm.states
    chunks = inner // CH
    gout = gout_ref[...].astype(F32)
    gmid, prod = norm_back(middle_ref[...], gain2_ref[...], gmoe_ref[...].astype(F32))
    ggain2_ref[...] = jnp.sum(prod, axis=0, keepdims=True)
    gmid = gmid + gout
    gmid_s[...] = gmid
    valid = row_iota((rows, 1)) < count_ref[0]
    gmix_s[...] = jnp.where(valid, gmid, 0.0).astype(LOW)
    expanded = exp_ref[...]
    lane = lane_iota((rows, LANES))
    rate = jnp.where(lane < sm.rank, expanded, 0.0).astype(LOW)
    spread(expanded, sm.rank, states, bb_s)
    spread(expanded, sm.rank + states, states, cc_s)
    grate_s[...] = jnp.zeros_like(grate_s)
    gcp_s[...] = jnp.zeros_like(gcp_s)
    gbp_s[...] = jnp.zeros_like(gbp_s)
    gnorm_s[...] = jnp.zeros_like(gnorm_s)
    hist_s[0:states, :] = jnp.zeros((states, CH), F32)

    @pl.loop(0, chunks)
    def _(k):
        gmix = gmix_s[...]
        gg = dot_nt(gmix, wout_ref[row_chunk(k), :])
        gwout_ref[row_chunk(k), :] = dot_tn(gated_ref[:, lane_chunk(k)], gmix).astype(LOW)
        gate = gate_ref[:, lane_chunk(k)]
        s = sigmoid(gate)
        gs = gg * (gate * s)
        ggate = (gg * ym_ref[:, lane_chunk(k)] * silu_grad(gate, s)).astype(LOW)
        ggate_s[:, lane_chunk(k)] = ggate
        gwin_ref[row_chunk(k, inner), :] = dot_tn(ggate, normed_ref[...]).astype(LOW)
        prm = params_of(small_ref, k)
        src = src_ref[:, lane_chunk(k)]
        masks = lag_masks(lens_ref, src.shape, sm.taps)
        pre = conv_pre(src, prm, sm, masks)
        conved = pre * sigmoid(pre)
        lin = lin_ref[:, lane_chunk(k)]
        delta = softplus(lin)
        _, _, opening = segments(lens_ref, lin.shape)
        dl_s[...] = jnp.where(opening, 1e30, delta)
        dt_s[...] = delta
        dx_s[...] = delta * conved
        gs_s[...] = gs
        a = -jnp.exp(prm[sm.alog : sm.alog + states, :])
        scan_forward(rows, dl_s, dx_s, a, bb_s, states, hist_ref=hist_s.at[pl.ds(states, rows * states), :], dec_ref=dec_s)
        galog = scan_backward(rows, states, a, gs_s, dx_s, dt_s, bb_s, cc_s, hist_s, dec_s, gcp_s, gbp_s, lbp_s, amp_s)
        lb = rows_sum8(lbp_s, rows)
        gdelta = rows_sum8(amp_s, rows) + conved * lb
        glin = gdelta * sigmoid(lin)
        gconv_s[:, lane_chunk(k)] = prm[sm.skip : sm.skip + 1, :] * gs + delta * lb
        glin_low = glin.astype(LOW)
        grate_s[...] += dot_nn(glin_low, small_ref[row_chunk(k), LANES : 2 * LANES])
        part = dot_tn(glin_low, rate)
        grows = jnp.concatenate(
            [
                jnp.zeros((sm.alog, CH), F32),
                galog,
                jnp.zeros((sm.taps + 1, CH), F32),
                jnp.sum(glin, axis=0, keepdims=True),
                jnp.sum(gs * conved, axis=0, keepdims=True),
                jnp.zeros((LANES - sm.end, CH), F32),
            ],
            axis=0,
        )
        gsmall_ref[row_chunk(k), LANES : 2 * LANES] = (part + jnp.transpose(grows)).astype(LOW)

    gexp = jnp.where(lane < sm.rank, grate_s[...], 0.0)
    for s in range(states):
        gb = jnp.sum(gbp_s[pl.ds(s, rows, stride=states), :], axis=1, keepdims=True)
        gc = jnp.sum(gcp_s[pl.ds(s, rows, stride=states), :], axis=1, keepdims=True)
        gexp = jnp.where(lane == sm.rank + s, gb, gexp)
        gexp = jnp.where(lane == sm.rank + states + s, gc, gexp)
    gexp_low = gexp.astype(LOW)

    @pl.loop(0, chunks)
    def _(k):
        prm = params_of(small_ref, k)
        src = src_ref[:, lane_chunk(k)]
        masks = lag_masks(lens_ref, src.shape, sm.taps)
        pre = conv_pre(src, prm, sm, masks)
        s = sigmoid(pre)
        conved_low = (pre * s).astype(LOW)
        gsmall_ref[row_chunk(k), 0:LANES] = dot_tn(conved_low, gexp_low).astype(LOW)
        gconv = gconv_s[:, lane_chunk(k)] + dot_nt(gexp_low, small_ref[row_chunk(k), 0:LANES])
        p = gconv * silu_grad(pre, s)
        gsrc = prm[sm.conv : sm.conv + 1, :] * p
        taps = [jnp.sum(p * src, axis=0, keepdims=True)]
        for lag in range(1, sm.taps):
            pm = jnp.where(masks[lag], p, 0.0)
            taps.append(jnp.sum(pm * pltpu.roll(src, lag, 0), axis=0, keepdims=True))
            gsrc = gsrc + prm[sm.conv + lag : sm.conv + lag + 1, :] * pltpu.roll(pm, rows - lag, 0)
        grows = jnp.concatenate(
            [jnp.zeros((sm.conv, CH), F32)]
            + taps
            + [jnp.sum(p, axis=0, keepdims=True), jnp.zeros((LANES - sm.bias - 1, CH), F32)],
            axis=0,
        )
        old = gsmall_ref[row_chunk(k), LANES : 2 * LANES].astype(F32)
        gsmall_ref[row_chunk(k), LANES : 2 * LANES] = (old + jnp.transpose(grows)).astype(LOW)
        gsrc_low = gsrc.astype(LOW)
        gwin_ref[row_chunk(k), :] = dot_tn(gsrc_low, normed_ref[...]).astype(LOW)
        gnorm_s[...] += dot_nn(gsrc_low, win_ref[row_chunk(k), :]) + dot_nn(
            ggate_s[:, lane_chunk(k)], win_ref[row_chunk(k, inner), :]
        )

    gtok, prod = norm_back(tok_ref[...].astype(F32), gain_ref[...], gnorm_s[...])
    ggain_ref[...] = jnp.sum(prod, axis=0, keepdims=True)
    gtok_ref[...] = gtok + gmid_s[...]


VMEM = pltpu.VMEM
SMEM_SPEC = pl.BlockSpec(memory_space=pltpu.SMEM)
VMEM_SPEC = pl.BlockSpec(memory_space=pltpu.VMEM)


def shape_of(shape, dtype):
    return jax.ShapeDtypeStruct(shape, dtype)


def mixer_forward(sm, lens, count, tokens, gain, win_t, small, wout, gain2):
    rows, width = tokens.shape
    inner = wout.shape[0]
    st = sm.states
    return pl.pallas_call(
        partial(mixer_forward_kernel, sm, inner),
        out_shape=(
            shape_of((rows, width), LOW),
            shape_of((rows, inner), F32),
            shape_of((rows, inner), F32),
            shape_of((rows, inner), F32),
            shape_of((rows, inner), F32),
            shape_of((rows, LANES), F32),
            shape_of((rows, inner), LOW),
            shape_of((rows, width), F32),
            shape_of((rows, width), LOW),
        ),
        in_specs=[SMEM_SPEC] * 2 + [VMEM_SPEC] * 6,
        out_specs=(VMEM_SPEC,) * 9,
        scratch_shapes=[
            VMEM((rows, inner), F32),
            VMEM((rows, CH), F32),
            VMEM((rows, CH), F32),
            VMEM((rows * st, LANES), F32),
            VMEM((rows * st, LANES), F32),
            VMEM((CH // LANES, rows * 8, LANES), F32),
            VMEM((rows, width), F32),
        ],
        compiler_params=pltpu.CompilerParams(vmem_limit_bytes=60 << 20),
        name="mixer_forward",
    )(lens, count, tokens, gain, win_t, small, wout, gain2)


def mixer_backward(sm, lens, count, tokens, gain, win_t, small, wout, gain2, saved, gmoe, gout):
    rows, width = tokens.shape
    inner = wout.shape[0]
    st = sm.states
    return pl.pallas_call(
        partial(mixer_backward_kernel, sm, inner),
        out_shape=(
            shape_of((rows, width), F32),
            shape_of((2 * inner, width), LOW),
            shape_of((inner, 2 * LANES), LOW),
            shape_of((inner, width), LOW),
            shape_of((1, width), F32),
            shape_of((1, width), F32),
        ),
        in_specs=[SMEM_SPEC] * 2 + [VMEM_SPEC] * 16,
        out_specs=(VMEM_SPEC,) * 6,
        scratch_shapes=[
            VMEM((rows, width), F32),
            VMEM((rows, width), LOW),
            VMEM((rows, inner), LOW),
            VMEM((rows, inner), F32),
            VMEM((rows, CH), F32),
            VMEM((rows, CH), F32),
            VMEM((rows, CH), F32),
            VMEM((rows, CH), F32),
            VMEM((rows * st, LANES), F32),
            VMEM((rows * st, LANES), F32),
            VMEM(((rows + 1) * st, CH), F32),
            VMEM((rows * st, CH), F32),
            VMEM((rows * st, LANES), F32),
            VMEM((rows * st, LANES), F32),
            VMEM((CH // LANES, rows * 8, LANES), F32),
            VMEM((CH // LANES, rows * 8, LANES), F32),
            VMEM((rows, LANES), F32),
            VMEM((rows, width), F32),
        ],
        compiler_params=pltpu.CompilerParams(vmem_limit_bytes=62 << 20),
        name="mixer_backward",
    )(lens, count, tokens, gain, win_t, small, wout, gain2, *saved, gmoe, gout)


def norm_rows(values, scale_gain):
    return values * lax.rsqrt(jnp.mean(values * values, axis=-1, keepdims=True) + EPS) * scale_gain


AXES = ("wide", "narrow")


def per_device(
    tokens, norm_gain, w_in, conv_w, conv_b, w_x, w_dt, dt_bias, a_log, d_skip, w_out, moe_gain, w_router, w_up,
    w_down, seq_lengths, valid_counts, expert_ids, out_grad,
):
    rows, width = tokens.shape
    sm = Small(w_dt.shape[0], a_log.shape[1], conv_w.shape[0])
    here = w_out.shape[0]
    experts = w_router.shape[1]
    small = jnp.concatenate(
        [
            w_x, jnp.zeros((here, LANES - w_x.shape[1]), LOW), w_dt.T, a_log, conv_w.T, conv_b[:, None], dt_bias[:, None],
            d_skip[:, None], jnp.zeros((here, LANES - sm.end), LOW),
        ],
        axis=1,
    )
    win_t = lax.all_gather(w_in.T, AXES, axis=0, tiled=True)
    rest = lax.all_gather(jnp.concatenate([w_out, small], axis=1), AXES, axis=0, tiled=True)
    wout_all, small_all = rest[:, :width], rest[:, width:]
    ups = lax.all_gather(w_up, AXES, axis=2, tiled=True)
    downs = lax.all_gather(w_down, AXES, axis=1, tiled=True)
    lens = seq_lengths[0]
    gain, gain2 = norm_gain[None], moe_gain[None]
    normed, src, gate, lin, ym, expanded, gated, middle, moe_in = mixer_forward(
        sm, lens, valid_counts, tokens, gain, win_t, small_all, wout_all, gain2
    )
    valid_rows = (jnp.arange(rows, dtype=jnp.int32) < valid_counts[0]).astype(F32)[:, None]
    router_probs = jax.nn.softmax(jnp.dot(moe_in, w_router, preferred_element_type=F32), axis=-1)
    onehot = (expert_ids[:, None] == jnp.arange(experts, dtype=jnp.int32)[None, :]).astype(F32)
    chosen = jnp.sum(router_probs * onehot, axis=-1, keepdims=True)
    grad_out = out_grad.astype(F32)
    grad_two = valid_rows * grad_out
    pre = jnp.einsum("td,edf->etf", moe_in, ups, preferred_element_type=F32)
    act, gelu_back = jax.vjp(lambda v: jax.nn.gelu(v, approximate=True), pre)
    hidden = act.astype(LOW)
    outs = jnp.einsum("etf,efd->etd", hidden, downs, preferred_element_type=F32)
    picked = jnp.sum(onehot.T[:, :, None] * outs, axis=0)
    branch_two = valid_rows * chosen * picked
    result = middle + branch_two
    branch_one = middle - tokens.astype(F32)
    grad_chosen = jnp.sum(grad_two * picked, axis=-1, keepdims=True)
    scaled = (chosen * grad_two).astype(LOW)
    grad_expert = onehot.T.astype(LOW)[:, :, None] * scaled[None]
    grad_down = jnp.einsum("etf,etd->fed", hidden, grad_expert, preferred_element_type=LOW)
    grad_act = jnp.einsum("etd,efd->etf", grad_expert, downs, preferred_element_type=F32)
    grad_pre = gelu_back(grad_act)[0].astype(LOW)
    grad_up = jnp.einsum("td,etf->fed", moe_in, grad_pre, preferred_element_type=LOW)
    grad_moe = jnp.einsum("etf,edf->td", grad_pre, ups, preferred_element_type=F32)
    grad_logits = (router_probs * (onehot - chosen) * grad_chosen).astype(LOW)
    grad_router = jnp.einsum("td,te->de", moe_in, grad_logits, preferred_element_type=F32)
    grad_moe = grad_moe + jnp.einsum("te,de->td", grad_logits, w_router, preferred_element_type=F32)
    gtok, gwin, gsmall, gwout, ggain, ggain2 = mixer_backward(
        sm, lens, valid_counts, tokens, gain, win_t, small_all, wout_all, gain2,
        (normed, src, gate, lin, ym, expanded, gated, middle), grad_moe, out_grad,
    )
    scatter = partial(lax.psum_scatter, axis_name=AXES, scatter_dimension=0, tiled=True)
    gwin = scatter(gwin).astype(F32)
    grest = scatter(jnp.concatenate([gwout, gsmall], axis=1)).astype(F32)
    gup = scatter(grad_up).astype(F32)
    gdown = scatter(grad_down).astype(F32)
    gsm = grest[:, width:]
    flat = jnp.concatenate(
        [
            ggain[0], ggain2[0], grad_router.reshape(-1), jnp.sum(valid_rows * result * result)[None],
            jnp.sum(branch_one * branch_one)[None], jnp.sum(branch_two * branch_two)[None], valid_counts.astype(F32),
        ]
    )
    flat = lax.psum(flat, AXES)
    ggain, ggain2, flat = flat[:width], flat[width : 2 * width], flat[2 * width :]
    grad_router, flat = flat[: width * experts].reshape(width, experts), flat[width * experts :]
    token_rms = jnp.sqrt(flat[:3] / (flat[3] * width))
    g2 = gsm[:, LANES:]
    return (
        result.astype(LOW), gtok, ggain, gwin.T, g2[:, sm.conv : sm.conv + sm.taps].T, g2[:, sm.bias], gsm[:, : w_x.shape[1]],
        g2[:, : sm.rank].T, g2[:, sm.rate], g2[:, sm.alog : sm.alog + sm.states], g2[:, sm.skip], grest[:, :width],
        ggain2, grad_router, gup.transpose(1, 2, 0), gdown.transpose(1, 0, 2), token_rms,
    )


def solution(mesh):
    both = ("wide", "narrow")
    rows2, cols, one, rep = P(both, None), P(None, both), P(both), P()
    in_specs = (
        rows2, rep, cols, cols, one, rows2, cols, one, rows2, one, rows2, rep, rep, P(None, None, both),
        P(None, both, None), rows2, one, one, rows2,
    )
    out_specs = (
        rows2, rows2, rep, cols, cols, one, rows2, cols, one, rows2, one, rows2, rep, rep, P(None, None, both),
        P(None, both, None), rep,
    )
    return jax.shard_map(per_device, mesh=mesh, in_specs=in_specs, out_specs=out_specs, check_vma=False)
```

```python
from functools import partial

import jax
import jax.numpy as jnp
from jax import lax
from jax.experimental import pallas as pl
from jax.experimental.pallas import tpu as pltpu
from jax.sharding import PartitionSpec as P

EPS = 1e-05
LOW = jnp.bfloat16
F32 = jnp.float32
LANES = 128
CH = 384


def dot_nn(a, b):
    return lax.dot_general(a, b, (((1,), (0,)), ((), ())), preferred_element_type=F32)


def dot_nt(a, b):
    return lax.dot_general(a, b, (((1,), (1,)), ((), ())), preferred_element_type=F32)


def dot_tn(a, b):
    return lax.dot_general(a, b, (((0,), (0,)), ((), ())), preferred_element_type=F32)


def sigmoid(v):
    return 1.0 / (1.0 + jnp.exp(-v))


def softplus(v):
    return jnp.maximum(v, 0.0) + jnp.log1p(jnp.exp(-jnp.abs(v)))


class Small:
    def __init__(self, rank, states, taps):
        self.rank, self.states, self.taps = rank, states, taps
        self.alog = -(-rank // 8) * 8
        self.conv = self.alog + states
        self.bias = self.conv + taps
        self.rate = self.bias + 1
        self.skip = self.bias + 2
        self.end = self.bias + 3


def row_iota(shape):
    return lax.broadcasted_iota(jnp.int32, shape, 0)


def lane_iota(shape):
    return lax.broadcasted_iota(jnp.int32, shape, 1)


def segments(lens_ref, shape):
    first = lens_ref[0]
    second = first + lens_ref[1]
    t = row_iota(shape)
    seg = (t >= first).astype(jnp.int32) + (t >= second).astype(jnp.int32)
    opening = (t == 0) | (t == first) | (t == second)
    return t, seg, opening


def lag_masks(lens_ref, shape, taps):
    first = lens_ref[0]
    second = first + lens_ref[1]
    t = row_iota(shape)
    masks = [None]
    for lag in range(1, taps):
        e = t - lag
        same = ((t >= first) == (e >= first)) & ((t >= second) == (e >= second)) & (e >= 0)
        masks.append(same)
    return masks


def conv_pre(src, prm, sm, masks):
    taps = sm.taps
    total = prm[sm.bias : sm.bias + 1, :] + prm[sm.conv : sm.conv + 1, :] * src
    for lag in range(1, taps):
        moved = jnp.where(masks[lag], pltpu.roll(src, lag, 0), 0.0)
        total = total + prm[sm.conv + lag : sm.conv + lag + 1, :] * moved
    return total


def params_of(small_ref, k):
    blk = small_ref[pl.ds(pl.multiple_of(k * CH, CH), CH), LANES : 2 * LANES]
    return jnp.transpose(blk.astype(F32))


def lanes3(v):
    return jnp.concatenate([v] * (CH // LANES), axis=1)


def fold3(v):
    out = v[:, 0:LANES]
    for i in range(1, CH // LANES):
        out = out + v[:, i * LANES : (i + 1) * LANES]
    return out


def spread(expanded, start, states, out_ref):
    rows = expanded.shape[0]
    for s in range(states):
        col = jnp.broadcast_to(expanded[:, start + s : start + s + 1], (rows, LANES))
        out_ref[pl.ds(s, rows, stride=states), :] = col


def rows_sum8(ref, rows):
    planes = []
    for i in range(CH // LANES):
        out = ref[i, pl.ds(0, rows, stride=8), :]
        for j in range(1, 8):
            out = out + ref[i, pl.ds(j, rows, stride=8), :]
        planes.append(out)
    return jnp.concatenate(planes, axis=1)


def put_planes(ref, at, v):
    for i in range(CH // LANES):
        ref[i, at, :] = v[:, i * LANES : (i + 1) * LANES]


def lane_chunk(k, base=0):
    return pl.ds(pl.multiple_of(base + k * CH, LANES), CH)


def row_chunk(k, base=0):
    return pl.ds(pl.multiple_of(base + k * CH, LANES), CH)


def norm_of(x, gain):
    r = lax.rsqrt(jnp.mean(x * x, axis=-1, keepdims=True) + EPS)
    return x * r * gain


def forward_chunk_conv(k, sm, lens_ref, normed_ref, win_ref, small_ref, src_ref, gate_ref, exp_acc, inner):
    normed = normed_ref[...]
    src = dot_nt(normed, win_ref[row_chunk(k), :])
    src_ref[:, lane_chunk(k)] = src
    gate_ref[:, lane_chunk(k)] = dot_nt(normed, win_ref[row_chunk(k, inner), :])
    prm = params_of(small_ref, k)
    masks = lag_masks(lens_ref, src.shape, sm.taps)
    pre = conv_pre(src, prm, sm, masks)
    conved = pre * sigmoid(pre)
    exp_acc[...] += dot_nn(conved.astype(LOW), small_ref[row_chunk(k), 0:LANES])
    return conved


def scan_forward(rows, dl_ref, dx_ref, a, bb_ref, states, cc_ref=None, yp_ref=None, hist_ref=None, dec_ref=None):
    def block(tb, h):
        t0 = pl.multiple_of(tb * 8, 8)
        d8 = dl_ref[pl.ds(t0, 8), :]
        x8 = dx_ref[pl.ds(t0, 8), :]
        for j in range(8):
            d = jnp.broadcast_to(d8[j : j + 1, :], (states, CH))
            x = jnp.broadcast_to(x8[j : j + 1, :], (states, CH))
            dec = jnp.exp(d * a)
            at = pl.ds(pl.multiple_of(t0 * states, 8 * states) + j * states, states)
            h = h * dec + x * lanes3(bb_ref[at, :])
            if hist_ref is not None:
                hist_ref[at, :] = h
                dec_ref[at, :] = dec
            if yp_ref is not None:
                p = h * lanes3(cc_ref[at, :])
                ps = p[0:8]
                for i in range(1, states // 8):
                    ps = ps + p[8 * i : 8 * i + 8]
                put_planes(yp_ref, pl.ds(pl.multiple_of(t0 * 8, 64) + j * 8, 8), ps)
        return h

    lax.fori_loop(0, rows // 8, block, jnp.zeros((states, CH), F32))


def mixer_forward_kernel(
    sm, inner,
    lens_ref, count_ref, tok_ref, gain_ref, win_ref, rest_ref, gain2_ref,
    normed_ref, src_ref, gate_ref, lin_ref, ym_ref, exp_ref, gated_ref, middle_ref, moe_ref, sum_ref,
    conved_s, dl_s, dx_s, bb_s, cc_s, yp_s, acc_s,
):
    rows, width = tok_ref.shape
    wout_ref, small_ref = rest_ref.at[:, 0:width], rest_ref.at[:, width : width + 2 * LANES]
    states = sm.states
    chunks = inner // CH
    tok = tok_ref[...].astype(F32)
    normed_ref[...] = norm_of(tok, gain_ref[...]).astype(LOW)
    exp_ref[...] = jnp.zeros_like(exp_ref)

    @pl.loop(0, chunks)
    def _(k):
        conved_s[:, lane_chunk(k)] = forward_chunk_conv(
            k, sm, lens_ref, normed_ref, win_ref, small_ref, src_ref, gate_ref, exp_ref, inner
        )

    expanded = exp_ref[...]
    lane = lane_iota((rows, LANES))
    rate = jnp.where(lane < sm.rank, expanded, 0.0).astype(LOW)
    spread(expanded, sm.rank, states, bb_s)
    spread(expanded, sm.rank + states, states, cc_s)
    acc_s[...] = jnp.zeros_like(acc_s)

    @pl.loop(0, chunks)
    def _(k):
        prm = params_of(small_ref, k)
        lin = dot_nt(rate, small_ref[row_chunk(k), LANES : 2 * LANES]) + prm[sm.rate : sm.rate + 1, :]
        lin_ref[:, lane_chunk(k)] = lin
        delta = softplus(lin)
        conved = conved_s[:, lane_chunk(k)]
        _, _, opening = segments(lens_ref, lin.shape)
        dl_s[...] = jnp.where(opening, 1e30, delta)
        dx_s[...] = delta * conved
        a = -jnp.exp(prm[sm.alog : sm.alog + states, :])
        scan_forward(rows, dl_s, dx_s, a, bb_s, states, cc_s, yp_s)
        ym = rows_sum8(yp_s, rows) + prm[sm.skip : sm.skip + 1, :] * conved
        ym_ref[:, lane_chunk(k)] = ym
        gate = gate_ref[:, lane_chunk(k)]
        gated = (ym * (gate * sigmoid(gate))).astype(LOW)
        gated_ref[:, lane_chunk(k)] = gated
        acc_s[...] += dot_nn(gated, wout_ref[row_chunk(k), :])

    valid = row_iota((rows, 1)) < count_ref[0]
    branch = jnp.where(valid, acc_s[...], 0.0)
    sum_ref[...] = jnp.broadcast_to(jnp.sum(branch * branch), sum_ref.shape)
    middle = tok + branch
    middle_ref[...] = middle
    moe_ref[...] = norm_of(middle, gain2_ref[...]).astype(LOW)


def silu_grad(v, s):
    return s * (1.0 + v * (1.0 - s))


def norm_back(x, gain, grad):
    r = lax.rsqrt(jnp.mean(x * x, axis=-1, keepdims=True) + EPS)
    n = x * r
    q = grad * gain
    return r * (q - n * jnp.mean(q * n, axis=-1, keepdims=True)), grad * n


def scan_backward(rows, states, a, gs_ref, dx_ref, dt_ref, bb_ref, cc_ref, hist_ref, dec_ref, gcp_ref, gbp_ref, lbp_ref, amp_ref):
    blocks = rows // 8

    def fold8(p):
        out = p[0:8]
        for i in range(1, states // 8):
            out = out + p[8 * i : 8 * i + 8]
        return out

    def block(i, carry):
        back, total = carry
        tb = blocks - 1 - i
        t0 = pl.multiple_of(tb * 8, 8)
        g8 = gs_ref[pl.ds(t0, 8), :]
        x8 = dx_ref[pl.ds(t0, 8), :]
        d8 = dt_ref[pl.ds(t0, 8), :]
        for j in range(7, -1, -1):
            base = pl.multiple_of(t0 * states, 8 * states) + j * states
            at = pl.ds(base + states, states)
            prev = pl.ds(base, states)
            here = pl.ds(base, states)
            g = jnp.broadcast_to(g8[j : j + 1, :], (states, CH))
            x = jnp.broadcast_to(x8[j : j + 1, :], (states, CH))
            d = jnp.broadcast_to(d8[j : j + 1, :], (states, CH))
            adj = g * lanes3(cc_ref[here, :]) + back
            gcp_ref[here, :] += fold3(hist_ref[at, :] * g)
            gbp_ref[here, :] += fold3(adj * x)
            out8 = pl.ds(pl.multiple_of(t0 * 8, 64) + j * 8, 8)
            put_planes(lbp_ref, out8, fold8(adj * lanes3(bb_ref[here, :])))
            back = adj * dec_ref[here, :]
            m = back * hist_ref[prev, :]
            put_planes(amp_ref, out8, fold8(m * a))
            total = total + m * d
        return back, total

    zero = jnp.zeros((states, CH), F32)
    _, total = lax.fori_loop(0, blocks, block, (zero, zero))
    return total * a


def route(rows_in, router, code, experts):
    logits = dot_nt(rows_in, router)
    lane = lane_iota(logits.shape)
    logits = jnp.where(lane < experts, logits, -1e30)
    e = jnp.exp(logits - jnp.max(logits, axis=-1, keepdims=True))
    probs = e / jnp.sum(e, axis=-1, keepdims=True)
    expert = jnp.where(code >= experts, code - experts, code)
    onehot = (lane.astype(F32) == expert).astype(F32)
    return probs, onehot, jnp.sum(probs * onehot, axis=-1, keepdims=True)


def mixer_backward_kernel(
    sm, inner, experts,
    lens_ref, count_ref, tok_ref, gain_ref, win_ref, rest_ref, gain2_ref,
    normed_ref, src_ref, gate_ref, lin_ref, ym_ref, exp_ref, gated_ref, middle_ref, moe_ref, sum_ref,
    gm_ref, picked_ref, gcode_ref, router_ref,
    result_ref, gtok_ref, gwin_ref, grest_ref, flat_ref,
    gmid_s, gmix_s, ggate_s, gconv_s, dl_s, dx_s, dt_s, gs_s, bb_s, cc_s, hist_s, dec_s, gcp_s, gbp_s, lbp_s, amp_s, grate_s, gnorm_s,
):
    rows, width = tok_ref.shape
    wout_ref, small_ref = rest_ref.at[:, 0:width], rest_ref.at[:, width : width + 2 * LANES]
    gwout_ref, gsmall_ref = grest_ref.at[:, 0:width], grest_ref.at[:, width : width + 2 * LANES]
    states = sm.states
    chunks = inner // CH
    pieces = width // LANES

    def put_flat(row, v):
        for i in range(pieces):
            flat_ref[row + i : row + i + 1, :] = v[:, i * LANES : (i + 1) * LANES]

    flat_ref[...] = jnp.zeros_like(flat_ref)
    gout = gcode_ref[:, 0:width].astype(F32)
    valid = row_iota((rows, 1)) < count_ref[0]
    code = gcode_ref[:, width : width + LANES].astype(F32)[:, 0:1]
    moe_in = moe_ref[...]
    probs, onehot, chosen = route(moe_in, router_ref[...], code, experts)
    picked = jnp.where(valid, picked_ref[...], 0.0)
    two = chosen * picked
    result = middle_ref[...] + two
    result_ref[...] = result.astype(LOW)
    gchosen = jnp.sum(gout * picked, axis=-1, keepdims=True)
    glogits = (probs * (onehot - chosen) * gchosen).astype(LOW)
    grouter = dot_tn(glogits, moe_in)
    for e in range(experts):
        put_flat((2 + e) * pieces, grouter[e : e + 1, :])
    squares = jnp.where(valid, result * result, 0.0)
    lane1 = lane_iota((1, LANES))
    stats = jnp.where(lane1 == 0, jnp.sum(squares), 0.0)
    stats = jnp.where(lane1 == 1, sum_ref[0:1, :], stats)
    stats = jnp.where(lane1 == 2, jnp.sum(two * two), stats)
    stats = jnp.where(lane1 == 3, count_ref[0].astype(F32), stats)
    flat_ref[(2 + experts) * pieces : (2 + experts) * pieces + 1, :] = stats
    gmoe = gm_ref[...] + dot_nn(glogits, router_ref[...])
    gmid, prod = norm_back(middle_ref[...], gain2_ref[...], gmoe)
    put_flat(pieces, jnp.sum(prod, axis=0, keepdims=True))
    gmid = gmid + gout
    gmid_s[...] = gmid
    gmix_s[...] = jnp.where(valid, gmid, 0.0).astype(LOW)
    expanded = exp_ref[...]
    lane = lane_iota((rows, LANES))
    rate = jnp.where(lane < sm.rank, expanded, 0.0).astype(LOW)
    spread(expanded, sm.rank, states, bb_s)
    spread(expanded, sm.rank + states, states, cc_s)
    grate_s[...] = jnp.zeros_like(grate_s)
    gcp_s[...] = jnp.zeros_like(gcp_s)
    gbp_s[...] = jnp.zeros_like(gbp_s)
    gnorm_s[...] = jnp.zeros_like(gnorm_s)
    hist_s[0:states, :] = jnp.zeros((states, CH), F32)

    @pl.loop(0, chunks)
    def _(k):
        gmix = gmix_s[...]
        gg = dot_nt(gmix, wout_ref[row_chunk(k), :])
        gwout_ref[row_chunk(k), :] = dot_tn(gated_ref[:, lane_chunk(k)], gmix).astype(LOW)
        gate = gate_ref[:, lane_chunk(k)]
        s = sigmoid(gate)
        gs = gg * (gate * s)
        ggate = (gg * ym_ref[:, lane_chunk(k)] * silu_grad(gate, s)).astype(LOW)
        ggate_s[:, lane_chunk(k)] = ggate
        gwin_ref[row_chunk(k, inner), :] = dot_tn(ggate, normed_ref[...]).astype(LOW)
        prm = params_of(small_ref, k)
        src = src_ref[:, lane_chunk(k)]
        masks = lag_masks(lens_ref, src.shape, sm.taps)
        pre = conv_pre(src, prm, sm, masks)
        conved = pre * sigmoid(pre)
        lin = lin_ref[:, lane_chunk(k)]
        delta = softplus(lin)
        _, _, opening = segments(lens_ref, lin.shape)
        dl_s[...] = jnp.where(opening, 1e30, delta)
        dt_s[...] = delta
        dx_s[...] = delta * conved
        gs_s[...] = gs
        a = -jnp.exp(prm[sm.alog : sm.alog + states, :])
        scan_forward(rows, dl_s, dx_s, a, bb_s, states, hist_ref=hist_s.at[pl.ds(states, rows * states), :], dec_ref=dec_s)
        galog = scan_backward(rows, states, a, gs_s, dx_s, dt_s, bb_s, cc_s, hist_s, dec_s, gcp_s, gbp_s, lbp_s, amp_s)
        lb = rows_sum8(lbp_s, rows)
        gdelta = rows_sum8(amp_s, rows) + conved * lb
        glin = gdelta * sigmoid(lin)
        gconv_s[:, lane_chunk(k)] = prm[sm.skip : sm.skip + 1, :] * gs + delta * lb
        glin_low = glin.astype(LOW)
        grate_s[...] += dot_nn(glin_low, small_ref[row_chunk(k), LANES : 2 * LANES])
        part = dot_tn(glin_low, rate)
        grows = jnp.concatenate(
            [
                jnp.zeros((sm.alog, CH), F32),
                galog,
                jnp.zeros((sm.taps + 1, CH), F32),
                jnp.sum(glin, axis=0, keepdims=True),
                jnp.sum(gs * conved, axis=0, keepdims=True),
                jnp.zeros((LANES - sm.end, CH), F32),
            ],
            axis=0,
        )
        gsmall_ref[row_chunk(k), LANES : 2 * LANES] = (part + jnp.transpose(grows)).astype(LOW)

    gexp = jnp.where(lane < sm.rank, grate_s[...], 0.0)
    for s in range(states):
        gb = jnp.sum(gbp_s[pl.ds(s, rows, stride=states), :], axis=1, keepdims=True)
        gc = jnp.sum(gcp_s[pl.ds(s, rows, stride=states), :], axis=1, keepdims=True)
        gexp = jnp.where(lane == sm.rank + s, gb, gexp)
        gexp = jnp.where(lane == sm.rank + states + s, gc, gexp)
    gexp_low = gexp.astype(LOW)

    @pl.loop(0, chunks)
    def _(k):
        prm = params_of(small_ref, k)
        src = src_ref[:, lane_chunk(k)]
        masks = lag_masks(lens_ref, src.shape, sm.taps)
        pre = conv_pre(src, prm, sm, masks)
        s = sigmoid(pre)
        conved_low = (pre * s).astype(LOW)
        gsmall_ref[row_chunk(k), 0:LANES] = dot_tn(conved_low, gexp_low).astype(LOW)
        gconv = gconv_s[:, lane_chunk(k)] + dot_nt(gexp_low, small_ref[row_chunk(k), 0:LANES])
        p = gconv * silu_grad(pre, s)
        gsrc = prm[sm.conv : sm.conv + 1, :] * p
        taps = [jnp.sum(p * src, axis=0, keepdims=True)]
        for lag in range(1, sm.taps):
            pm = jnp.where(masks[lag], p, 0.0)
            taps.append(jnp.sum(pm * pltpu.roll(src, lag, 0), axis=0, keepdims=True))
            gsrc = gsrc + prm[sm.conv + lag : sm.conv + lag + 1, :] * pltpu.roll(pm, rows - lag, 0)
        grows = jnp.concatenate(
            [jnp.zeros((sm.conv, CH), F32)]
            + taps
            + [jnp.sum(p, axis=0, keepdims=True), jnp.zeros((LANES - sm.bias - 1, CH), F32)],
            axis=0,
        )
        old = gsmall_ref[row_chunk(k), LANES : 2 * LANES].astype(F32)
        gsmall_ref[row_chunk(k), LANES : 2 * LANES] = (old + jnp.transpose(grows)).astype(LOW)
        gsrc_low = gsrc.astype(LOW)
        gwin_ref[row_chunk(k), :] = dot_tn(gsrc_low, normed_ref[...]).astype(LOW)
        gnorm_s[...] += dot_nn(gsrc_low, win_ref[row_chunk(k), :]) + dot_nn(
            ggate_s[:, lane_chunk(k)], win_ref[row_chunk(k, inner), :]
        )

    gtok, prod = norm_back(tok_ref[...].astype(F32), gain_ref[...], gnorm_s[...])
    put_flat(0, jnp.sum(prod, axis=0, keepdims=True))
    gtok_ref[...] = gtok + gmid_s[...]


VMEM = pltpu.VMEM
SMEM_SPEC = pl.BlockSpec(memory_space=pltpu.SMEM)
VMEM_SPEC = pl.BlockSpec(memory_space=pltpu.VMEM)


def shape_of(shape, dtype):
    return jax.ShapeDtypeStruct(shape, dtype)


def mixer_forward(sm, lens, count, tokens, gain, win_t, rest, gain2):
    rows, width = tokens.shape
    inner = rest.shape[0]
    st = sm.states
    return pl.pallas_call(
        partial(mixer_forward_kernel, sm, inner),
        out_shape=(
            shape_of((rows, width), LOW),
            shape_of((rows, inner), F32),
            shape_of((rows, inner), F32),
            shape_of((rows, inner), F32),
            shape_of((rows, inner), F32),
            shape_of((rows, LANES), F32),
            shape_of((rows, inner), LOW),
            shape_of((rows, width), F32),
            shape_of((rows, width), LOW),
            shape_of((8, LANES), F32),
        ),
        in_specs=[SMEM_SPEC] * 2 + [VMEM_SPEC] * 5,
        out_specs=(VMEM_SPEC,) * 10,
        scratch_shapes=[
            VMEM((rows, inner), F32),
            VMEM((rows, CH), F32),
            VMEM((rows, CH), F32),
            VMEM((rows * st, LANES), F32),
            VMEM((rows * st, LANES), F32),
            VMEM((CH // LANES, rows * 8, LANES), F32),
            VMEM((rows, width), F32),
        ],
        compiler_params=pltpu.CompilerParams(vmem_limit_bytes=60 << 20),
        name="mixer_forward",
    )(lens, count, tokens, gain, win_t, rest, gain2)


def flat_rows(width, experts):
    return -(-((2 + experts) * (width // LANES) + 1) // 8) * 8


def mixer_backward(sm, experts, lens, count, tokens, gain, win_t, rest, gain2, saved, gm, picked, gcode, router):
    rows, width = tokens.shape
    inner = rest.shape[0]
    st = sm.states
    return pl.pallas_call(
        partial(mixer_backward_kernel, sm, inner, experts),
        out_shape=(
            shape_of((rows, width), LOW),
            shape_of((rows, width), F32),
            shape_of((2 * inner, width), LOW),
            shape_of((inner, width + 2 * LANES), LOW),
            shape_of((flat_rows(width, experts), LANES), F32),
        ),
        in_specs=[SMEM_SPEC] * 2 + [VMEM_SPEC] * 19,
        out_specs=(VMEM_SPEC,) * 5,
        scratch_shapes=[
            VMEM((rows, width), F32),
            VMEM((rows, width), LOW),
            VMEM((rows, inner), LOW),
            VMEM((rows, inner), F32),
            VMEM((rows, CH), F32),
            VMEM((rows, CH), F32),
            VMEM((rows, CH), F32),
            VMEM((rows, CH), F32),
            VMEM((rows * st, LANES), F32),
            VMEM((rows * st, LANES), F32),
            VMEM(((rows + 1) * st, CH), F32),
            VMEM((rows * st, CH), F32),
            VMEM((rows * st, LANES), F32),
            VMEM((rows * st, LANES), F32),
            VMEM((CH // LANES, rows * 8, LANES), F32),
            VMEM((CH // LANES, rows * 8, LANES), F32),
            VMEM((rows, LANES), F32),
            VMEM((rows, width), F32),
        ],
        compiler_params=pltpu.CompilerParams(vmem_limit_bytes=63 << 20),
        name="mixer_backward",
    )(lens, count, tokens, gain, win_t, rest, gain2, *saved, gm, picked, gcode, router)


MESH = pl.DeviceIdType.MESH


class Place:
    def __init__(self, nz):
        self.nz = nz
        w, n = lax.axis_index("wide"), lax.axis_index("narrow")
        self.z, self.y, self.x, self.c = w // 2, w % 2, n // 2, n % 2

    def flips(self, f2, f3):
        fx = f2 * (1 - self.c) + f3 * self.c
        fy = f3 * (1 - self.c) + f2 * self.c
        return self.x + fx - 2 * self.x * fx, self.y + fy - 2 * self.y * fy

    def device(self, z, f2, f3, fc):
        x, y = self.flips(f2, f3)
        core = 1 - self.c if fc else self.c
        return (z * 2 + y, x * 2 + core)

    def target(self, kind):
        if kind == "sib":
            return self.device(self.z, 0, 0, 1)
        if kind == "d2":
            return self.device(self.z, 1, 0, 0)
        if kind == "d3":
            return self.device(self.z, 0, 1, 0)
        return self.device(self.z + kind, 0, 0, 0)

    def block(self, zloc, f2, f3, fc):
        x, y = self.flips(f2, f3)
        core = 1 - self.c if fc else self.c
        return zloc * 8 + y * 4 + x * 2 + core

    def has(self, side, group):
        at = self.z % group + side
        return (at >= 0) & (at < group)

    def barrier(self):
        sem = pltpu.get_barrier_semaphore()
        for kind in ("sib", "d2", "d3"):
            pl.semaphore_signal(sem, inc=1, device_id=self.target(kind), device_id_type=MESH)
        for side in (-1, 1):
            @pl.when(self.has(side, self.nz))
            def _():
                pl.semaphore_signal(sem, inc=1, device_id=self.target(side), device_id_type=MESH)
        below = (self.z + self.nz - 1) // self.nz
        above = (2 * self.nz - 2 - self.z) // self.nz
        pl.semaphore_wait(sem, 3 + below + above)


def when(cond, body):
    if cond is True:
        body()
    else:
        pl.when(cond)(body)


class Gather:
    def __init__(self, place, src, out, send, recv, local, group):
        self.place, self.src, self.out, self.send, self.recv, self.local, self.group = place, src, out, send, recv, local, group
        self.slots = 0
        self.sent = []

    def copy(self, src, p, kind, slot):
        return pltpu.make_async_remote_copy(
            src, self.out.at[p], self.send.at[slot], self.recv.at[p], device_id=self.place.target(kind), device_id_type=MESH
        )

    def push(self, rel, kinds):
        for kind in kinds:
            slot = self.slots
            self.slots += 1
            self.sent.append((rel, kind, slot))

            def go(kind=kind, slot=slot):
                p, src = self.source(rel)
                self.copy(src, p, kind, slot).start()

            when(self.extra(kind), go)

    def extra(self, kind):
        return True if isinstance(kind, str) else self.place.has(kind, self.group)

    def source(self, rel):
        zloc = self.place.z % self.group
        if rel is None:
            return self.place.block(zloc, 0, 0, 0), self.src
        p = self.place.block(zloc + rel[0], rel[1], rel[2], 0)
        return p, self.out.at[p]

    def begin(self):
        p, src = self.source(None)
        self.push(None, [-1, 1, "d2", "d3", "sib"])
        pltpu.make_async_copy(src, self.out.at[p], self.local).start()

    def wait_block(self, p):
        self.copy(self.src, p, "sib", 0).wait_recv()

    def events(self):
        out = []
        for dist in range(-self.group + 1, self.group):
            for f2 in (0, 1):
                for f3 in (0, 1):
                    if dist or f2 or f3:
                        out.append((abs(dist) + f2 + 2 * f3, dist, f2, f3))
        return sorted(out)

    def handle(self, dist, f2, f3):
        zloc = self.place.z % self.group
        cond = True if dist == 0 else self.place.has(dist, self.group)
        kinds = ["sib"]
        if not f3:
            kinds = ["d3"] + kinds
            if not f2:
                kinds = [1 if dist < 0 else -1, "d2"] + kinds

        def body():
            self.wait_block(self.place.block(zloc + dist, f2, f3, 0))
            self.push((dist, f2, f3), kinds)

        when(cond, body)

    def finish(self):
        p, src = self.source(None)
        pltpu.make_async_copy(src, self.out.at[p], self.local).wait()
        for f2 in (0, 1):
            for f3 in (0, 1):
                for z in range(self.group):
                    self.wait_block(self.place.block(z, f2, f3, 1))
        for rel, kind, slot in self.sent:
            def end(rel=rel, kind=kind, slot=slot):
                def inner():
                    p, src = self.source(rel)
                    self.copy(src, p, kind, slot).wait_send()

                when(self.extra(kind), inner)

            when(True if rel is None or not rel[0] else self.place.has(rel[0], self.group), end)

    @staticmethod
    def sends(group):
        return 5 + sum(2 + (not f3) + 2 * ((not f3) and (not f2)) for d in range(-group + 1, group) for f2 in (0, 1) for f3 in (0, 1))


def run_gathers(gathers):
    for g in gathers:
        g.begin()
    events = []
    for i, g in enumerate(gathers):
        events += [(e[0], i) + e[1:] for e in g.events()]
    for _, i, dist, f2, f3 in sorted(events):
        gathers[i].handle(dist, f2, f3)
    for g in gathers:
        g.finish()


class Scatter:
    def __init__(self, place, src, acc, rsib, rd3, rd2, rz, send, recv, local, group):
        self.place, self.src, self.acc = place, src, acc
        self.rsib, self.rd3, self.rd2, self.rz = rsib, rd3, rd2, rz
        self.send, self.recv, self.local, self.group = send, recv, local, group
        z = place.z % group
        self.zloc = z
        if group == 2:
            self.order = [(1 - z, 1 - 2 * z)]
        else:
            h, low = z // 2, z % 2
            self.order = [(3 * (1 - h), 1 - 2 * h), (2 - h, 1 - 2 * h), (2 * h + 1 - low, 1 - 2 * low)]
        self.dests = [zz for zz, _ in self.order] + [z]

    def copy(self, src, dst, send, recv, target):
        return pltpu.make_async_remote_copy(
            src, dst, self.send.at[send], self.recv.at[recv], device_id=target, device_id_type=MESH
        )

    def to_sib(self, k, f2, f3):
        at = self.dests[k] * 4 + f3 * 2 + f2
        src = self.src.at[self.place.block(self.dests[k], f2, f3, 1)]
        return self.copy(src, self.rsib.at[at], k * 4 + f2 * 2 + f3, at, self.place.target("sib"))

    def to_d3(self, k, f2):
        zz, group = self.dests[k], self.group
        row = 4 * group + k * 2 + f2
        return self.copy(
            self.acc.at[zz * 4 + f2 * 2 + 1], self.rd3.at[zz * 2 + f2], row, 4 * group + zz * 2 + f2, self.place.target("d3")
        )

    def to_d2(self, k):
        zz, group = self.dests[k], self.group
        return self.copy(self.acc.at[zz * 4 + 2], self.rd2.at[zz], 6 * group + k, 6 * group + zz, self.place.target("d2"))

    def zrow(self, zz, side):
        return zz + self.group * (1 + side) // 2

    def to_z(self, k):
        zz, side = self.order[k]
        row = self.zrow(zz, side)
        return self.copy(self.acc.at[zz * 4], self.rz.at[row], 7 * self.group + k, 7 * self.group + row, self.place.target(side))

    def received(self, ref, row):
        pltpu.make_async_remote_copy(
            ref, ref, self.send.at[0], self.recv.at[row], device_id=self.place.target("sib"), device_id_type=MESH
        ).wait_recv()
        return ref

    def from_z(self, zz, side):
        row = self.zrow(zz, side)
        return self.received(self.rz.at[row], 7 * self.group + row)

    def local_copy(self, k, f2, f3):
        at = self.dests[k] * 4 + f2 * 2 + f3
        return pltpu.make_async_copy(
            self.src.at[self.place.block(self.dests[k], f2, f3, 0)], self.acc.at[at], self.local.at[k * 4 + f2 * 2 + f3]
        )

    def begin(self):
        for k in range(self.group):
            for f2, f3 in ((1, 1), (1, 0), (0, 1), (0, 0)):
                self.to_sib(k, f2, f3).start()
            for f2, f3 in ((1, 1), (0, 1), (1, 0), (0, 0)):
                self.local_copy(k, f2, f3).start()

    def add(self, at, ref):
        acc = self.acc

        @pl.loop(0, ref.shape[-1] // LANES)
        def _(i):
            lanes = pl.ds(pl.multiple_of(i * LANES, LANES), LANES)
            acc[at, :, lanes] = acc[at, :, lanes] + ref[:, lanes]

    def own(self, k, f2, f3):
        at = self.dests[k] * 4 + f2 * 2 + f3
        self.local_copy(k, f2, f3).wait()
        self.add(at, self.received(self.rsib.at[at], at))
        return at

    def step_a(self, k):
        for f2 in (1, 0):
            self.own(k, f2, 1)
            self.to_d3(k, f2).start()

    def add_d3(self, k, f2, at):
        row = self.dests[k] * 2 + f2
        self.add(at, self.received(self.rd3.at[row], 4 * self.group + row))

    def step_b(self, k):
        at = self.own(k, 1, 0)
        self.add_d3(k, 1, at)
        self.to_d2(k).start()

    def step_c(self, k):
        at = self.own(k, 0, 0)
        self.add_d3(k, 0, at)
        zz = self.dests[k]
        self.add(at, self.received(self.rd2.at[zz], 6 * self.group + zz))
        if k < self.group - 1:
            side = self.order[k][1]

            @pl.when(self.place.has(-side, self.group))
            def _():
                self.add(at, self.from_z(zz, side))

            self.to_z(k).start()

    def result(self, out):
        out[...] = self.acc[self.zloc * 4].astype(out.dtype)
        for side in (-1, 1):
            @pl.when(self.place.has(side, self.group))
            def _():
                out[...] += self.from_z(self.zloc, -side)[...].astype(out.dtype)

    def steps(self):
        out = []
        for k in range(self.group):
            out += [(3 * k, self.step_a, k), (3 * k + 4, self.step_b, k), (3 * k + 8, self.step_c, k)]
        return sorted(out, key=lambda e: e[0])

    def finish(self):
        for k in range(self.group):
            for f2 in (0, 1):
                for f3 in (0, 1):
                    self.to_sib(k, f2, f3).wait_send()
                self.to_d3(k, f2).wait_send()
            self.to_d2(k).wait_send()
            if k < self.group - 1:
                self.to_z(k).wait_send()

    @staticmethod
    def scratch(group, rows, cols, dtype):
        return [
            VMEM((4 * group, rows, cols), dtype),
            VMEM((4 * group, rows, cols), dtype),
            VMEM((2 * group, rows, cols), dtype),
            VMEM((group, rows, cols), dtype),
            VMEM((2 * group, rows, cols), dtype),
            pltpu.SemaphoreType.DMA((8 * group,)),
            pltpu.SemaphoreType.DMA((9 * group,)),
            pltpu.SemaphoreType.DMA((4 * group,)),
        ]


def run_scatters(scatters, outs, gathers=()):
    for g in gathers:
        g.begin()
    for s in scatters:
        s.begin()
    steps = []
    for i, s in enumerate(scatters):
        steps += [(t, i, step, k) for t, step, k in s.steps()]
    for _, _, step, k in sorted(steps, key=lambda e: e[:2]):
        step(k)
    for g in gathers:
        for _, dist, f2, f3 in g.events():
            g.handle(dist, f2, f3)
    for s, out in zip(scatters, outs):
        s.result(out)
    for s in scatters:
        s.finish()
    for g in gathers:
        g.finish()


ANY_SPEC = pl.BlockSpec(memory_space=pl.ANY)


def gather_scratch(group):
    return [
        pltpu.SemaphoreType.DMA((Gather.sends(group),)),
        pltpu.SemaphoreType.DMA((group * 8,)),
        pltpu.SemaphoreType.DMA,
    ]


def gather_kernel(nz, groups, *refs):
    n = len(groups)
    srcs, outs, scr = refs[:n], refs[n : 2 * n], refs[2 * n :]
    place = Place(nz)
    place.barrier()
    run_gathers(
        [Gather(place, srcs[i], outs[i], *scr[3 * i : 3 * i + 3], groups[i]) for i in range(n)]
    )


def gather_call(nz, groups, arrays, collective_id):
    return pl.pallas_call(
        partial(gather_kernel, nz, groups),
        out_shape=tuple(shape_of((g * 8,) + a.shape, a.dtype) for g, a in zip(groups, arrays)),
        in_specs=[ANY_SPEC] * len(arrays),
        out_specs=(ANY_SPEC,) * len(arrays),
        scratch_shapes=sum([gather_scratch(g) for g in groups], []),
        compiler_params=pltpu.CompilerParams(collective_id=collective_id, has_side_effects=True, vmem_limit_bytes=60 << 20),
        name="gather_blocks",
    )(*arrays)


def scatter_kernel(nz, groups, gathered, *refs):
    n = len(groups)
    g = len(gathered)
    srcs, gsrcs, outs, gouts, scr = refs[:n], refs[n : n + g], refs[n + g : 2 * n + g], refs[2 * n + g : 2 * n + 2 * g], refs[2 * n + 2 * g :]
    place = Place(nz)
    place.barrier()
    scatters = [Scatter(place, srcs[i], *scr[8 * i : 8 * i + 8], groups[i]) for i in range(n)]
    more = scr[8 * n :]
    gathers = [Gather(place, gsrcs[i], gouts[i], *more[3 * i : 3 * i + 3], gathered[i]) for i in range(g)]
    run_scatters(scatters, outs, gathers)


def scatter_call(nz, groups, arrays, gathered, garrays, collective_id):
    return pl.pallas_call(
        partial(scatter_kernel, nz, groups, gathered),
        out_shape=tuple(shape_of(a.shape[1:], F32) for a in arrays)
        + tuple(shape_of((g * 8,) + a.shape, a.dtype) for g, a in zip(gathered, garrays)),
        in_specs=[ANY_SPEC] * (len(arrays) + len(garrays)),
        out_specs=(VMEM_SPEC,) * len(arrays) + (ANY_SPEC,) * len(garrays),
        scratch_shapes=sum([Scatter.scratch(g, a.shape[1], a.shape[2], a.dtype) for g, a in zip(groups, arrays)], [])
        + sum([gather_scratch(g) for g in gathered], []),
        compiler_params=pltpu.CompilerParams(collective_id=collective_id, has_side_effects=True, vmem_limit_bytes=60 << 20),
        name="scatter_blocks",
    )(*arrays, *garrays)


GELU_A = 0.7978845608028654
GELU_B = 0.044715


def gelu_parts(v):
    inside = GELU_A * (v + GELU_B * v * v * v)
    t = jnp.tanh(inside)
    slope = 0.5 * (1.0 + t) + 0.5 * v * (1.0 - t * t) * (GELU_A * (1.0 + 3.0 * GELU_B * v * v))
    return 0.5 * v * (1.0 + t), slope


def expert_kernel(experts, block, moe_ref, gcode_ref, mine_ref, other_ref, router_ref, picked_ref, gm_ref, gmine_ref, gother_ref, wu_s, wd_s, gu_s, gd_s):
    tokens, width = moe_ref.shape
    units = mine_ref.shape[0] // 2
    per = units // experts
    wu_s[0:units, :] = mine_ref[0:units, :]
    wu_s[units : 2 * units, :] = other_ref[0:units, :]
    wd_s[0:units, :] = mine_ref[units : 2 * units, :]
    wd_s[units : 2 * units, :] = other_ref[units : 2 * units, :]
    gu_s[...] = jnp.zeros_like(gu_s)
    gd_s[...] = jnp.zeros_like(gd_s)

    @pl.loop(0, tokens // block)
    def _(i):
        at = pl.ds(pl.multiple_of(i * block, block), block)
        m = moe_ref[at, :]
        code = gcode_ref[at, width : width + LANES].astype(F32)[:, 0:1]
        _, _, chosen = route(m, router_ref[...], code, experts)
        live = code < experts
        expert = jnp.where(live, code, code - experts)
        col = lane_iota((block, 2 * units))
        col = jnp.where(col >= units, col - units, col).astype(F32)
        mask = (col >= expert * per) & (col < (expert + 1.0) * per)
        pre = dot_nt(m, wu_s[...])
        act, slope = gelu_parts(pre)
        hidden = jnp.where(mask, act, 0.0).astype(LOW)
        picked_ref[at, :] = dot_nn(hidden, wd_s[...]).astype(LOW)
        go = (jnp.where(live, chosen, 0.0) * gcode_ref[at, 0:width].astype(F32)).astype(LOW)
        gpre = jnp.where(mask, dot_nt(go, wd_s[...]) * slope, 0.0).astype(LOW)
        gm_ref[at, :] = dot_nn(gpre, wu_s[...]).astype(LOW)
        gu_s[...] += dot_tn(gpre, m)
        gd_s[...] += dot_tn(hidden, go)

    gmine_ref[0:units, :] = gu_s[0:units, :]
    gmine_ref[units : 2 * units, :] = gd_s[0:units, :]
    gother_ref[0:units, :] = gu_s[units : 2 * units, :].astype(LOW)
    gother_ref[units : 2 * units, :] = gd_s[units : 2 * units, :].astype(LOW)


def expert_call(experts, moe_all, gcode_all, mine, other, router):
    tokens, width = moe_all.shape
    units = mine.shape[0]
    return pl.pallas_call(
        partial(expert_kernel, experts, 256),
        out_shape=(
            shape_of((tokens, width), LOW),
            shape_of((tokens, width), LOW),
            shape_of((units, width), F32),
            shape_of((units, width), LOW),
        ),
        in_specs=[VMEM_SPEC] * 5,
        out_specs=(VMEM_SPEC,) * 4,
        scratch_shapes=[VMEM((units, width), LOW), VMEM((units, width), LOW), VMEM((units, width), F32), VMEM((units, width), F32)],
        compiler_params=pltpu.CompilerParams(vmem_limit_bytes=60 << 20),
        name="experts",
    )(moe_all, gcode_all, mine, other, router)


AXES = ("wide", "narrow")


def experts_local(moe_in, gcode, w_up, w_down, router, experts):
    width = moe_in.shape[1]
    ups = lax.all_gather(w_up, AXES, axis=2, tiled=True)
    downs = lax.all_gather(w_down, AXES, axis=1, tiled=True)
    code = gcode[:, width : width + 1].astype(F32)
    _, onehot, chosen = route(moe_in, router, code, experts)
    onehot = onehot[:, :experts]
    pre = jnp.einsum("td,edf->etf", moe_in, ups, preferred_element_type=F32)
    act, slope = gelu_parts(pre)
    hidden = act.astype(LOW)
    outs = jnp.einsum("etf,efd->etd", hidden, downs, preferred_element_type=F32)
    picked = jnp.sum(onehot.T[:, :, None] * outs, axis=0)
    scaled = (jnp.where(code < experts, chosen, 0.0) * gcode[:, :width].astype(F32)).astype(LOW)
    grad_expert = onehot.T.astype(LOW)[:, :, None] * scaled[None]
    grad_down = jnp.einsum("etf,etd->fed", hidden, grad_expert, preferred_element_type=LOW)
    grad_act = jnp.einsum("etd,efd->etf", grad_expert, downs, preferred_element_type=F32)
    grad_pre = (grad_act * slope).astype(LOW)
    grad_up = jnp.einsum("td,etf->fed", moe_in, grad_pre, preferred_element_type=LOW)
    gm = jnp.einsum("etf,edf->td", grad_pre, ups, preferred_element_type=F32)
    scatter = partial(lax.psum_scatter, axis_name=AXES, scatter_dimension=0, tiled=True)
    gup = scatter(grad_up).astype(F32).transpose(1, 2, 0)
    gdown = scatter(grad_down).astype(F32).transpose(1, 0, 2)
    return picked, gm, gup, gdown


def per_device(
    nz, tokens, norm_gain, w_in, conv_w, conv_b, w_x, w_dt, dt_bias, a_log, d_skip, w_out, moe_gain, w_router, w_up,
    w_down, seq_lengths, valid_counts, expert_ids, out_grad,
):
    rows, width = tokens.shape
    sm = Small(w_dt.shape[0], a_log.shape[1], conv_w.shape[0])
    here = w_out.shape[0]
    experts, per = w_up.shape[0], w_up.shape[2]
    rest = jnp.concatenate(
        [
            w_out, w_x, jnp.zeros((here, LANES - w_x.shape[1]), LOW), w_dt.T, a_log, conv_w.T, conv_b[:, None],
            dt_bias[:, None], d_skip[:, None], jnp.zeros((here, LANES - sm.end), LOW),
        ],
        axis=1,
    )
    router = jnp.concatenate([w_router.T, jnp.zeros((LANES - experts, width), LOW)], axis=0)
    live = jnp.arange(rows, dtype=jnp.int32) < valid_counts[0]
    code = jnp.where(live, expert_ids, expert_ids + experts).astype(LOW)
    gcode = jnp.concatenate([out_grad, jnp.broadcast_to(code[:, None], (rows, LANES))], axis=1)
    lens = seq_lengths[0]
    gain, gain2 = norm_gain[None], moe_gain[None]
    if nz:
        mine = jnp.concatenate([w_up.transpose(0, 2, 1).reshape(experts * per, width), w_down.reshape(experts * per, width)])
        half = [(w, w ^ 4) for w in range(2 * nz)]
        other = lax.ppermute(mine, "wide", half)
        win_all, rest_all, gcode_all = gather_call(nz, (nz, nz, 2), (w_in.T, rest, gcode), 0)
        win_all = win_all.reshape(-1, width)
        rest_all = rest_all.reshape(-1, rest.shape[1])
    else:
        win_all = lax.all_gather(w_in.T, AXES, axis=0, tiled=True)
        rest_all = lax.all_gather(rest, AXES, axis=0, tiled=True)
    saved = mixer_forward(sm, lens, valid_counts, tokens, gain, win_all, rest_all, gain2)
    moe_in = saved[8]
    if nz:
        (moe_all,) = gather_call(nz, (2,), (moe_in,), 1)
        picked, gm, gmine, gother = expert_call(
            experts, moe_all.reshape(-1, width), gcode_all.reshape(-1, gcode.shape[1]), mine, other, router
        )
        gother = lax.ppermute(gother, "wide", half)
        blocks = (2 * 8, rows, width)
        gm, picked = scatter_call(nz, (2, 2), (gm.reshape(blocks), picked.reshape(blocks)), (), (), 2)
    else:
        picked, gm, gup, gdown = experts_local(moe_in, gcode, w_up, w_down, router, experts)
    result, gtok, gwin, grest, flat = mixer_backward(
        sm, experts, lens, valid_counts, tokens, gain, win_all, rest_all, gain2, saved, gm, picked, gcode, router
    )
    if nz:
        devices = 8 * nz
        gwin, grest, flat = scatter_call(
            nz, (nz, nz), (gwin.reshape(devices, -1, width), grest.reshape(devices, here, -1)), (nz,), (flat,), 3
        )
        flat = jnp.sum(flat, axis=0)
        gmine = gmine + gother.astype(F32)
        gup = gmine[: experts * per].reshape(experts, per, width).transpose(0, 2, 1)
        gdown = gmine[experts * per :].reshape(experts, per, width)
    else:
        scatter = partial(lax.psum_scatter, axis_name=AXES, scatter_dimension=0, tiled=True)
        gwin = scatter(gwin).astype(F32)
        grest = scatter(grest).astype(F32)
        flat = lax.psum(flat, AXES)
    flat = flat.reshape(-1)
    ggain, ggain2, flat = flat[:width], flat[width : 2 * width], flat[2 * width :]
    grad_router, flat = flat[: width * experts].reshape(experts, width).T, flat[width * experts :]
    token_rms = jnp.sqrt(flat[:3] / (flat[3] * width))
    g1 = grest[:, width:]
    g2 = g1[:, LANES:]
    return (
        result, gtok, ggain, gwin.T, g2[:, sm.conv : sm.conv + sm.taps].T, g2[:, sm.bias], g1[:, : w_x.shape[1]],
        g2[:, : sm.rank].T, g2[:, sm.rate], g2[:, sm.alog : sm.alog + sm.states], g2[:, sm.skip], grest[:, :width],
        ggain2, grad_router, gup, gdown, token_rms,
    )


def solution(mesh):
    wide, narrow = mesh.shape["wide"], mesh.shape["narrow"]
    nz = wide // 2 if narrow == 4 and wide == 8 else 0
    both = ("wide", "narrow")
    rows2, cols, one, rep = P(both, None), P(None, both), P(both), P()
    in_specs = (
        rows2, rep, cols, cols, one, rows2, cols, one, rows2, one, rows2, rep, rep, P(None, None, both),
        P(None, both, None), rows2, one, one, rows2,
    )
    out_specs = (
        rows2, rows2, rep, cols, cols, one, rows2, cols, one, rows2, one, rows2, rep, rep, P(None, None, both),
        P(None, both, None), rep,
    )
    return jax.shard_map(partial(per_device, nz), mesh=mesh, in_specs=in_specs, out_specs=out_specs, check_vma=False)
```

```python
from functools import partial

import jax
import jax.numpy as jnp
from jax import lax
from jax.experimental import pallas as pl
from jax.experimental.pallas import tpu as pltpu
from jax.sharding import PartitionSpec as P

EPS = 1e-05
LOW = jnp.bfloat16
F32 = jnp.float32
LANES = 128
CH = 384


def dot_nn(a, b):
    return lax.dot_general(a, b, (((1,), (0,)), ((), ())), preferred_element_type=F32)


def dot_nt(a, b):
    return lax.dot_general(a, b, (((1,), (1,)), ((), ())), preferred_element_type=F32)


def dot_tn(a, b):
    return lax.dot_general(a, b, (((0,), (0,)), ((), ())), preferred_element_type=F32)


def sigmoid(v):
    return 1.0 / (1.0 + jnp.exp(-v))


def softplus(v):
    return jnp.maximum(v, 0.0) + jnp.log1p(jnp.exp(-jnp.abs(v)))


class Small:
    def __init__(self, rank, states, taps):
        self.rank, self.states, self.taps = rank, states, taps
        self.alog = -(-rank // 8) * 8
        self.conv = self.alog + states
        self.bias = self.conv + taps
        self.rate = self.bias + 1
        self.skip = self.bias + 2
        self.end = self.bias + 3


def row_iota(shape):
    return lax.broadcasted_iota(jnp.int32, shape, 0)


def lane_iota(shape):
    return lax.broadcasted_iota(jnp.int32, shape, 1)


def segments(lens_ref, shape):
    first = lens_ref[0]
    second = first + lens_ref[1]
    t = row_iota(shape)
    seg = (t >= first).astype(jnp.int32) + (t >= second).astype(jnp.int32)
    opening = (t == 0) | (t == first) | (t == second)
    return t, seg, opening


def lag_masks(lens_ref, shape, taps):
    first = lens_ref[0]
    second = first + lens_ref[1]
    t = row_iota(shape)
    masks = [None]
    for lag in range(1, taps):
        e = t - lag
        same = ((t >= first) == (e >= first)) & ((t >= second) == (e >= second)) & (e >= 0)
        masks.append(same)
    return masks


def conv_pre(src, prm, sm, masks):
    taps = sm.taps
    total = prm[sm.bias : sm.bias + 1, :] + prm[sm.conv : sm.conv + 1, :] * src
    for lag in range(1, taps):
        moved = jnp.where(masks[lag], pltpu.roll(src, lag, 0), 0.0)
        total = total + prm[sm.conv + lag : sm.conv + lag + 1, :] * moved
    return total


def params_of(small_ref, k):
    blk = small_ref[pl.ds(pl.multiple_of(k * CH, CH), CH), LANES : 2 * LANES]
    return jnp.transpose(blk.astype(F32))


def lanes3(v):
    return jnp.concatenate([v] * (CH // LANES), axis=1)


def fold3(v):
    out = v[:, 0:LANES]
    for i in range(1, CH // LANES):
        out = out + v[:, i * LANES : (i + 1) * LANES]
    return out


def spread(expanded, start, states, out_ref):
    rows = expanded.shape[0]
    for s in range(states):
        col = jnp.broadcast_to(expanded[:, start + s : start + s + 1], (rows, LANES))
        out_ref[pl.ds(s, rows, stride=states), :] = col


def rows_sum8(ref, rows):
    planes = []
    for i in range(CH // LANES):
        out = ref[i, pl.ds(0, rows, stride=8), :]
        for j in range(1, 8):
            out = out + ref[i, pl.ds(j, rows, stride=8), :]
        planes.append(out)
    return jnp.concatenate(planes, axis=1)


def put_planes(ref, at, v):
    for i in range(CH // LANES):
        ref[i, at, :] = v[:, i * LANES : (i + 1) * LANES]


def lane_chunk(k, base=0):
    return pl.ds(pl.multiple_of(base + k * CH, LANES), CH)


def row_chunk(k, base=0):
    return pl.ds(pl.multiple_of(base + k * CH, LANES), CH)


def norm_of(x, gain):
    r = lax.rsqrt(jnp.mean(x * x, axis=-1, keepdims=True) + EPS)
    return x * r * gain


def forward_chunk_conv(k, sm, lens_ref, normed_ref, win_ref, small_ref, src_ref, gate_ref, exp_acc, inner):
    normed = normed_ref[...]
    src = dot_nt(normed, win_ref[row_chunk(k), :])
    src_ref[:, lane_chunk(k)] = src
    gate_ref[:, lane_chunk(k)] = dot_nt(normed, win_ref[row_chunk(k, inner), :])
    prm = params_of(small_ref, k)
    masks = lag_masks(lens_ref, src.shape, sm.taps)
    pre = conv_pre(src, prm, sm, masks)
    conved = pre * sigmoid(pre)
    exp_acc[...] += dot_nn(conved.astype(LOW), small_ref[row_chunk(k), 0:LANES])
    return conved


def scan_forward(rows, dl_ref, dx_ref, a, bb_ref, states, cc_ref=None, yp_ref=None, hist_ref=None, dec_ref=None):
    def block(tb, h):
        t0 = pl.multiple_of(tb * 8, 8)
        d8 = dl_ref[pl.ds(t0, 8), :]
        x8 = dx_ref[pl.ds(t0, 8), :]
        for j in range(8):
            d = jnp.broadcast_to(d8[j : j + 1, :], (states, CH))
            x = jnp.broadcast_to(x8[j : j + 1, :], (states, CH))
            dec = jnp.exp(d * a)
            at = pl.ds(pl.multiple_of(t0 * states, 8 * states) + j * states, states)
            h = h * dec + x * lanes3(bb_ref[at, :])
            if hist_ref is not None:
                hist_ref[at, :] = h
                dec_ref[at, :] = dec
            if yp_ref is not None:
                p = h * lanes3(cc_ref[at, :])
                ps = p[0:8]
                for i in range(1, states // 8):
                    ps = ps + p[8 * i : 8 * i + 8]
                put_planes(yp_ref, pl.ds(pl.multiple_of(t0 * 8, 64) + j * 8, 8), ps)
        return h

    lax.fori_loop(0, rows // 8, block, jnp.zeros((states, CH), F32))


class Forward:
    def __init__(self, sm, inner, lens_ref, count_ref, tok_ref, gain_ref, gain2_ref, win_ref, small_ref, wout_ref, outs, scratch):
        self.sm, self.inner = sm, inner
        self.lens, self.count, self.tok, self.gain, self.gain2 = lens_ref, count_ref, tok_ref, gain_ref, gain2_ref
        self.win, self.small, self.wout = win_ref, small_ref, wout_ref
        (self.normed, self.src, self.gate, self.lin, self.ym, self.exp, self.gated, self.middle, self.moe, self.sum) = outs
        self.conved, self.dl, self.dx, self.bb, self.cc, self.yp = scratch
        self.chunks = inner // CH
        self.rows = tok_ref.shape[0]

    def start(self):
        self.normed[...] = norm_of(self.tok[...].astype(F32), self.gain[...]).astype(LOW)
        self.exp[...] = jnp.zeros_like(self.exp)

    def project(self, k):
        self.conved[:, lane_chunk(k)] = forward_chunk_conv(
            k, self.sm, self.lens, self.normed, self.win, self.small, self.src, self.gate, self.exp, self.inner
        )

    def spread(self):
        sm = self.sm
        expanded = self.exp[...]
        spread(expanded, sm.rank, sm.states, self.bb)
        spread(expanded, sm.rank + sm.states, sm.states, self.cc)

    def scan(self, k):
        sm = self.sm
        expanded = self.exp[...]
        rate = jnp.where(lane_iota(expanded.shape) < sm.rank, expanded, 0.0).astype(LOW)
        prm = params_of(self.small, k)
        lin = dot_nt(rate, self.small[row_chunk(k), LANES : 2 * LANES]) + prm[sm.rate : sm.rate + 1, :]
        self.lin[:, lane_chunk(k)] = lin
        delta = softplus(lin)
        conved = self.conved[:, lane_chunk(k)]
        _, _, opening = segments(self.lens, lin.shape)
        self.dl[...] = jnp.where(opening, 1e30, delta)
        self.dx[...] = delta * conved
        a = -jnp.exp(prm[sm.alog : sm.alog + sm.states, :])
        scan_forward(self.rows, self.dl, self.dx, a, self.bb, sm.states, self.cc, self.yp)
        ym = rows_sum8(self.yp, self.rows) + prm[sm.skip : sm.skip + 1, :] * conved
        self.ym[:, lane_chunk(k)] = ym
        gate = self.gate[:, lane_chunk(k)]
        self.gated[:, lane_chunk(k)] = (ym * (gate * sigmoid(gate))).astype(LOW)

    def end(self):
        valid = row_iota((self.rows, 1)) < self.count[0]
        branch = jnp.where(valid, dot_nn(self.gated[...], self.wout[...]), 0.0)
        self.sum[...] = jnp.broadcast_to(jnp.sum(branch * branch), self.sum.shape)
        middle = self.tok[...].astype(F32) + branch
        self.middle[...] = middle
        self.moe[...] = norm_of(middle, self.gain2[...]).astype(LOW)


def mixer_forward_kernel(sm, inner, lens_ref, count_ref, tok_ref, gain_ref, gain2_ref, win_ref, small_ref, wout_ref, *refs):
    f = Forward(sm, inner, lens_ref, count_ref, tok_ref, gain_ref, gain2_ref, win_ref, small_ref, wout_ref, refs[:10], refs[10:])
    f.start()
    pl.loop(0, f.chunks)(f.project)
    f.spread()
    pl.loop(0, f.chunks)(f.scan)
    f.end()


def silu_grad(v, s):
    return s * (1.0 + v * (1.0 - s))


def norm_back(x, gain, grad):
    r = lax.rsqrt(jnp.mean(x * x, axis=-1, keepdims=True) + EPS)
    n = x * r
    q = grad * gain
    return r * (q - n * jnp.mean(q * n, axis=-1, keepdims=True)), grad * n


def scan_backward(rows, states, a, gs_ref, dx_ref, dt_ref, bb_ref, cc_ref, hist_ref, dec_ref, gcp_ref, gbp_ref, lbp_ref, amp_ref):
    blocks = rows // 8

    def fold8(p):
        out = p[0:8]
        for i in range(1, states // 8):
            out = out + p[8 * i : 8 * i + 8]
        return out

    def block(i, carry):
        back, total = carry
        tb = blocks - 1 - i
        t0 = pl.multiple_of(tb * 8, 8)
        g8 = gs_ref[pl.ds(t0, 8), :]
        x8 = dx_ref[pl.ds(t0, 8), :]
        d8 = dt_ref[pl.ds(t0, 8), :]
        for j in range(7, -1, -1):
            base = pl.multiple_of(t0 * states, 8 * states) + j * states
            at = pl.ds(base + states, states)
            prev = pl.ds(base, states)
            here = pl.ds(base, states)
            g = jnp.broadcast_to(g8[j : j + 1, :], (states, CH))
            x = jnp.broadcast_to(x8[j : j + 1, :], (states, CH))
            d = jnp.broadcast_to(d8[j : j + 1, :], (states, CH))
            adj = g * lanes3(cc_ref[here, :]) + back
            gcp_ref[here, :] += fold3(hist_ref[at, :] * g)
            gbp_ref[here, :] += fold3(adj * x)
            out8 = pl.ds(pl.multiple_of(t0 * 8, 64) + j * 8, 8)
            put_planes(lbp_ref, out8, fold8(adj * lanes3(bb_ref[here, :])))
            back = adj * dec_ref[here, :]
            m = back * hist_ref[prev, :]
            put_planes(amp_ref, out8, fold8(m * a))
            total = total + m * d
        return back, total

    zero = jnp.zeros((states, CH), F32)
    _, total = lax.fori_loop(0, blocks, block, (zero, zero))
    return total * a


def route(rows_in, router, code, experts):
    logits = dot_nt(rows_in, router)
    lane = lane_iota(logits.shape)
    logits = jnp.where(lane < experts, logits, -1e30)
    e = jnp.exp(logits - jnp.max(logits, axis=-1, keepdims=True))
    probs = e / jnp.sum(e, axis=-1, keepdims=True)
    expert = jnp.where(code >= experts, code - experts, code)
    onehot = (lane.astype(F32) == expert).astype(F32)
    return probs, onehot, jnp.sum(probs * onehot, axis=-1, keepdims=True)


def some(work, k, chunks):
    per = -(-len(work) // chunks)
    for i in range(chunks):
        share = work[i * per : (i + 1) * per]
        if share:
            def run(share=share):
                for item in share:
                    item()

            pl.when(k == i)(run)


def mixer_backward_kernel(
    sm, inner, experts, nz,
    lens_ref, count_ref, tok_ref, gain_ref, small_ref, gain2_ref,
    normed_ref, src_ref, gate_ref, lin_ref, ym_ref, exp_ref, gated_ref, middle_ref, moe_ref, sum_ref,
    gm_ref, gch_ref, gcode_ref, router_ref, win_ref, wout_ref, picked_ref,
    result_ref, gtok_ref, flat_ref, gsmall_ref, gwin_ref, gwout_ref, *refs,
):
    if nz:
        home_ref, refs = refs[0], refs[1:]
    (
        gmid_s, gmix_s, ggate_s, gconv_s, gs_s, dl_s, dx_s, dt_s, bb_s, cc_s, hist_s, dec_s, gcp_s, gbp_s, lbp_s, amp_s,
        grate_s, gnorm_s, pick_s, wbuf, outs, wsem, osem,
    ) = refs[:23]
    rows, width = tok_ref.shape
    states = sm.states
    chunks = inner // CH
    pieces = width // LANES

    def wout_in(k):
        return pltpu.make_async_copy(wout_ref.at[row_chunk(k), :], wbuf.at[k], wsem.at[k])

    for k in range(chunks):
        wout_in(k).start()
    todo = []
    if nz:
        place = Place(nz)
        place.barrier()
        s_out = Scatter(place, gwout_ref, *refs[23:31], nz)
        s_pick = Scatter(place, picked_ref, *refs[31:39], 2)
        todo = sorted(
            [(t, 0, step, k) for t, step, k in s_out.steps()] + [(t + 4, 1, step, k) for t, step, k in s_pick.steps()],
            key=lambda e: e[:2],
        )
        todo = [partial(step, k) for _, _, step, k in todo]
    early = todo[: 2 * chunks]
    late = todo[2 * chunks :]

    def put_flat(row, v):
        for i in range(pieces):
            flat_ref[row + i : row + i + 1, :] = v[:, i * LANES : (i + 1) * LANES]

    flat_ref[...] = jnp.zeros_like(flat_ref)
    gout = gcode_ref[:, 0:width].astype(F32)
    valid = row_iota((rows, 1)) < count_ref[0]
    code = gcode_ref[:, width : width + LANES].astype(F32)[:, 0:1]
    moe_in = moe_ref[...]
    probs, onehot, chosen = route(moe_in, router_ref[...], code, experts)
    if nz:
        gchosen = jnp.transpose(jnp.broadcast_to(gch_ref[0:1, :], (rows, LANES)))[:, 0:1]
    else:
        gchosen = jnp.sum(gout * picked_ref[...], axis=-1, keepdims=True)
    gchosen = jnp.where(valid, gchosen, 0.0)
    glogits = (probs * (onehot - chosen) * gchosen).astype(LOW)
    grouter = dot_tn(glogits, moe_in)
    for e in range(experts):
        put_flat((2 + e) * pieces, grouter[e : e + 1, :])
    gmoe = gm_ref[...] + dot_nn(glogits, router_ref[...])
    gmid, prod = norm_back(middle_ref[...], gain2_ref[...], gmoe)
    put_flat(pieces, jnp.sum(prod, axis=0, keepdims=True))
    gmid = gmid + gout
    gmid_s[...] = gmid
    gmix_s[...] = jnp.where(valid, gmid, 0.0).astype(LOW)

    def out_copy(which, k, base):
        dst = (gwout_ref, gwin_ref)[which]
        return pltpu.make_async_copy(outs.at[which, k % 2], dst.at[row_chunk(k, base), :], osem.at[which, k % 2])

    def put_out(which, k, base, v):
        @pl.when(k >= 2)
        def _():
            out_copy(which, k - 2, base).wait()

        outs[which, k % 2] = v.astype(LOW)
        out_copy(which, k, base).start()

    def end_out(which, base):
        for k in (chunks - 2, chunks - 1):
            out_copy(which, k, base).wait()

    @pl.loop(0, chunks)
    def _(k):
        wout_in(k).wait()
        gmix = gmix_s[...]
        gg = dot_nt(gmix, wbuf[k])
        put_out(0, k, 0, dot_tn(gated_ref[:, lane_chunk(k)], gmix))
        gate = gate_ref[:, lane_chunk(k)]
        s = sigmoid(gate)
        gs_s[:, lane_chunk(k)] = gg * (gate * s)
        ggate = (gg * ym_ref[:, lane_chunk(k)] * silu_grad(gate, s)).astype(LOW)
        ggate_s[:, lane_chunk(k)] = ggate
        put_out(1, k, inner, dot_tn(ggate, normed_ref[...]))

    end_out(0, 0)
    if nz:
        s_out.begin()
        s_pick.begin()
    end_out(1, inner)

    slots = chunks // 2

    def win_in(k, half):
        slot = (k % slots) * 2 + half
        return pltpu.make_async_copy(win_ref.at[row_chunk(k, half * inner), :], wbuf.at[slot], wsem.at[slot])

    for k in range(slots):
        win_in(k, 0).start()
        win_in(k, 1).start()
    expanded = exp_ref[...]
    lane = lane_iota((rows, LANES))
    rate = jnp.where(lane < sm.rank, expanded, 0.0).astype(LOW)
    spread(expanded, sm.rank, states, bb_s)
    spread(expanded, sm.rank + states, states, cc_s)
    grate_s[...] = jnp.zeros_like(grate_s)
    gcp_s[...] = jnp.zeros_like(gcp_s)
    gbp_s[...] = jnp.zeros_like(gbp_s)
    gnorm_s[...] = jnp.zeros_like(gnorm_s)
    hist_s[0:states, :] = jnp.zeros((states, CH), F32)

    @pl.loop(0, chunks)
    def _(k):
        prm = params_of(small_ref, k)
        src = src_ref[:, lane_chunk(k)]
        masks = lag_masks(lens_ref, src.shape, sm.taps)
        pre = conv_pre(src, prm, sm, masks)
        conved = pre * sigmoid(pre)
        lin = lin_ref[:, lane_chunk(k)]
        delta = softplus(lin)
        _, _, opening = segments(lens_ref, lin.shape)
        dl_s[...] = jnp.where(opening, 1e30, delta)
        dt_s[...] = delta
        dx_s[...] = delta * conved
        a = -jnp.exp(prm[sm.alog : sm.alog + states, :])
        gs_ref = gs_s.at[:, lane_chunk(k)]
        scan_forward(rows, dl_s, dx_s, a, bb_s, states, hist_ref=hist_s.at[pl.ds(states, rows * states), :], dec_ref=dec_s)
        galog = scan_backward(rows, states, a, gs_ref, dx_s, dt_s, bb_s, cc_s, hist_s, dec_s, gcp_s, gbp_s, lbp_s, amp_s)
        gs = gs_ref[...]
        lb = rows_sum8(lbp_s, rows)
        gdelta = rows_sum8(amp_s, rows) + conved * lb
        glin = gdelta * sigmoid(lin)
        gconv_s[:, lane_chunk(k)] = prm[sm.skip : sm.skip + 1, :] * gs + delta * lb
        glin_low = glin.astype(LOW)
        grate_s[...] += dot_nn(glin_low, small_ref[row_chunk(k), LANES : 2 * LANES])
        part = dot_tn(glin_low, rate)
        grows = jnp.concatenate(
            [
                jnp.zeros((sm.alog, CH), F32),
                galog,
                jnp.zeros((sm.taps + 1, CH), F32),
                jnp.sum(glin, axis=0, keepdims=True),
                jnp.sum(gs * conved, axis=0, keepdims=True),
                jnp.zeros((LANES - sm.end, CH), F32),
            ],
            axis=0,
        )
        gsmall_ref[row_chunk(k), LANES : 2 * LANES] = (part + jnp.transpose(grows)).astype(LOW)
        some(early, k, chunks)

    gexp = jnp.where(lane < sm.rank, grate_s[...], 0.0)
    for s in range(states):
        gb = jnp.sum(gbp_s[pl.ds(s, rows, stride=states), :], axis=1, keepdims=True)
        gc = jnp.sum(gcp_s[pl.ds(s, rows, stride=states), :], axis=1, keepdims=True)
        gexp = jnp.where(lane == sm.rank + s, gb, gexp)
        gexp = jnp.where(lane == sm.rank + states + s, gc, gexp)
    gexp_low = gexp.astype(LOW)

    @pl.loop(0, chunks)
    def _(k):
        prm = params_of(small_ref, k)
        src = src_ref[:, lane_chunk(k)]
        masks = lag_masks(lens_ref, src.shape, sm.taps)
        pre = conv_pre(src, prm, sm, masks)
        s = sigmoid(pre)
        conved_low = (pre * s).astype(LOW)
        gsmall_ref[row_chunk(k), 0:LANES] = dot_tn(conved_low, gexp_low).astype(LOW)
        gconv = gconv_s[:, lane_chunk(k)] + dot_nt(gexp_low, small_ref[row_chunk(k), 0:LANES])
        p = gconv * silu_grad(pre, s)
        gsrc = prm[sm.conv : sm.conv + 1, :] * p
        taps = [jnp.sum(p * src, axis=0, keepdims=True)]
        for lag in range(1, sm.taps):
            pm = jnp.where(masks[lag], p, 0.0)
            taps.append(jnp.sum(pm * pltpu.roll(src, lag, 0), axis=0, keepdims=True))
            gsrc = gsrc + prm[sm.conv + lag : sm.conv + lag + 1, :] * pltpu.roll(pm, rows - lag, 0)
        grows = jnp.concatenate(
            [jnp.zeros((sm.conv, CH), F32)]
            + taps
            + [jnp.sum(p, axis=0, keepdims=True), jnp.zeros((LANES - sm.bias - 1, CH), F32)],
            axis=0,
        )
        old = gsmall_ref[row_chunk(k), LANES : 2 * LANES].astype(F32)
        gsmall_ref[row_chunk(k), LANES : 2 * LANES] = (old + jnp.transpose(grows)).astype(LOW)
        gsrc_low = gsrc.astype(LOW)
        put_out(1, k, 0, dot_tn(gsrc_low, normed_ref[...]))
        win_in(k, 0).wait()
        win_in(k, 1).wait()
        slot = (k % slots) * 2
        gnorm_s[...] += dot_nn(gsrc_low, wbuf[slot]) + dot_nn(ggate_s[:, lane_chunk(k)], wbuf[slot + 1])

        @pl.when(k + slots < chunks)
        def _():
            win_in(k + slots, 0).start()
            win_in(k + slots, 1).start()

        some(late, k, chunks)

    gtok, prod = norm_back(tok_ref[...].astype(F32), gain_ref[...], gnorm_s[...])
    put_flat(0, jnp.sum(prod, axis=0, keepdims=True))
    gtok_ref[...] = gtok + gmid_s[...]
    end_out(1, 0)
    if nz:
        s_pick.result(pick_s)
        picked = pick_s[...]
    else:
        picked = picked_ref[...]
    two = chosen * jnp.where(valid, picked, 0.0)
    result = middle_ref[...] + two
    result_ref[...] = result.astype(LOW)
    squares = jnp.where(valid, result * result, 0.0)
    lane1 = lane_iota((1, LANES))
    stats = jnp.where(lane1 == 0, jnp.sum(squares), 0.0)
    stats = jnp.where(lane1 == 1, sum_ref[0:1, :], stats)
    stats = jnp.where(lane1 == 2, jnp.sum(two * two), stats)
    stats = jnp.where(lane1 == 3, count_ref[0].astype(F32), stats)
    flat_ref[(2 + experts) * pieces : (2 + experts) * pieces + 1, :] = stats
    if nz:
        s_out.result(home_ref)
        s_out.finish()
        s_pick.finish()


VMEM = pltpu.VMEM
SMEM_SPEC = pl.BlockSpec(memory_space=pltpu.SMEM)
VMEM_SPEC = pl.BlockSpec(memory_space=pltpu.VMEM)


def shape_of(shape, dtype):
    return jax.ShapeDtypeStruct(shape, dtype)


def forward_outs(sm, rows, width, inner):
    return (
        shape_of((rows, width), LOW),
        shape_of((rows, inner), F32),
        shape_of((rows, inner), F32),
        shape_of((rows, inner), F32),
        shape_of((rows, inner), F32),
        shape_of((rows, LANES), F32),
        shape_of((rows, inner), LOW),
        shape_of((rows, width), F32),
        shape_of((rows, width), LOW),
        shape_of((8, LANES), F32),
    )


def forward_scratch(sm, rows, inner):
    st = sm.states
    return [
        VMEM((rows, inner), F32),
        VMEM((rows, CH), F32),
        VMEM((rows, CH), F32),
        VMEM((rows * st, LANES), F32),
        VMEM((rows * st, LANES), F32),
        VMEM((CH // LANES, rows * 8, LANES), F32),
    ]


def mixer_forward(sm, lens, count, tokens, gain, gain2, win, small, wout):
    rows, width = tokens.shape
    inner = wout.shape[0]
    return pl.pallas_call(
        partial(mixer_forward_kernel, sm, inner),
        out_shape=forward_outs(sm, rows, width, inner),
        in_specs=[SMEM_SPEC] * 2 + [VMEM_SPEC] * 6,
        out_specs=(VMEM_SPEC,) * 10,
        scratch_shapes=forward_scratch(sm, rows, inner),
        compiler_params=pltpu.CompilerParams(vmem_limit_bytes=60 << 20),
        name="mixer_forward",
    )(lens, count, tokens, gain, gain2, win, small, wout)


def flat_rows(width, experts):
    return -(-((2 + experts) * (width // LANES) + 1) // 8) * 8


MESH = pl.DeviceIdType.MESH


class Place:
    def __init__(self, nz):
        self.nz = nz
        w, n = lax.axis_index("wide"), lax.axis_index("narrow")
        self.z, self.y, self.x, self.c = w // 2, w % 2, n // 2, n % 2

    def flips(self, f2, f3):
        fx = f2 * (1 - self.c) + f3 * self.c
        fy = f3 * (1 - self.c) + f2 * self.c
        return self.x + fx - 2 * self.x * fx, self.y + fy - 2 * self.y * fy

    def device(self, z, f2, f3, fc):
        x, y = self.flips(f2, f3)
        core = 1 - self.c if fc else self.c
        return (z * 2 + y, x * 2 + core)

    def target(self, kind):
        if kind == "sib":
            return self.device(self.z, 0, 0, 1)
        if kind == "d2":
            return self.device(self.z, 1, 0, 0)
        if kind == "d3":
            return self.device(self.z, 0, 1, 0)
        if kind == "far":
            return self.device((self.z + self.nz // 2) % self.nz, 0, 0, 0)
        return self.device(self.z + kind, 0, 0, 0)

    def block(self, zloc, f2, f3, fc):
        x, y = self.flips(f2, f3)
        return zloc * 8 + y * 4 + x * 2 + self.c + fc - 2 * fc * self.c

    def has(self, side, group):
        at = self.z % group + side
        return (at >= 0) & (at < group)

    def barrier(self, far=0):
        sem = pltpu.get_barrier_semaphore()
        for kind in ("sib", "d2", "d3") + (("far",) if far else ()):
            pl.semaphore_signal(sem, inc=1, device_id=self.target(kind), device_id_type=MESH)
        for side in (-1, 1):
            @pl.when(self.has(side, self.nz))
            def _():
                pl.semaphore_signal(sem, inc=1, device_id=self.target(side), device_id_type=MESH)
        below = (self.z + self.nz - 1) // self.nz
        above = (2 * self.nz - 2 - self.z) // self.nz
        pl.semaphore_wait(sem, 3 + far + below + above)


def when(cond, body):
    if cond is True:
        body()
    else:
        pl.when(cond)(body)


class Gather:
    def __init__(self, place, src, out, send, recv, local, group):
        self.place, self.src, self.out, self.send, self.recv, self.local, self.group = place, src, out, send, recv, local, group
        self.rows = src.shape[0]
        self.slots = 0
        self.sent = []

    def at(self, p):
        return self.out.at[pl.ds(pl.multiple_of(p * self.rows, 8), self.rows), :]

    def copy(self, src, p, kind, slot):
        return pltpu.make_async_remote_copy(
            src, self.at(p), self.send.at[slot], self.recv.at[p], device_id=self.place.target(kind), device_id_type=MESH
        )

    def push(self, rel, kinds):
        for kind in kinds:
            slot = self.slots
            self.slots += 1
            self.sent.append((rel, kind, slot))

            def go(kind=kind, slot=slot):
                p, src = self.source(rel)
                self.copy(src, p, kind, slot).start()

            when(self.extra(kind), go)

    def extra(self, kind):
        return True if isinstance(kind, str) else self.place.has(kind, self.group)

    def source(self, rel):
        zloc = self.place.z % self.group
        if rel is None:
            return self.place.block(zloc, 0, 0, 0), self.src
        p = self.place.block(zloc + rel[0], rel[1], rel[2], 0)
        return p, self.at(p)

    def begin(self):
        p, src = self.source(None)
        self.push(None, [-1, 1, "d2", "d3", "sib"])
        pltpu.make_async_copy(src, self.at(p), self.local).start()

    def wait_block(self, p):
        self.copy(self.src, p, "sib", 0).wait_recv()

    def events(self):
        out = []
        for dist in range(-self.group + 1, self.group):
            for f2 in (0, 1):
                for f3 in (0, 1):
                    if dist or f2 or f3:
                        out.append((abs(dist) + f2 + 2 * f3, dist, f2, f3))
        return sorted(out)

    def handle(self, dist, f2, f3):
        zloc = self.place.z % self.group
        cond = True if dist == 0 else self.place.has(dist, self.group)
        kinds = ["sib"]
        if not f3:
            kinds = ["d3"] + kinds
            if not f2:
                kinds = [1 if dist < 0 else -1, "d2"] + kinds

        def body():
            self.wait_block(self.place.block(zloc + dist, f2, f3, 0))
            self.push((dist, f2, f3), kinds)

        when(cond, body)

    def own_wait(self):
        p, src = self.source(None)
        pltpu.make_async_copy(src, self.at(p), self.local).wait()

    def finish(self):
        self.own_wait()
        for f2 in (0, 1):
            for f3 in (0, 1):
                for z in range(self.group):
                    self.wait_block(self.place.block(z, f2, f3, 1))
        self.finish_sends()

    def finish_sends(self):
        for rel, kind, slot in self.sent:
            def end(rel=rel, kind=kind, slot=slot):
                def inner():
                    p, src = self.source(rel)
                    self.copy(src, p, kind, slot).wait_send()

                when(self.extra(kind), inner)

            when(True if rel is None or not rel[0] else self.place.has(rel[0], self.group), end)

    @staticmethod
    def sends(group):
        return 5 + sum(2 + (not f3) + 2 * ((not f3) and (not f2)) for d in range(-group + 1, group) for f2 in (0, 1) for f3 in (0, 1))


def run_gathers(gathers):
    for g in gathers:
        g.begin()
    events = []
    for i, g in enumerate(gathers):
        events += [(e[0], i) + e[1:] for e in g.events()]
    for _, i, dist, f2, f3 in sorted(events):
        gathers[i].handle(dist, f2, f3)
    for g in gathers:
        g.finish()


class Exchange:
    def __init__(self, place, src, out, sems):
        self.copy = pltpu.make_async_remote_copy(
            src, out, sems.at[0], sems.at[1], device_id=place.target("far"), device_id_type=MESH
        )
        self.start, self.wait = self.copy.start, self.copy.wait


class Scatter:
    def __init__(self, place, src, acc, rsib, rd3, rd2, rz, send, recv, local, group):
        self.place, self.src, self.acc = place, src, acc
        self.rows = rsib.shape[1]
        self.rsib, self.rd3, self.rd2, self.rz = rsib, rd3, rd2, rz
        self.send, self.recv, self.local, self.group = send, recv, local, group
        z = place.z % group
        self.zloc = z
        if group == 2:
            self.order = [(1 - z, 1 - 2 * z)]
        else:
            h, low = z // 2, z % 2
            self.order = [(3 * (1 - h), 1 - 2 * h), (2 - h, 1 - 2 * h), (2 * h + 1 - low, 1 - 2 * low)]
        self.dests = [zz for zz, _ in self.order] + [z]

    def copy(self, src, dst, send, recv, target):
        return pltpu.make_async_remote_copy(
            src, dst, self.send.at[send], self.recv.at[recv], device_id=target, device_id_type=MESH
        )

    def part(self, p):
        if len(self.src.shape) == 3:
            return self.src.at[p]
        return self.src.at[pl.ds(pl.multiple_of(p * self.rows, 8), self.rows), :]

    def sum(self, zz, f2, f3):
        if self.acc is None:
            return self.part(self.place.block(zz, f2, f3, 0))
        return self.acc.at[zz * 4 + f2 * 2 + f3]

    def to_sib(self, k, f2, f3):
        at = self.dests[k] * 4 + f3 * 2 + f2
        src = self.part(self.place.block(self.dests[k], f2, f3, 1))
        return self.copy(src, self.rsib.at[at], k * 4 + f2 * 2 + f3, at, self.place.target("sib"))

    def to_d3(self, k, f2):
        zz, group = self.dests[k], self.group
        row = 4 * group + k * 2 + f2
        return self.copy(
            self.sum(zz, f2, 1), self.rd3.at[zz * 2 + f2], row, 4 * group + zz * 2 + f2, self.place.target("d3")
        )

    def to_d2(self, k):
        zz, group = self.dests[k], self.group
        return self.copy(self.sum(zz, 1, 0), self.rd2.at[zz], 6 * group + k, 6 * group + zz, self.place.target("d2"))

    def zrow(self, zz, side):
        return zz + self.group * (1 + side) // 2

    def to_z(self, k):
        zz, side = self.order[k]
        row = self.zrow(zz, side)
        return self.copy(self.sum(zz, 0, 0), self.rz.at[row], 7 * self.group + k, 7 * self.group + row, self.place.target(side))

    def received(self, ref, row):
        pltpu.make_async_remote_copy(
            ref, ref, self.send.at[0], self.recv.at[row], device_id=self.place.target("sib"), device_id_type=MESH
        ).wait_recv()
        return ref

    def from_z(self, zz, side):
        row = self.zrow(zz, side)
        return self.received(self.rz.at[row], 7 * self.group + row)

    def local_copy(self, k, f2, f3):
        return pltpu.make_async_copy(
            self.part(self.place.block(self.dests[k], f2, f3, 0)),
            self.sum(self.dests[k], f2, f3),
            self.local.at[k * 4 + f2 * 2 + f3],
        )

    def begin(self):
        for k in range(self.group):
            for f2, f3 in ((1, 1), (1, 0), (0, 1), (0, 0)):
                self.to_sib(k, f2, f3).start()
            if self.acc is not None:
                for f2, f3 in ((1, 1), (0, 1), (1, 0), (0, 0)):
                    self.local_copy(k, f2, f3).start()

    def add(self, acc, ref):
        @pl.loop(0, ref.shape[-1] // LANES)
        def _(i):
            lanes = pl.ds(pl.multiple_of(i * LANES, LANES), LANES)
            acc[:, lanes] = acc[:, lanes] + ref[:, lanes]

    def own(self, k, f2, f3):
        at = self.dests[k] * 4 + f2 * 2 + f3
        if self.acc is not None:
            self.local_copy(k, f2, f3).wait()
        acc = self.sum(self.dests[k], f2, f3)
        self.add(acc, self.received(self.rsib.at[at], at))
        return acc

    def step_a(self, k):
        for f2 in (1, 0):
            self.own(k, f2, 1)
            self.to_d3(k, f2).start()

    def add_d3(self, k, f2, at):
        row = self.dests[k] * 2 + f2
        self.add(at, self.received(self.rd3.at[row], 4 * self.group + row))

    def step_b(self, k):
        at = self.own(k, 1, 0)
        self.add_d3(k, 1, at)
        self.to_d2(k).start()

    def step_c(self, k):
        at = self.own(k, 0, 0)
        self.add_d3(k, 0, at)
        zz = self.dests[k]
        self.add(at, self.received(self.rd2.at[zz], 6 * self.group + zz))
        if k < self.group - 1:
            side = self.order[k][1]

            @pl.when(self.place.has(-side, self.group))
            def _():
                self.add(at, self.from_z(zz, side))

            self.to_z(k).start()

    def result(self, out):
        out[...] = self.sum(self.zloc, 0, 0)[...].astype(out.dtype)
        for side in (-1, 1):
            @pl.when(self.place.has(side, self.group))
            def _():
                out[...] += self.from_z(self.zloc, -side)[...].astype(out.dtype)

    def steps(self):
        out = []
        for k in range(self.group):
            out += [(3 * k, self.step_a, k), (3 * k + 4, self.step_b, k), (3 * k + 8, self.step_c, k)]
        return sorted(out, key=lambda e: e[0])

    def finish(self):
        for k in range(self.group):
            for f2 in (0, 1):
                for f3 in (0, 1):
                    self.to_sib(k, f2, f3).wait_send()
                self.to_d3(k, f2).wait_send()
            self.to_d2(k).wait_send()
            if k < self.group - 1:
                self.to_z(k).wait_send()

    @staticmethod
    def scratch(group, rows, cols, dtype, in_place=False):
        return [
            VMEM((8, LANES) if in_place else (4 * group, rows, cols), dtype),
            VMEM((4 * group, rows, cols), dtype),
            VMEM((2 * group, rows, cols), dtype),
            VMEM((group, rows, cols), dtype),
            VMEM((2 * group, rows, cols), dtype),
            pltpu.SemaphoreType.DMA((8 * group,)),
            pltpu.SemaphoreType.DMA((9 * group,)),
            pltpu.SemaphoreType.DMA((4 * group,)),
        ]


def run_scatters(scatters, outs, gathers=()):
    for g in gathers:
        g.begin()
    for s in scatters:
        s.begin()
    steps = []
    for i, s in enumerate(scatters):
        steps += [(t, i, step, k) for t, step, k in s.steps()]
    for _, _, step, k in sorted(steps, key=lambda e: e[:2]):
        step(k)
    for g in gathers:
        for _, dist, f2, f3 in g.events():
            g.handle(dist, f2, f3)
    for s, out in zip(scatters, outs):
        s.result(out)
    for s in scatters:
        s.finish()
    for g in gathers:
        g.finish()


ANY_SPEC = pl.BlockSpec(memory_space=pl.ANY)


def gather_scratch(group):
    return [
        pltpu.SemaphoreType.DMA((Gather.sends(group),)),
        pltpu.SemaphoreType.DMA((group * 8,)),
        pltpu.SemaphoreType.DMA,
    ]


def gather_kernel(nz, groups, *refs):
    n = len(groups)
    srcs, outs, scr = refs[:n], refs[n : 2 * n], refs[2 * n :]
    place = Place(nz)
    place.barrier()
    run_gathers(
        [Gather(place, srcs[i], outs[i], *scr[3 * i : 3 * i + 3], groups[i]) for i in range(n)]
    )


def gather_call(nz, groups, arrays, collective_id):
    return pl.pallas_call(
        partial(gather_kernel, nz, groups),
        out_shape=tuple(shape_of((g * 8 * a.shape[0], a.shape[1]), a.dtype) for g, a in zip(groups, arrays)),
        in_specs=[ANY_SPEC] * len(arrays),
        out_specs=(ANY_SPEC,) * len(arrays),
        scratch_shapes=sum([gather_scratch(g) for g in groups], []),
        compiler_params=pltpu.CompilerParams(collective_id=collective_id, has_side_effects=True, vmem_limit_bytes=60 << 20),
        name="gather_blocks",
    )(*arrays)


def scatter_kernel(nz, groups, gathered, *refs):
    n = len(groups)
    g = len(gathered)
    srcs, gsrcs, outs, gouts, scr = refs[:n], refs[n : n + g], refs[n + g : 2 * n + g], refs[2 * n + g : 2 * n + 2 * g], refs[2 * n + 2 * g :]
    place = Place(nz)
    place.barrier()
    scatters = [Scatter(place, srcs[i], *scr[8 * i : 8 * i + 8], groups[i]) for i in range(n)]
    more = scr[8 * n :]
    gathers = [Gather(place, gsrcs[i], gouts[i], *more[3 * i : 3 * i + 3], gathered[i]) for i in range(g)]
    run_scatters(scatters, outs, gathers)


def scatter_call(nz, groups, arrays, gathered, garrays, collective_id):
    return pl.pallas_call(
        partial(scatter_kernel, nz, groups, gathered),
        out_shape=tuple(shape_of((a.shape[0] // (8 * g), a.shape[1]), F32) for g, a in zip(groups, arrays))
        + tuple(shape_of((g * 8 * a.shape[0], a.shape[1]), a.dtype) for g, a in zip(gathered, garrays)),
        in_specs=[ANY_SPEC] * (len(arrays) + len(garrays)),
        out_specs=(VMEM_SPEC,) * len(arrays) + (ANY_SPEC,) * len(garrays),
        scratch_shapes=sum([Scatter.scratch(g, a.shape[0] // (8 * g), a.shape[1], a.dtype) for g, a in zip(groups, arrays)], [])
        + sum([gather_scratch(g) for g in gathered], []),
        compiler_params=pltpu.CompilerParams(collective_id=collective_id, has_side_effects=True, vmem_limit_bytes=60 << 20),
        name="scatter_blocks",
    )(*arrays, *garrays)


def forward_gather_kernel(sm, inner, nz, lens_ref, count_ref, tok_ref, gain_ref, gain2_ref, *refs):
    srcs, mine, outs, alls, other, refs = refs[:4], refs[4], refs[5:15], refs[15:19], refs[19], refs[20:]
    win_v, small_v, wout_v, load = refs[:4]
    fwd_scratch, far, sems = refs[4:10], refs[10], refs[11:]
    place = Place(nz)
    f = Forward(sm, inner, lens_ref, count_ref, tok_ref, gain_ref, gain2_ref, win_v, small_v, wout_v, outs, fwd_scratch)
    place.barrier(1)
    exchange = Exchange(place, mine, other, far)
    groups = (nz, nz, nz, 2)
    g_win, g_small, g_wout, g_code = (
        Gather(place, srcs[i], alls[i], *sems[3 * i : 3 * i + 3], groups[i]) for i in range(4)
    )
    win_hbm, small_hbm, wout_hbm = alls[:3]
    g_small.begin()
    g_win.begin()
    f.start()
    events = [(e[0], i) + e[1:] for i, g in ((0, g_small), (1, g_win)) for e in g.events()]
    events = sorted(events)
    last_z = max(n for n, e in enumerate(events) if e[3] == 0 and e[4] == 0)
    late = len(events) * 3 // 4
    for n, (_, i, dist, f2, f3) in enumerate(events):
        (g_small, g_win)[i].handle(dist, f2, f3)
        if n == last_z:
            exchange.start()
        if n == late:
            g_wout.begin()
    g_small.finish()
    small_in = pltpu.make_async_copy(small_hbm, small_v, load.at[0])
    small_in.start()
    g_win.finish()

    def win_in(k, half):
        rows = row_chunk(k, half * inner)
        return pltpu.make_async_copy(win_hbm.at[rows, :], win_v.at[rows, :], load.at[2 + 2 * k + half])

    for k in range(f.chunks):
        win_in(k, 0).start()
        win_in(k, 1).start()
    small_in.wait()
    todo = [partial(g_wout.handle, *e[1:]) for e in g_wout.events()]
    todo = todo + [g_code.begin] + [partial(g_code.handle, *e[1:]) for e in g_code.events()]
    split = len(todo) // 3
    first, second = todo[:split], todo[split:]

    @pl.loop(0, f.chunks)
    def _(k):
        win_in(k, 0).wait()
        win_in(k, 1).wait()
        f.project(k)
        some(first, k, f.chunks)

    f.spread()

    @pl.loop(0, f.chunks)
    def _(k):
        f.scan(k)
        some(second, k, f.chunks)

    g_wout.finish()
    wout_in = pltpu.make_async_copy(wout_hbm, wout_v, load.at[1])
    wout_in.start()
    wout_in.wait()
    f.end()
    g_code.finish()
    exchange.wait()


def forward_gather(sm, nz, lens, count, tokens, gain, gain2, win, small, wout, gcode, mine, collective_id):
    rows, width = tokens.shape
    devices = 8 * nz
    inner = wout.shape[0] * devices
    alls = tuple(shape_of((a.shape[0] * g * 8, a.shape[1]), a.dtype) for g, a in ((nz, win), (nz, small), (nz, wout), (2, gcode)))
    return pl.pallas_call(
        partial(forward_gather_kernel, sm, inner, nz),
        out_shape=forward_outs(sm, rows, width, inner) + alls + (shape_of(mine.shape, mine.dtype),),
        in_specs=[SMEM_SPEC] * 2 + [VMEM_SPEC] * 3 + [ANY_SPEC] * 5,
        out_specs=(VMEM_SPEC,) * 10 + (ANY_SPEC,) * 5,
        scratch_shapes=[VMEM(a.shape, a.dtype) for a in alls[:3]]
        + [pltpu.SemaphoreType.DMA((2 + 2 * (inner // CH),))]
        + forward_scratch(sm, rows, inner)
        + [pltpu.SemaphoreType.DMA((2,))]
        + sum([gather_scratch(g) for g in (nz, nz, nz, 2)], []),
        compiler_params=pltpu.CompilerParams(collective_id=collective_id, has_side_effects=True, vmem_limit_bytes=62 << 20),
        name="forward_gather",
    )(lens, count, tokens, gain, gain2, win, small, wout, gcode, mine)


GELU_A = 0.7978845608028654
GELU_B = 0.044715


def gelu_parts(v):
    inside = GELU_A * (v + GELU_B * v * v * v)
    t = jnp.tanh(inside)
    slope = 0.5 * (1.0 + t) + 0.5 * v * (1.0 - t * t) * (GELU_A * (1.0 + 3.0 * GELU_B * v * v))
    return 0.5 * v * (1.0 + t), slope


def expert_kernel(
    experts, nz, moe_ref, gcode_ref, mine_ref, other_ref, router_ref,
    picked_ref, gm_ref, gch_ref, gmine_ref, gother_ref,
    all_s, wu_s, wd_s, gm_s, gch_s, go_s, gpre_s, hid_s, *refs,
):
    sems, refs = refs[:3], refs[3:]
    group = 2
    rows, width = moe_ref.shape
    block = 2 * rows
    units = mine_ref.shape[0] // 2
    per = units // experts
    place = Place(nz)
    place.barrier()
    gather = Gather(place, moe_ref, all_s, *sems, group)
    grads = Scatter(place, gm_s, None, *refs[1:8], group)
    chosens = Scatter(place, gch_s, None, *refs[9:16], group)
    gather.begin()
    wu_s[0:units, :] = mine_ref[0:units, :]
    wu_s[units : 2 * units, :] = other_ref[0:units, :]
    wd_s[0:units, :] = mine_ref[units : 2 * units, :]
    wd_s[units : 2 * units, :] = other_ref[units : 2 * units, :]
    chips = [(fy, fx, far) for fy in (0, 1) for fx in (0, 1) for far in (0, 1)]
    own = {1: [(0, 0)], 2: [(1, 0), (0, 1)], 3: [(1, 0), (0, 1)], 6: [(1, 1)], 7: [(1, 1)]}
    zloc = place.z % group
    zfar = 1 - zloc

    def turn(fx, fy):
        return fx * (1 - place.c) + fy * place.c, fy * (1 - place.c) + fx * place.c

    @pl.loop(0, len(chips))
    def _(i):
        for j, (fy, fx, far) in enumerate(chips):
            @pl.when(i == j)
            def _():
                if j == 0:
                    gather.own_wait()
                for f2, f3 in own.get(j, []):
                    for dist in (-1, 1) if far else (0,):
                        gather.handle(dist, f2, f3)
                gather.wait_block(place.block(zfar if far else zloc, *turn(fx, fy), 1))

        far, fx, fy = i % 2, (i // 2) % 2, i // 4
        first = place.block(zloc + far - 2 * far * zloc, *turn(fx, fy), place.c)
        chip = first // 2
        at = pl.ds(pl.multiple_of(chip * block, block), block)
        m = all_s[at, :]
        code = gcode_ref[at, width : width + LANES].astype(F32)[:, 0:1]
        _, _, chosen = route(m, router_ref[...], code, experts)
        live = code < experts
        expert = jnp.where(live, code, code - experts)
        scale = jnp.where(live, chosen, 0.0)
        col = lane_iota((block, 2 * units))
        col = jnp.where(col >= units, col - units, col).astype(F32)
        mask = (col >= expert * per) & (col < (expert + 1.0) * per)
        act, slope = gelu_parts(dot_nt(m, wu_s[...]))
        act = jnp.where(mask, act, 0.0)
        hidden = act.astype(LOW)
        picked_ref[at, :] = dot_nn(hidden, wd_s[...]).astype(LOW)
        g = gcode_ref[at, 0:width]
        back = dot_nt(g, wd_s[...])
        gch = jnp.sum(hidden.astype(F32) * back, axis=1, keepdims=True)
        gpre = jnp.where(mask, scale * back * slope, 0.0).astype(LOW)
        gm = dot_nn(gpre, wu_s[...]).astype(LOW)
        for c in range(2):
            gm_s[2 * chip + c] = gm[c * rows : (c + 1) * rows, :]
            turned = jnp.transpose(jnp.broadcast_to(gch[c * rows : (c + 1) * rows, :], (rows, LANES)))
            gch_s[2 * chip + c] = turned[0:8, :]
        go_s[at, :] = (scale * g.astype(F32)).astype(LOW)
        lanes = pl.ds(pl.multiple_of(chip * block, block), block)
        gpre_s[:, lanes] = jnp.transpose(gpre)
        hid_s[:, lanes] = jnp.transpose(hidden)
        for j, (fy, fx, far) in enumerate(chips):
            @pl.when(i == j)
            def _():
                grads.to_sib(1 - far, *turn(fx, fy)).start()
                chosens.to_sib(1 - far, *turn(fx, fy)).start()

    def weights(j):
        half = 3
        left, right, base = (gpre_s, all_s, 0) if j < half else (hid_s, go_s, units)
        step = width // half
        at = slice((j % half) * step, (j % half + 1) * step)
        part = dot_nn(left[...], right[:, at])
        gmine_ref[base : base + units, at] = part[0:units, :]
        gother_ref[base : base + units, at] = part[units : 2 * units, :].astype(LOW)

    steps = [(grads.step_a, 0), (grads.step_a, 1), (grads.step_b, 0), (grads.step_b, 1), (grads.step_c, 0), (grads.step_c, 1)]
    for j, (step, k) in enumerate(steps):
        step(k)
        (chosens.step_a, chosens.step_b, chosens.step_c)[j // 2](k)
        weights(j)
    grads.result(gm_ref)
    chosens.result(gch_ref)
    grads.finish()
    chosens.finish()
    gather.finish_sends()


def expert_call(experts, nz, moe_in, gcode_all, mine, other, router, collective_id):
    rows, width = moe_in.shape
    tokens = rows * 16
    units = mine.shape[0]
    return pl.pallas_call(
        partial(expert_kernel, experts, nz),
        out_shape=(
            shape_of((tokens, width), LOW),
            shape_of((rows, width), F32),
            shape_of((8, LANES), F32),
            shape_of((units, width), F32),
            shape_of((units, width), LOW),
        ),
        in_specs=[ANY_SPEC] + [VMEM_SPEC] * 4,
        out_specs=(VMEM_SPEC,) * 5,
        scratch_shapes=[
            VMEM((tokens, width), LOW),
            VMEM((units, width), LOW),
            VMEM((units, width), LOW),
            VMEM((16, rows, width), LOW),
            VMEM((16, 8, LANES), F32),
            VMEM((tokens, width), LOW),
            VMEM((units, tokens), LOW),
            VMEM((units, tokens), LOW),
        ]
        + gather_scratch(2)
        + Scatter.scratch(2, rows, width, LOW, True)
        + Scatter.scratch(2, 8, LANES, F32, True),
        compiler_params=pltpu.CompilerParams(collective_id=collective_id, has_side_effects=True, vmem_limit_bytes=62 << 20),
        name="experts",
    )(moe_in, gcode_all, mine, other, router)


def mixer_backward(sm, experts, nz, lens, count, tokens, gain, small, gain2, saved, gm, gch, gcode, router, win, wout, picked, collective_id):
    rows, width = tokens.shape
    inner = wout.shape[0]
    st = sm.states
    chunks = inner // CH
    here = inner // (8 * nz) if nz else 0
    return pl.pallas_call(
        partial(mixer_backward_kernel, sm, inner, experts, nz),
        out_shape=(
            shape_of((rows, width), LOW),
            shape_of((rows, width), F32),
            shape_of((flat_rows(width, experts), LANES), F32),
            shape_of((inner, 2 * LANES), LOW),
            shape_of((2 * inner, width), LOW),
            shape_of((inner, width), LOW),
        )
        + ((shape_of((here, width), F32),) if nz else ()),
        in_specs=[SMEM_SPEC] * 2 + [VMEM_SPEC] * 18 + [ANY_SPEC] * 2 + [ANY_SPEC if nz else VMEM_SPEC],
        out_specs=(VMEM_SPEC,) * 4 + (ANY_SPEC,) * 2 + ((VMEM_SPEC,) if nz else ()),
        scratch_shapes=[
            VMEM((rows, width), F32),
            VMEM((rows, width), LOW),
            VMEM((rows, inner), LOW),
            VMEM((rows, inner), F32),
            VMEM((rows, inner), F32),
            VMEM((rows, CH), F32),
            VMEM((rows, CH), F32),
            VMEM((rows, CH), F32),
            VMEM((rows * st, LANES), F32),
            VMEM((rows * st, LANES), F32),
            VMEM(((rows + 1) * st, CH), F32),
            VMEM((rows * st, CH), F32),
            VMEM((rows * st, LANES), F32),
            VMEM((rows * st, LANES), F32),
            VMEM((CH // LANES, rows * 8, LANES), F32),
            VMEM((CH // LANES, rows * 8, LANES), F32),
            VMEM((rows, LANES), F32),
            VMEM((rows, width), F32),
            VMEM((rows, width), F32),
            VMEM((chunks, CH, width), LOW),
            VMEM((2, 2, CH, width), LOW),
            pltpu.SemaphoreType.DMA((chunks,)),
            pltpu.SemaphoreType.DMA((2, 2)),
        ]
        + (Scatter.scratch(nz, here, width, LOW) + Scatter.scratch(2, rows, width, LOW) if nz else []),
        compiler_params=pltpu.CompilerParams(
            collective_id=collective_id if nz else None, has_side_effects=bool(nz), vmem_limit_bytes=63 << 20
        ),
        name="mixer_backward",
    )(lens, count, tokens, gain, small, gain2, *saved, gm, gch, gcode, router, win, wout, picked)


AXES = ("wide", "narrow")


def experts_local(moe_in, gcode, w_up, w_down, router, experts):
    width = moe_in.shape[1]
    ups = lax.all_gather(w_up, AXES, axis=2, tiled=True)
    downs = lax.all_gather(w_down, AXES, axis=1, tiled=True)
    code = gcode[:, width : width + 1].astype(F32)
    _, onehot, chosen = route(moe_in, router, code, experts)
    onehot = onehot[:, :experts]
    pre = jnp.einsum("td,edf->etf", moe_in, ups, preferred_element_type=F32)
    act, slope = gelu_parts(pre)
    hidden = act.astype(LOW)
    outs = jnp.einsum("etf,efd->etd", hidden, downs, preferred_element_type=F32)
    picked = jnp.sum(onehot.T[:, :, None] * outs, axis=0)
    scaled = (jnp.where(code < experts, chosen, 0.0) * gcode[:, :width].astype(F32)).astype(LOW)
    grad_expert = onehot.T.astype(LOW)[:, :, None] * scaled[None]
    grad_down = jnp.einsum("etf,etd->fed", hidden, grad_expert, preferred_element_type=LOW)
    grad_act = jnp.einsum("etd,efd->etf", grad_expert, downs, preferred_element_type=F32)
    grad_pre = (grad_act * slope).astype(LOW)
    grad_up = jnp.einsum("td,etf->fed", moe_in, grad_pre, preferred_element_type=LOW)
    gm = jnp.einsum("etf,edf->td", grad_pre, ups, preferred_element_type=F32)
    scatter = partial(lax.psum_scatter, axis_name=AXES, scatter_dimension=0, tiled=True)
    gup = scatter(grad_up).astype(F32).transpose(1, 2, 0)
    gdown = scatter(grad_down).astype(F32).transpose(1, 0, 2)
    return picked, gm, gup, gdown


def per_device(
    nz, tokens, norm_gain, w_in, conv_w, conv_b, w_x, w_dt, dt_bias, a_log, d_skip, w_out, moe_gain, w_router, w_up,
    w_down, seq_lengths, valid_counts, expert_ids, out_grad,
):
    rows, width = tokens.shape
    sm = Small(w_dt.shape[0], a_log.shape[1], conv_w.shape[0])
    here = w_out.shape[0]
    experts, per = w_up.shape[0], w_up.shape[2]
    small = jnp.concatenate(
        [
            w_x, jnp.zeros((here, LANES - w_x.shape[1]), LOW), w_dt.T, a_log, conv_w.T, conv_b[:, None],
            dt_bias[:, None], d_skip[:, None], jnp.zeros((here, LANES - sm.end), LOW),
        ],
        axis=1,
    )
    router = jnp.concatenate([w_router.T, jnp.zeros((LANES - experts, width), LOW)], axis=0)
    live = jnp.arange(rows, dtype=jnp.int32) < valid_counts[0]
    code = jnp.where(live, expert_ids, expert_ids + experts).astype(LOW)
    gcode = jnp.concatenate([out_grad, jnp.broadcast_to(code[:, None], (rows, LANES))], axis=1)
    lens = seq_lengths[0]
    gain, gain2 = norm_gain[None], moe_gain[None]
    if nz:
        mine = jnp.concatenate([w_up.transpose(0, 2, 1).reshape(experts * per, width), w_down.reshape(experts * per, width)])
        half = [(w, w ^ 4) for w in range(2 * nz)]
        *saved, win_all, small_all, wout_all, gcode_all, other = forward_gather(
            sm, nz, lens, valid_counts, tokens, gain, gain2, w_in.T, small, w_out, gcode, mine, 0
        )
    else:
        win_all = lax.all_gather(w_in.T, AXES, axis=0, tiled=True)
        rest_all = lax.all_gather(jnp.concatenate([w_out, small], axis=1), AXES, axis=0, tiled=True)
        wout_all, small_all = rest_all[:, :width], rest_all[:, width:]
        saved = mixer_forward(sm, lens, valid_counts, tokens, gain, gain2, win_all, small_all, wout_all)
    moe_in = saved[8]
    if nz:
        picked, gm, gch, gmine, gother = expert_call(experts, nz, moe_in, gcode_all, mine, other, router, 1)
        gother = lax.ppermute(gother, "wide", half)
    else:
        picked, gm, gup, gdown = experts_local(moe_in, gcode, w_up, w_down, router, experts)
        gch = jnp.zeros((8, LANES), F32)
    result, gtok, flat, gsmall, gwin, gwout, *home = mixer_backward(
        sm, experts, nz, lens, valid_counts, tokens, gain, small_all, gain2, saved, gm, gch, gcode, router, win_all,
        wout_all, picked, 2,
    )
    if nz:
        (gwout,) = home
        gwin, gsmall, flat = scatter_call(nz, (nz, nz), (gwin, gsmall), (nz,), (flat,), 3)
        flat = jnp.sum(flat.reshape(8 * nz, -1, LANES), axis=0)
        gmine = gmine + gother.astype(F32)
        gup = gmine[: experts * per].reshape(experts, per, width).transpose(0, 2, 1)
        gdown = gmine[experts * per :].reshape(experts, per, width)
    else:
        scatter = partial(lax.psum_scatter, axis_name=AXES, scatter_dimension=0, tiled=True)
        gwin = scatter(gwin).astype(F32)
        gall = scatter(jnp.concatenate([gwout, gsmall], axis=1)).astype(F32)
        gwout, gsmall = gall[:, :width], gall[:, width:]
        flat = lax.psum(flat, AXES)
    flat = flat.reshape(-1)
    ggain, ggain2, flat = flat[:width], flat[width : 2 * width], flat[2 * width :]
    grad_router, flat = flat[: width * experts].reshape(experts, width).T, flat[width * experts :]
    token_rms = jnp.sqrt(flat[:3] / (flat[3] * width))
    g2 = gsmall[:, LANES:]
    return (
        result, gtok, ggain, gwin.T, g2[:, sm.conv : sm.conv + sm.taps].T, g2[:, sm.bias], gsmall[:, : w_x.shape[1]],
        g2[:, : sm.rank].T, g2[:, sm.rate], g2[:, sm.alog : sm.alog + sm.states], g2[:, sm.skip], gwout,
        ggain2, grad_router, gup, gdown, token_rms,
    )


def solution(mesh):
    wide, narrow = mesh.shape["wide"], mesh.shape["narrow"]
    nz = wide // 2 if narrow == 4 and wide == 8 else 0
    both = ("wide", "narrow")
    rows2, cols, one, rep = P(both, None), P(None, both), P(both), P()
    in_specs = (
        rows2, rep, cols, cols, one, rows2, cols, one, rows2, one, rows2, rep, rep, P(None, None, both),
        P(None, both, None), rows2, one, one, rows2,
    )
    out_specs = (
        rows2, rows2, rep, cols, cols, one, rows2, cols, one, rows2, one, rows2, rep, rep, P(None, None, both),
        P(None, both, None), rep,
    )
    return jax.shard_map(partial(per_device, nz), mesh=mesh, in_specs=in_specs, out_specs=out_specs, check_vma=False)
```

```python
from functools import partial

import jax
import jax.numpy as jnp
from jax import lax
from jax.experimental import pallas as pl
from jax.experimental.pallas import tpu as pltpu
from jax.sharding import PartitionSpec as P

EPS = 1e-05
LOW = jnp.bfloat16
F32 = jnp.float32
LANES = 128
CH = 384


def dot_nn(a, b):
    return lax.dot_general(a, b, (((1,), (0,)), ((), ())), preferred_element_type=F32)


def dot_nt(a, b):
    return lax.dot_general(a, b, (((1,), (1,)), ((), ())), preferred_element_type=F32)


def dot_tn(a, b):
    return lax.dot_general(a, b, (((0,), (0,)), ((), ())), preferred_element_type=F32)


def sigmoid(v):
    return 1.0 / (1.0 + jnp.exp(-v))


def softplus(v):
    return jnp.maximum(v, 0.0) + jnp.log1p(jnp.exp(-jnp.abs(v)))


class Small:
    def __init__(self, rank, states, taps):
        self.rank, self.states, self.taps = rank, states, taps
        self.alog = -(-rank // 8) * 8
        self.conv = self.alog + states
        self.bias = self.conv + taps
        self.rate = self.bias + 1
        self.skip = self.bias + 2
        self.end = self.bias + 3


def row_iota(shape):
    return lax.broadcasted_iota(jnp.int32, shape, 0)


def lane_iota(shape):
    return lax.broadcasted_iota(jnp.int32, shape, 1)


def segments(lens_ref, shape):
    first = lens_ref[0]
    second = first + lens_ref[1]
    t = row_iota(shape)
    seg = (t >= first).astype(jnp.int32) + (t >= second).astype(jnp.int32)
    opening = (t == 0) | (t == first) | (t == second)
    return t, seg, opening


def lag_masks(lens_ref, shape, taps):
    first = lens_ref[0]
    second = first + lens_ref[1]
    t = row_iota(shape)
    masks = [None]
    for lag in range(1, taps):
        e = t - lag
        same = ((t >= first) == (e >= first)) & ((t >= second) == (e >= second)) & (e >= 0)
        masks.append(same)
    return masks


def conv_pre(src, prm, sm, masks):
    taps = sm.taps
    total = prm[sm.bias : sm.bias + 1, :] + prm[sm.conv : sm.conv + 1, :] * src
    for lag in range(1, taps):
        moved = jnp.where(masks[lag], pltpu.roll(src, lag, 0), 0.0)
        total = total + prm[sm.conv + lag : sm.conv + lag + 1, :] * moved
    return total


def params_of(small_ref, k):
    blk = small_ref[pl.ds(pl.multiple_of(k * CH, CH), CH), LANES : 2 * LANES]
    return jnp.transpose(blk.astype(F32))


def lanes3(v):
    return jnp.concatenate([v] * (CH // LANES), axis=1)


def fold3(v):
    out = v[:, 0:LANES]
    for i in range(1, CH // LANES):
        out = out + v[:, i * LANES : (i + 1) * LANES]
    return out


def spread(expanded, start, states, out_ref):
    rows = expanded.shape[0]
    for s in range(states):
        col = jnp.broadcast_to(expanded[:, start + s : start + s + 1], (rows, LANES))
        out_ref[pl.ds(s, rows, stride=states), :] = col


def rows_sum8(ref, rows):
    planes = []
    for i in range(CH // LANES):
        out = ref[i, pl.ds(0, rows, stride=8), :]
        for j in range(1, 8):
            out = out + ref[i, pl.ds(j, rows, stride=8), :]
        planes.append(out)
    return jnp.concatenate(planes, axis=1)


def put_planes(ref, at, v):
    for i in range(CH // LANES):
        ref[i, at, :] = v[:, i * LANES : (i + 1) * LANES]


def lane_chunk(k, base=0):
    return pl.ds(pl.multiple_of(base + k * CH, LANES), CH)


def row_chunk(k, base=0):
    return pl.ds(pl.multiple_of(base + k * CH, LANES), CH)


def norm_of(x, gain):
    r = lax.rsqrt(jnp.mean(x * x, axis=-1, keepdims=True) + EPS)
    return x * r * gain


def forward_chunk_conv(k, sm, lens_ref, normed_ref, win_ref, small_ref, src_ref, gate_ref, exp_acc, inner):
    normed = normed_ref[...]
    src = dot_nt(normed, win_ref[row_chunk(k), :])
    src_ref[:, lane_chunk(k)] = src
    gate_ref[:, lane_chunk(k)] = dot_nt(normed, win_ref[row_chunk(k, inner), :])
    prm = params_of(small_ref, k)
    masks = lag_masks(lens_ref, src.shape, sm.taps)
    pre = conv_pre(src, prm, sm, masks)
    conved = pre * sigmoid(pre)
    exp_acc[...] += dot_nn(conved.astype(LOW), small_ref[row_chunk(k), 0:LANES])
    return conved


def scan_forward(rows, dl_ref, dx_ref, a, bb_ref, states, cc_ref=None, yp_ref=None, hist_ref=None, dec_ref=None):
    def block(tb, h):
        t0 = pl.multiple_of(tb * 8, 8)
        d8 = dl_ref[pl.ds(t0, 8), :]
        x8 = dx_ref[pl.ds(t0, 8), :]
        for j in range(8):
            d = jnp.broadcast_to(d8[j : j + 1, :], (states, CH))
            x = jnp.broadcast_to(x8[j : j + 1, :], (states, CH))
            dec = jnp.exp(d * a)
            at = pl.ds(pl.multiple_of(t0 * states, 8 * states) + j * states, states)
            h = h * dec + x * lanes3(bb_ref[at, :])
            if hist_ref is not None:
                hist_ref[at, :] = h
                dec_ref[at, :] = dec
            if yp_ref is not None:
                p = h * lanes3(cc_ref[at, :])
                ps = p[0:8]
                for i in range(1, states // 8):
                    ps = ps + p[8 * i : 8 * i + 8]
                put_planes(yp_ref, pl.ds(pl.multiple_of(t0 * 8, 64) + j * 8, 8), ps)
        return h

    lax.fori_loop(0, rows // 8, block, jnp.zeros((states, CH), F32))


def row_of(ref):
    return ref[...].reshape(1, -1)


class Forward:
    def __init__(self, sm, inner, lens_ref, count_ref, tok_ref, gain_ref, gain2_ref, win_ref, small_ref, wout_ref, outs, scratch):
        self.sm, self.inner = sm, inner
        self.lens, self.count, self.tok, self.gain, self.gain2 = lens_ref, count_ref, tok_ref, gain_ref, gain2_ref
        self.win, self.small, self.wout = win_ref, small_ref, wout_ref
        (self.normed, self.src, self.gate, self.lin, self.ym, self.exp, self.gated, self.middle, self.moe, self.sum) = outs
        self.conved, self.dl, self.dx, self.bb, self.cc, self.yp = scratch
        self.chunks = inner // CH
        self.rows = tok_ref.shape[0]

    def start(self):
        self.normed[...] = norm_of(self.tok[...].astype(F32), row_of(self.gain)).astype(LOW)
        self.exp[...] = jnp.zeros_like(self.exp)

    def project(self, k):
        self.conved[:, lane_chunk(k)] = forward_chunk_conv(
            k, self.sm, self.lens, self.normed, self.win, self.small, self.src, self.gate, self.exp, self.inner
        )

    def spread(self):
        sm = self.sm
        expanded = self.exp[...]
        spread(expanded, sm.rank, sm.states, self.bb)
        spread(expanded, sm.rank + sm.states, sm.states, self.cc)

    def scan(self, k):
        sm = self.sm
        expanded = self.exp[...]
        rate = jnp.where(lane_iota(expanded.shape) < sm.rank, expanded, 0.0).astype(LOW)
        prm = params_of(self.small, k)
        lin = dot_nt(rate, self.small[row_chunk(k), LANES : 2 * LANES]) + prm[sm.rate : sm.rate + 1, :]
        self.lin[:, lane_chunk(k)] = lin
        delta = softplus(lin)
        conved = self.conved[:, lane_chunk(k)]
        _, _, opening = segments(self.lens, lin.shape)
        self.dl[...] = jnp.where(opening, 1e30, delta)
        self.dx[...] = delta * conved
        a = -jnp.exp(prm[sm.alog : sm.alog + sm.states, :])
        scan_forward(self.rows, self.dl, self.dx, a, self.bb, sm.states, self.cc, self.yp)
        ym = rows_sum8(self.yp, self.rows) + prm[sm.skip : sm.skip + 1, :] * conved
        self.ym[:, lane_chunk(k)] = ym
        gate = self.gate[:, lane_chunk(k)]
        self.gated[:, lane_chunk(k)] = (ym * (gate * sigmoid(gate))).astype(LOW)

    def end(self):
        valid = row_iota((self.rows, 1)) < self.count[0]
        branch = jnp.where(valid, dot_nn(self.gated[...], self.wout[...]), 0.0)
        self.sum[...] = jnp.broadcast_to(jnp.sum(branch * branch), self.sum.shape)
        middle = self.tok[...].astype(F32) + branch
        self.middle[...] = middle
        self.moe[...] = norm_of(middle, row_of(self.gain2)).astype(LOW)


def mixer_forward_kernel(sm, inner, lens_ref, count_ref, tok_ref, gain_ref, gain2_ref, win_ref, small_ref, wout_ref, *refs):
    f = Forward(sm, inner, lens_ref, count_ref, tok_ref, gain_ref, gain2_ref, win_ref, small_ref, wout_ref, refs[:10], refs[10:])
    f.start()
    pl.loop(0, f.chunks)(f.project)
    f.spread()
    pl.loop(0, f.chunks)(f.scan)
    f.end()


def silu_grad(v, s):
    return s * (1.0 + v * (1.0 - s))


def norm_back(x, gain, grad):
    r = lax.rsqrt(jnp.mean(x * x, axis=-1, keepdims=True) + EPS)
    n = x * r
    q = grad * gain
    return r * (q - n * jnp.mean(q * n, axis=-1, keepdims=True)), grad * n


def scan_backward(rows, states, a, gs_ref, dx_ref, dt_ref, bb_ref, cc_ref, hist_ref, dec_ref, gcp_ref, gbp_ref, lbp_ref, amp_ref):
    blocks = rows // 8

    def fold8(p):
        out = p[0:8]
        for i in range(1, states // 8):
            out = out + p[8 * i : 8 * i + 8]
        return out

    def block(i, carry):
        back, total = carry
        tb = blocks - 1 - i
        t0 = pl.multiple_of(tb * 8, 8)
        g8 = gs_ref[pl.ds(t0, 8), :]
        x8 = dx_ref[pl.ds(t0, 8), :]
        d8 = dt_ref[pl.ds(t0, 8), :]
        for j in range(7, -1, -1):
            base = pl.multiple_of(t0 * states, 8 * states) + j * states
            at = pl.ds(base + states, states)
            prev = pl.ds(base, states)
            here = pl.ds(base, states)
            g = jnp.broadcast_to(g8[j : j + 1, :], (states, CH))
            x = jnp.broadcast_to(x8[j : j + 1, :], (states, CH))
            d = jnp.broadcast_to(d8[j : j + 1, :], (states, CH))
            adj = g * lanes3(cc_ref[here, :]) + back
            gcp_ref[here, :] += fold3(hist_ref[at, :] * g)
            gbp_ref[here, :] += fold3(adj * x)
            out8 = pl.ds(pl.multiple_of(t0 * 8, 64) + j * 8, 8)
            put_planes(lbp_ref, out8, fold8(adj * lanes3(bb_ref[here, :])))
            back = adj * dec_ref[here, :]
            m = back * hist_ref[prev, :]
            put_planes(amp_ref, out8, fold8(m * a))
            total = total + m * d
        return back, total

    zero = jnp.zeros((states, CH), F32)
    _, total = lax.fori_loop(0, blocks, block, (zero, zero))
    return total * a


def column(row):
    return jnp.transpose(jnp.broadcast_to(row, (LANES, LANES)))[:, 0:1]


def padded_router(ref):
    experts, width = ref.shape
    rows = jnp.concatenate([ref[...].astype(F32), jnp.zeros((LANES - experts, width), F32)], axis=0)
    return rows.astype(LOW)


def route(rows_in, router, expert, experts):
    logits = dot_nt(rows_in, router)
    lane = lane_iota(logits.shape)
    logits = jnp.where(lane < experts, logits, -1e30)
    e = jnp.exp(logits - jnp.max(logits, axis=-1, keepdims=True))
    probs = e / jnp.sum(e, axis=-1, keepdims=True)
    onehot = (lane.astype(F32) == expert).astype(F32)
    return probs, onehot, jnp.sum(probs * onehot, axis=-1, keepdims=True)


def some(work, k, chunks):
    per = -(-len(work) // chunks)
    for i in range(chunks):
        share = work[i * per : (i + 1) * per]
        if share:
            def run(share=share):
                for item in share:
                    item()

            pl.when(k == i)(run)


def mixer_backward_kernel(
    sm, inner, experts, nz,
    lens_ref, count_ref, tok_ref, gain_ref, small_ref, gain2_ref,
    normed_ref, src_ref, gate_ref, lin_ref, ym_ref, exp_ref, gated_ref, middle_ref, moe_ref, sum_ref,
    gm_ref, gch_ref, gout_ref, ids_ref, router_ref, win_ref, wout_ref, picked_ref, mine_ref,
    result_ref, gtok_ref, flat_ref, gsmall_ref, gwin_ref, gwout_ref, *refs,
):
    if nz:
        home_ref, other_ref, refs = refs[0], refs[1], refs[2:]
    (
        gmid_s, gmix_s, ggate_s, gconv_s, gs_s, dl_s, dx_s, dt_s, bb_s, cc_s, hist_s, dec_s, gcp_s, gbp_s, lbp_s, amp_s,
        grate_s, gnorm_s, pick_s, wbuf, outs, wsem, osem,
    ) = refs[:23]
    rows, width = tok_ref.shape
    states = sm.states
    chunks = inner // CH
    pieces = width // LANES

    def wout_in(k):
        return pltpu.make_async_copy(wout_ref.at[row_chunk(k), :], wbuf.at[k], wsem.at[k])

    for k in range(chunks):
        wout_in(k).start()
    todo = []
    if nz:
        place = Place(nz)
        place.barrier(1)
        exchange = Exchange(place, mine_ref.at[pl.ds(0, other_ref.shape[0]), :], other_ref, refs[39])
        for i in range(exchange.parts):
            exchange.start(i)
        s_out = Scatter(place, gwout_ref, *refs[23:31], nz)
        s_pick = Scatter(place, picked_ref, *refs[31:39], 2)
        todo = sorted(
            [(t, 0, step, k) for t, step, k in s_out.steps()] + [(t + 4, 1, step, k) for t, step, k in s_pick.steps()],
            key=lambda e: e[:2],
        )
        todo = [partial(step, k) for _, _, step, k in todo]
    early = todo[: 2 * chunks]
    late = todo[2 * chunks :]

    def put_flat(row, v):
        for i in range(pieces):
            flat_ref[row + i : row + i + 1, :] = v[:, i * LANES : (i + 1) * LANES]

    flat_ref[...] = jnp.zeros_like(flat_ref)
    gout = gout_ref[...].astype(F32)
    valid = row_iota((rows, 1)) < count_ref[0]
    expert = column(ids_ref[...].astype(F32))
    moe_in = moe_ref[...]
    router = padded_router(router_ref)
    probs, onehot, chosen = route(moe_in, router, expert, experts)
    if nz:
        gchosen = column(gch_ref[0:1, :])
    else:
        gchosen = jnp.sum(gout * picked_ref[...], axis=-1, keepdims=True)
    gchosen = jnp.where(valid, gchosen, 0.0)
    glogits = (probs * (onehot - chosen) * gchosen).astype(LOW)
    grouter = dot_tn(glogits, moe_in)
    for e in range(experts):
        put_flat((2 + e) * pieces, grouter[e : e + 1, :])
    gmoe = gm_ref[...] + dot_nn(glogits, router)
    gmid, prod = norm_back(middle_ref[...], row_of(gain2_ref), gmoe)
    put_flat(pieces, jnp.sum(prod, axis=0, keepdims=True))
    gmid = gmid + gout
    gmid_s[...] = gmid
    gmix_s[...] = jnp.where(valid, gmid, 0.0).astype(LOW)

    def out_copy(which, k, base):
        dst = (gwout_ref, gwin_ref)[which]
        return pltpu.make_async_copy(outs.at[which, k % 2], dst.at[row_chunk(k, base), :], osem.at[which, k % 2])

    def put_out(which, k, base, v):
        @pl.when(k >= 2)
        def _():
            out_copy(which, k - 2, base).wait()

        outs[which, k % 2] = v.astype(LOW)
        out_copy(which, k, base).start()

    def end_out(which, base):
        for k in (chunks - 2, chunks - 1):
            out_copy(which, k, base).wait()

    @pl.loop(0, chunks)
    def _(k):
        wout_in(k).wait()
        gmix = gmix_s[...]
        gg = dot_nt(gmix, wbuf[k])
        put_out(0, k, 0, dot_tn(gated_ref[:, lane_chunk(k)], gmix))
        gate = gate_ref[:, lane_chunk(k)]
        s = sigmoid(gate)
        gs_s[:, lane_chunk(k)] = gg * (gate * s)
        ggate = (gg * ym_ref[:, lane_chunk(k)] * silu_grad(gate, s)).astype(LOW)
        ggate_s[:, lane_chunk(k)] = ggate
        put_out(1, k, inner, dot_tn(ggate, normed_ref[...]))

    end_out(0, 0)
    if nz:
        s_out.begin()
        s_pick.begin()
    end_out(1, inner)

    slots = chunks // 2

    def win_in(k, half):
        slot = (k % slots) * 2 + half
        return pltpu.make_async_copy(win_ref.at[row_chunk(k, half * inner), :], wbuf.at[slot], wsem.at[slot])

    for k in range(slots):
        win_in(k, 0).start()
        win_in(k, 1).start()
    expanded = exp_ref[...]
    lane = lane_iota((rows, LANES))
    rate = jnp.where(lane < sm.rank, expanded, 0.0).astype(LOW)
    spread(expanded, sm.rank, states, bb_s)
    spread(expanded, sm.rank + states, states, cc_s)
    grate_s[...] = jnp.zeros_like(grate_s)
    gcp_s[...] = jnp.zeros_like(gcp_s)
    gbp_s[...] = jnp.zeros_like(gbp_s)
    gnorm_s[...] = jnp.zeros_like(gnorm_s)
    hist_s[0:states, :] = jnp.zeros((states, CH), F32)

    @pl.loop(0, chunks)
    def _(k):
        prm = params_of(small_ref, k)
        src = src_ref[:, lane_chunk(k)]
        masks = lag_masks(lens_ref, src.shape, sm.taps)
        pre = conv_pre(src, prm, sm, masks)
        conved = pre * sigmoid(pre)
        lin = lin_ref[:, lane_chunk(k)]
        delta = softplus(lin)
        _, _, opening = segments(lens_ref, lin.shape)
        dl_s[...] = jnp.where(opening, 1e30, delta)
        dt_s[...] = delta
        dx_s[...] = delta * conved
        a = -jnp.exp(prm[sm.alog : sm.alog + states, :])
        gs_ref = gs_s.at[:, lane_chunk(k)]
        scan_forward(rows, dl_s, dx_s, a, bb_s, states, hist_ref=hist_s.at[pl.ds(states, rows * states), :], dec_ref=dec_s)
        galog = scan_backward(rows, states, a, gs_ref, dx_s, dt_s, bb_s, cc_s, hist_s, dec_s, gcp_s, gbp_s, lbp_s, amp_s)
        gs = gs_ref[...]
        lb = rows_sum8(lbp_s, rows)
        gdelta = rows_sum8(amp_s, rows) + conved * lb
        glin = gdelta * sigmoid(lin)
        gconv_s[:, lane_chunk(k)] = prm[sm.skip : sm.skip + 1, :] * gs + delta * lb
        glin_low = glin.astype(LOW)
        grate_s[...] += dot_nn(glin_low, small_ref[row_chunk(k), LANES : 2 * LANES])
        part = dot_tn(glin_low, rate)
        grows = jnp.concatenate(
            [
                jnp.zeros((sm.alog, CH), F32),
                galog,
                jnp.zeros((sm.taps + 1, CH), F32),
                jnp.sum(glin, axis=0, keepdims=True),
                jnp.sum(gs * conved, axis=0, keepdims=True),
                jnp.zeros((LANES - sm.end, CH), F32),
            ],
            axis=0,
        )
        gsmall_ref[row_chunk(k), LANES : 2 * LANES] = (part + jnp.transpose(grows)).astype(LOW)
        some(early, k, chunks)

    gexp = jnp.where(lane < sm.rank, grate_s[...], 0.0)
    for s in range(states):
        gb = jnp.sum(gbp_s[pl.ds(s, rows, stride=states), :], axis=1, keepdims=True)
        gc = jnp.sum(gcp_s[pl.ds(s, rows, stride=states), :], axis=1, keepdims=True)
        gexp = jnp.where(lane == sm.rank + s, gb, gexp)
        gexp = jnp.where(lane == sm.rank + states + s, gc, gexp)
    gexp_low = gexp.astype(LOW)

    @pl.loop(0, chunks)
    def _(k):
        prm = params_of(small_ref, k)
        src = src_ref[:, lane_chunk(k)]
        masks = lag_masks(lens_ref, src.shape, sm.taps)
        pre = conv_pre(src, prm, sm, masks)
        s = sigmoid(pre)
        conved_low = (pre * s).astype(LOW)
        gsmall_ref[row_chunk(k), 0:LANES] = dot_tn(conved_low, gexp_low).astype(LOW)
        gconv = gconv_s[:, lane_chunk(k)] + dot_nt(gexp_low, small_ref[row_chunk(k), 0:LANES])
        p = gconv * silu_grad(pre, s)
        gsrc = prm[sm.conv : sm.conv + 1, :] * p
        taps = [jnp.sum(p * src, axis=0, keepdims=True)]
        for lag in range(1, sm.taps):
            pm = jnp.where(masks[lag], p, 0.0)
            taps.append(jnp.sum(pm * pltpu.roll(src, lag, 0), axis=0, keepdims=True))
            gsrc = gsrc + prm[sm.conv + lag : sm.conv + lag + 1, :] * pltpu.roll(pm, rows - lag, 0)
        grows = jnp.concatenate(
            [jnp.zeros((sm.conv, CH), F32)]
            + taps
            + [jnp.sum(p, axis=0, keepdims=True), jnp.zeros((LANES - sm.bias - 1, CH), F32)],
            axis=0,
        )
        old = gsmall_ref[row_chunk(k), LANES : 2 * LANES].astype(F32)
        gsmall_ref[row_chunk(k), LANES : 2 * LANES] = (old + jnp.transpose(grows)).astype(LOW)
        gsrc_low = gsrc.astype(LOW)
        put_out(1, k, 0, dot_tn(gsrc_low, normed_ref[...]))
        win_in(k, 0).wait()
        win_in(k, 1).wait()
        slot = (k % slots) * 2
        gnorm_s[...] += dot_nn(gsrc_low, wbuf[slot]) + dot_nn(ggate_s[:, lane_chunk(k)], wbuf[slot + 1])

        @pl.when(k + slots < chunks)
        def _():
            win_in(k + slots, 0).start()
            win_in(k + slots, 1).start()

        some(late, k, chunks)

    gtok, prod = norm_back(tok_ref[...].astype(F32), row_of(gain_ref), gnorm_s[...])
    put_flat(0, jnp.sum(prod, axis=0, keepdims=True))
    gtok_ref[...] = gtok + gmid_s[...]
    end_out(1, 0)
    if nz:
        s_pick.result(pick_s)
        picked = pick_s[...]
    else:
        picked = picked_ref[...]
    two = chosen * jnp.where(valid, picked, 0.0)
    result = middle_ref[...] + two
    result_ref[...] = result.astype(LOW)
    squares = jnp.where(valid, result * result, 0.0)
    lane1 = lane_iota((1, LANES))
    stats = jnp.where(lane1 == 0, jnp.sum(squares), 0.0)
    stats = jnp.where(lane1 == 1, sum_ref[0:1, :], stats)
    stats = jnp.where(lane1 == 2, jnp.sum(two * two), stats)
    stats = jnp.where(lane1 == 3, count_ref[0].astype(F32), stats)
    flat_ref[(2 + experts) * pieces : (2 + experts) * pieces + 1, :] = stats
    if nz:
        s_out.result(home_ref)
        s_out.finish()
        s_pick.finish()
        exchange.wait()


VMEM = pltpu.VMEM
SMEM_SPEC = pl.BlockSpec(memory_space=pltpu.SMEM)
VMEM_SPEC = pl.BlockSpec(memory_space=pltpu.VMEM)


def shape_of(shape, dtype):
    return jax.ShapeDtypeStruct(shape, dtype)


def forward_outs(sm, rows, width, inner):
    return (
        shape_of((rows, width), LOW),
        shape_of((rows, inner), F32),
        shape_of((rows, inner), F32),
        shape_of((rows, inner), F32),
        shape_of((rows, inner), F32),
        shape_of((rows, LANES), F32),
        shape_of((rows, inner), LOW),
        shape_of((rows, width), F32),
        shape_of((rows, width), LOW),
        shape_of((8, LANES), F32),
    )


def forward_scratch(sm, rows, inner):
    st = sm.states
    return [
        VMEM((rows, inner), F32),
        VMEM((rows, CH), F32),
        VMEM((rows, CH), F32),
        VMEM((rows * st, LANES), F32),
        VMEM((rows * st, LANES), F32),
        VMEM((CH // LANES, rows * 8, LANES), F32),
    ]


def mixer_forward(sm, lens, count, tokens, gain, gain2, win, small, wout):
    rows, width = tokens.shape
    inner = wout.shape[0]
    return pl.pallas_call(
        partial(mixer_forward_kernel, sm, inner),
        out_shape=forward_outs(sm, rows, width, inner),
        in_specs=[SMEM_SPEC] * 2 + [VMEM_SPEC] * 6,
        out_specs=(VMEM_SPEC,) * 10,
        scratch_shapes=forward_scratch(sm, rows, inner),
        compiler_params=pltpu.CompilerParams(vmem_limit_bytes=60 << 20),
        name="mixer_forward",
    )(lens, count, tokens, gain, gain2, win, small, wout)


def flat_rows(width, experts):
    return -(-((2 + experts) * (width // LANES) + 1) // 8) * 8


MESH = pl.DeviceIdType.MESH


class Place:
    def __init__(self, nz):
        self.nz = nz
        w, n = lax.axis_index("wide"), lax.axis_index("narrow")
        self.z, self.y, self.x, self.c = w // 2, w % 2, n // 2, n % 2

    def flips(self, f2, f3):
        fx = f2 * (1 - self.c) + f3 * self.c
        fy = f3 * (1 - self.c) + f2 * self.c
        return self.x + fx - 2 * self.x * fx, self.y + fy - 2 * self.y * fy

    def device(self, z, f2, f3, fc):
        x, y = self.flips(f2, f3)
        core = 1 - self.c if fc else self.c
        return (z * 2 + y, x * 2 + core)

    def target(self, kind):
        if kind == "sib":
            return self.device(self.z, 0, 0, 1)
        if kind == "d2":
            return self.device(self.z, 1, 0, 0)
        if kind == "d3":
            return self.device(self.z, 0, 1, 0)
        if kind == "far":
            return self.device((self.z + self.nz // 2) % self.nz, 0, 0, 0)
        return self.device(self.z + kind, 0, 0, 0)

    def block(self, zloc, f2, f3, fc):
        x, y = self.flips(f2, f3)
        return zloc * 8 + y * 4 + x * 2 + self.c + fc - 2 * fc * self.c

    def has(self, side, group):
        at = self.z % group + side
        return (at >= 0) & (at < group)

    def barrier(self, far=0):
        sem = pltpu.get_barrier_semaphore()
        for kind in ("sib", "d2", "d3") + (("far",) if far else ()):
            pl.semaphore_signal(sem, inc=1, device_id=self.target(kind), device_id_type=MESH)
        for side in (-1, 1):
            @pl.when(self.has(side, self.nz))
            def _():
                pl.semaphore_signal(sem, inc=1, device_id=self.target(side), device_id_type=MESH)
        below = (self.z + self.nz - 1) // self.nz
        above = (2 * self.nz - 2 - self.z) // self.nz
        pl.semaphore_wait(sem, 3 + far + below + above)


def when(cond, body):
    if cond is True:
        body()
    else:
        pl.when(cond)(body)


class Gather:
    def __init__(self, place, src, out, send, recv, local, group):
        self.place, self.src, self.out, self.send, self.recv, self.local, self.group = place, src, out, send, recv, local, group
        self.rows = src.shape[0]
        self.slots = 0
        self.sent = []

    def at(self, p):
        return self.out.at[pl.ds(pl.multiple_of(p * self.rows, 8), self.rows), :]

    def copy(self, src, p, kind, slot):
        return pltpu.make_async_remote_copy(
            src, self.at(p), self.send.at[slot], self.recv.at[p], device_id=self.place.target(kind), device_id_type=MESH
        )

    def push(self, rel, kinds):
        for kind in kinds:
            slot = self.slots
            self.slots += 1
            self.sent.append((rel, kind, slot))

            def go(kind=kind, slot=slot):
                p, src = self.source(rel)
                self.copy(src, p, kind, slot).start()

            when(self.extra(kind), go)

    def extra(self, kind):
        return True if isinstance(kind, str) else self.place.has(kind, self.group)

    def source(self, rel):
        zloc = self.place.z % self.group
        if rel is None:
            return self.place.block(zloc, 0, 0, 0), self.src
        p = self.place.block(zloc + rel[0], rel[1], rel[2], 0)
        return p, self.at(p)

    def begin(self):
        p, src = self.source(None)
        self.push(None, [-1, 1, "d2", "d3", "sib"])
        pltpu.make_async_copy(src, self.at(p), self.local).start()

    def begin_z(self):
        self.push(None, [-1, 1])

    def handle_z(self, dist):
        def body():
            self.wait_block(self.place.block(self.place.z % self.group + dist, 0, 0, 0))
            self.push((dist, 0, 0), [1 if dist < 0 else -1])

        when(self.place.has(dist, self.group), body)

    def begin_xy(self):
        p, src = self.source(None)
        self.push(None, ["d2", "d3", "sib"])
        pltpu.make_async_copy(src, self.at(p), self.local).start()

    def pass_on(self, dist):
        def body():
            self.push((dist, 0, 0), ["d2", "d3", "sib"])

        when(self.place.has(dist, self.group), body)

    def wait_block(self, p):
        self.copy(self.src, p, "sib", 0).wait_recv()

    def events(self):
        out = []
        for dist in range(-self.group + 1, self.group):
            for f2 in (0, 1):
                for f3 in (0, 1):
                    if dist or f2 or f3:
                        out.append((abs(dist) + f2 + 2 * f3, dist, f2, f3))
        return sorted(out)

    def handle(self, dist, f2, f3):
        zloc = self.place.z % self.group
        cond = True if dist == 0 else self.place.has(dist, self.group)
        kinds = ["sib"]
        if not f3:
            kinds = ["d3"] + kinds
            if not f2:
                kinds = [1 if dist < 0 else -1, "d2"] + kinds

        def body():
            self.wait_block(self.place.block(zloc + dist, f2, f3, 0))
            self.push((dist, f2, f3), kinds)

        when(cond, body)

    def own_wait(self):
        p, src = self.source(None)
        pltpu.make_async_copy(src, self.at(p), self.local).wait()

    def finish(self):
        self.own_wait()
        for f2 in (0, 1):
            for f3 in (0, 1):
                for z in range(self.group):
                    self.wait_block(self.place.block(z, f2, f3, 1))
        self.finish_sends()

    def finish_sends(self):
        for rel, kind, slot in self.sent:
            def end(rel=rel, kind=kind, slot=slot):
                def inner():
                    p, src = self.source(rel)
                    self.copy(src, p, kind, slot).wait_send()

                when(self.extra(kind), inner)

            when(True if rel is None or not rel[0] else self.place.has(rel[0], self.group), end)

    @staticmethod
    def sends(group):
        return 5 + sum(2 + (not f3) + 2 * ((not f3) and (not f2)) for d in range(-group + 1, group) for f2 in (0, 1) for f3 in (0, 1))


def run_gathers(gathers):
    for g in gathers:
        g.begin()
    events = []
    for i, g in enumerate(gathers):
        events += [(e[0], i) + e[1:] for e in g.events()]
    for _, i, dist, f2, f3 in sorted(events):
        gathers[i].handle(dist, f2, f3)
    for g in gathers:
        g.finish()


class Exchange:
    parts = 4

    def __init__(self, place, src, out, sems):
        rows = src.shape[0] // self.parts
        self.copies = [
            pltpu.make_async_remote_copy(
                src.at[pl.ds(i * rows, rows), :], out.at[pl.ds(i * rows, rows), :], sems.at[0, i], sems.at[1, i],
                device_id=place.target("far"), device_id_type=MESH,
            )
            for i in range(self.parts)
        ]

    def start(self, i):
        self.copies[i].start()

    def wait(self):
        for copy in self.copies:
            copy.wait()


class Scatter:
    def __init__(self, place, src, acc, rsib, rd3, rd2, rz, send, recv, local, group):
        self.place, self.src, self.acc = place, src, acc
        self.rows = rsib.shape[1]
        self.rsib, self.rd3, self.rd2, self.rz = rsib, rd3, rd2, rz
        self.send, self.recv, self.local, self.group = send, recv, local, group
        z = place.z % group
        self.zloc = z
        if group == 2:
            self.order = [(1 - z, 1 - 2 * z)]
        else:
            h, low = z // 2, z % 2
            self.order = [(3 * (1 - h), 1 - 2 * h), (2 - h, 1 - 2 * h), (2 * h + 1 - low, 1 - 2 * low)]
        self.dests = [zz for zz, _ in self.order] + [z]

    def copy(self, src, dst, send, recv, target):
        return pltpu.make_async_remote_copy(
            src, dst, self.send.at[send], self.recv.at[recv], device_id=target, device_id_type=MESH
        )

    def part(self, p):
        if len(self.src.shape) == 3:
            return self.src.at[p]
        return self.src.at[pl.ds(pl.multiple_of(p * self.rows, 8), self.rows), :]

    def sum(self, zz, f2, f3):
        if self.acc is None:
            return self.part(self.place.block(zz, f2, f3, 0))
        return self.acc.at[zz * 4 + f2 * 2 + f3]

    def to_sib(self, k, f2, f3):
        at = self.dests[k] * 4 + f3 * 2 + f2
        src = self.part(self.place.block(self.dests[k], f2, f3, 1))
        return self.copy(src, self.rsib.at[at], k * 4 + f2 * 2 + f3, at, self.place.target("sib"))

    def to_d3(self, k, f2):
        zz, group = self.dests[k], self.group
        row = 4 * group + k * 2 + f2
        return self.copy(
            self.sum(zz, f2, 1), self.rd3.at[zz * 2 + f2], row, 4 * group + zz * 2 + f2, self.place.target("d3")
        )

    def to_d2(self, k):
        zz, group = self.dests[k], self.group
        return self.copy(self.sum(zz, 1, 0), self.rd2.at[zz], 6 * group + k, 6 * group + zz, self.place.target("d2"))

    def zrow(self, zz, side):
        return zz + self.group * (1 + side) // 2

    def to_z(self, k):
        zz, side = self.order[k]
        row = self.zrow(zz, side)
        return self.copy(self.sum(zz, 0, 0), self.rz.at[row], 7 * self.group + k, 7 * self.group + row, self.place.target(side))

    def received(self, ref, row):
        pltpu.make_async_remote_copy(
            ref, ref, self.send.at[0], self.recv.at[row], device_id=self.place.target("sib"), device_id_type=MESH
        ).wait_recv()
        return ref

    def from_z(self, zz, side):
        row = self.zrow(zz, side)
        return self.received(self.rz.at[row], 7 * self.group + row)

    def local_copy(self, k, f2, f3):
        return pltpu.make_async_copy(
            self.part(self.place.block(self.dests[k], f2, f3, 0)),
            self.sum(self.dests[k], f2, f3),
            self.local.at[k * 4 + f2 * 2 + f3],
        )

    def begin(self):
        for k in range(self.group):
            for f2, f3 in ((1, 1), (1, 0), (0, 1), (0, 0)):
                self.to_sib(k, f2, f3).start()
            if self.acc is not None:
                for f2, f3 in ((1, 1), (0, 1), (1, 0), (0, 0)):
                    self.local_copy(k, f2, f3).start()

    def add(self, acc, ref):
        @pl.loop(0, ref.shape[-1] // LANES)
        def _(i):
            lanes = pl.ds(pl.multiple_of(i * LANES, LANES), LANES)
            acc[:, lanes] = acc[:, lanes] + ref[:, lanes]

    def own(self, k, f2, f3):
        at = self.dests[k] * 4 + f2 * 2 + f3
        if self.acc is not None:
            self.local_copy(k, f2, f3).wait()
        acc = self.sum(self.dests[k], f2, f3)
        self.add(acc, self.received(self.rsib.at[at], at))
        return acc

    def step_a(self, k):
        for f2 in (1, 0):
            self.own(k, f2, 1)
            self.to_d3(k, f2).start()

    def add_d3(self, k, f2, at):
        row = self.dests[k] * 2 + f2
        self.add(at, self.received(self.rd3.at[row], 4 * self.group + row))

    def step_b(self, k):
        at = self.own(k, 1, 0)
        self.add_d3(k, 1, at)
        self.to_d2(k).start()

    def step_c(self, k):
        at = self.own(k, 0, 0)
        self.add_d3(k, 0, at)
        zz = self.dests[k]
        self.add(at, self.received(self.rd2.at[zz], 6 * self.group + zz))
        if k < self.group - 1:
            side = self.order[k][1]

            @pl.when(self.place.has(-side, self.group))
            def _():
                self.add(at, self.from_z(zz, side))

            self.to_z(k).start()

    def result(self, out):
        out[...] = self.sum(self.zloc, 0, 0)[...].astype(out.dtype)
        for side in (-1, 1):
            @pl.when(self.place.has(side, self.group))
            def _():
                out[...] += self.from_z(self.zloc, -side)[...].astype(out.dtype)

    def steps(self):
        out = []
        for k in range(self.group):
            out += [(3 * k, self.step_a, k), (3 * k + 4, self.step_b, k), (3 * k + 8, self.step_c, k)]
        return sorted(out, key=lambda e: e[0])

    def finish(self):
        for k in range(self.group):
            for f2 in (0, 1):
                for f3 in (0, 1):
                    self.to_sib(k, f2, f3).wait_send()
                self.to_d3(k, f2).wait_send()
            self.to_d2(k).wait_send()
            if k < self.group - 1:
                self.to_z(k).wait_send()

    @staticmethod
    def scratch(group, rows, cols, dtype, in_place=False):
        return [
            VMEM((8, LANES) if in_place else (4 * group, rows, cols), dtype),
            VMEM((4 * group, rows, cols), dtype),
            VMEM((2 * group, rows, cols), dtype),
            VMEM((group, rows, cols), dtype),
            VMEM((2 * group, rows, cols), dtype),
            pltpu.SemaphoreType.DMA((8 * group,)),
            pltpu.SemaphoreType.DMA((9 * group,)),
            pltpu.SemaphoreType.DMA((4 * group,)),
        ]


def run_scatters(scatters, outs, gathers=()):
    for g in gathers:
        g.begin()
    for s in scatters:
        s.begin()
    steps = []
    for i, s in enumerate(scatters):
        steps += [(t, i, step, k) for t, step, k in s.steps()]
    for _, _, step, k in sorted(steps, key=lambda e: e[:2]):
        step(k)
    for g in gathers:
        for _, dist, f2, f3 in g.events():
            g.handle(dist, f2, f3)
    for s, out in zip(scatters, outs):
        s.result(out)
    for s in scatters:
        s.finish()
    for g in gathers:
        g.finish()


ANY_SPEC = pl.BlockSpec(memory_space=pl.ANY)


def gather_scratch(group):
    return [
        pltpu.SemaphoreType.DMA((Gather.sends(group),)),
        pltpu.SemaphoreType.DMA((group * 8,)),
        pltpu.SemaphoreType.DMA,
    ]


def gather_kernel(nz, groups, *refs):
    n = len(groups)
    srcs, outs, scr = refs[:n], refs[n : 2 * n], refs[2 * n :]
    place = Place(nz)
    place.barrier()
    run_gathers(
        [Gather(place, srcs[i], outs[i], *scr[3 * i : 3 * i + 3], groups[i]) for i in range(n)]
    )


def gather_call(nz, groups, arrays, collective_id):
    return pl.pallas_call(
        partial(gather_kernel, nz, groups),
        out_shape=tuple(shape_of((g * 8 * a.shape[0], a.shape[1]), a.dtype) for g, a in zip(groups, arrays)),
        in_specs=[ANY_SPEC] * len(arrays),
        out_specs=(ANY_SPEC,) * len(arrays),
        scratch_shapes=sum([gather_scratch(g) for g in groups], []),
        compiler_params=pltpu.CompilerParams(collective_id=collective_id, has_side_effects=True, vmem_limit_bytes=60 << 20),
        name="gather_blocks",
    )(*arrays)


def scatter_kernel(nz, groups, gathered, *refs):
    n = len(groups)
    g = len(gathered)
    srcs, gsrcs, outs, gouts, scr = refs[:n], refs[n : n + g], refs[n + g : 2 * n + g], refs[2 * n + g : 2 * n + 2 * g], refs[2 * n + 2 * g :]
    place = Place(nz)
    place.barrier()
    scatters = [Scatter(place, srcs[i], *scr[8 * i : 8 * i + 8], groups[i]) for i in range(n)]
    more = scr[8 * n :]
    gathers = [Gather(place, gsrcs[i], gouts[i], *more[3 * i : 3 * i + 3], gathered[i]) for i in range(g)]
    run_scatters(scatters, outs, gathers)


def scatter_call(nz, groups, arrays, gathered, garrays, collective_id):
    return pl.pallas_call(
        partial(scatter_kernel, nz, groups, gathered),
        out_shape=tuple(shape_of((a.shape[0] // (8 * g), a.shape[1]), F32) for g, a in zip(groups, arrays))
        + tuple(shape_of((g * 8 * a.shape[0], a.shape[1]), a.dtype) for g, a in zip(gathered, garrays)),
        in_specs=[ANY_SPEC] * (len(arrays) + len(garrays)),
        out_specs=(VMEM_SPEC,) * len(arrays) + (ANY_SPEC,) * len(garrays),
        scratch_shapes=sum([Scatter.scratch(g, a.shape[0] // (8 * g), a.shape[1], a.dtype) for g, a in zip(groups, arrays)], [])
        + sum([gather_scratch(g) for g in gathered], []),
        compiler_params=pltpu.CompilerParams(collective_id=collective_id, has_side_effects=True, vmem_limit_bytes=60 << 20),
        name="scatter_blocks",
    )(*arrays, *garrays)


FAR_AT = 5.0
FAR_STEP = 0.0


def forward_gather_kernel(sm, inner, nz, lens_ref, count_ref, tok_ref, gain_ref, gain2_ref, *refs):
    (win_src, wout_src, up_ref, wx_ref, wdt_ref, alog_ref, convw_ref, convb_ref, rate_ref, skip_ref) = refs[:10]
    outs, alls, other, refs = refs[10:20], refs[20:23], refs[23], refs[24:]
    win_v, small_v, wout_v, load, small_src, turned = refs[:6]
    fwd_scratch, far, sems = refs[6:12], refs[12], refs[13:]
    here = small_src.shape[0]
    srcs = (win_src, small_src, wout_src)
    place = Place(nz)
    f = Forward(sm, inner, lens_ref, count_ref, tok_ref, gain_ref, gain2_ref, win_v, small_v, wout_v, outs, fwd_scratch)
    place.barrier(1)
    exchange = Exchange(place, up_ref, other, far)
    g_win, g_small, g_wout = (Gather(place, srcs[i], alls[i], *sems[3 * i : 3 * i + 3], nz) for i in range(3))
    win_hbm, small_hbm, wout_hbm = alls
    g_win.begin()
    turned[...] = jnp.zeros_like(turned)
    for at, ref in ((0, wdt_ref), (sm.alog, alog_ref), (sm.conv, convw_ref), (sm.bias, convb_ref), (sm.rate, rate_ref), (sm.skip, skip_ref)):
        turned[at : at + ref.shape[0], 0:here] = ref[...].astype(F32)
    small_src[:, 0:LANES] = jnp.zeros((here, LANES), LOW)
    small_src[:, 0 : wx_ref.shape[1]] = wx_ref[...]
    small_src[:, LANES : 2 * LANES] = jnp.transpose(turned[...])[0:here, :].astype(LOW)
    g_small.begin()
    g_wout.begin_z()
    f.start()
    events = []
    for i, g in enumerate((g_small, g_win)):
        events += [(e[0], i, partial(g.handle, *e[1:])) for e in g.events()]
    span = nz - 1
    for dist in range(1, nz):
        for side in (-1, 1):
            events.append((span + dist / 2, 2, partial(g_wout.handle_z, side * dist)))
    for i in range(Exchange.parts):
        events.append((FAR_AT + FAR_STEP * i, 3, partial(exchange.start, i)))
    events.append((span + 2, 4, g_wout.begin_xy))
    for _, _, event in sorted(events, key=lambda e: e[:2]):
        event()
    g_small.finish()
    small_in = pltpu.make_async_copy(small_hbm, small_v, load.at[0])
    small_in.start()
    g_win.finish()

    def win_in(k, half):
        rows = row_chunk(k, half * inner)
        return pltpu.make_async_copy(win_hbm.at[rows, :], win_v.at[rows, :], load.at[2 + 2 * k + half])

    for k in range(f.chunks):
        win_in(k, 0).start()
        win_in(k, 1).start()
    small_in.wait()
    near = sorted(((abs(d), d) for d in range(1 - nz, nz) if d))
    todo = [partial(g_wout.pass_on, d) for _, d in near]
    todo += [partial(g_wout.handle, *e[1:]) for e in g_wout.events() if e[2] or e[3]]
    split = len(todo) // 2
    first, second = todo[:split], todo[split:]

    @pl.loop(0, f.chunks)
    def _(k):
        win_in(k, 0).wait()
        win_in(k, 1).wait()
        f.project(k)
        some(first, k, f.chunks)

    f.spread()

    @pl.loop(0, f.chunks)
    def _(k):
        f.scan(k)
        some(second, k, f.chunks)

    g_wout.finish()
    wout_in = pltpu.make_async_copy(wout_hbm, wout_v, load.at[1])
    wout_in.start()
    wout_in.wait()
    f.end()
    exchange.wait()


def forward_gather(sm, nz, lens, count, tokens, gain, gain2, win, wout, up, smalls, collective_id):
    rows, width = tokens.shape
    devices = 8 * nz
    inner = wout.shape[0] * devices
    here = wout.shape[0]
    alls = (shape_of((2 * inner, width), LOW), shape_of((inner, 2 * LANES), LOW), shape_of((inner, width), LOW))
    return pl.pallas_call(
        partial(forward_gather_kernel, sm, inner, nz),
        out_shape=forward_outs(sm, rows, width, inner) + alls + (shape_of(up.shape, up.dtype),),
        in_specs=[SMEM_SPEC] * 2 + [VMEM_SPEC] * 3 + [ANY_SPEC] * 3 + [VMEM_SPEC] * 7,
        out_specs=(VMEM_SPEC,) * 10 + (ANY_SPEC,) * 4,
        scratch_shapes=[VMEM(a.shape, a.dtype) for a in alls[:3]]
        + [pltpu.SemaphoreType.DMA((2 + 2 * (inner // CH),)), VMEM((here, 2 * LANES), LOW), VMEM((LANES, LANES), F32)]
        + forward_scratch(sm, rows, inner)
        + [pltpu.SemaphoreType.DMA((2, Exchange.parts))]
        + sum([gather_scratch(g) for g in (nz, nz, nz)], []),
        compiler_params=pltpu.CompilerParams(collective_id=collective_id, has_side_effects=True, vmem_limit_bytes=62 << 20),
        name="forward_gather",
    )(lens, count, tokens, gain, gain2, win, wout, up, *smalls)


GELU_A = 0.7978845608028654
GELU_B = 0.044715


def gelu_parts(v):
    inside = GELU_A * (v + GELU_B * v * v * v)
    t = jnp.tanh(inside)
    slope = 0.5 * (1.0 + t) + 0.5 * v * (1.0 - t * t) * (GELU_A * (1.0 + 3.0 * GELU_B * v * v))
    return 0.5 * v * (1.0 + t), slope


def expert_kernel(
    experts, nz, count_ref, moe_ref, gout_ref, ids_ref, up_ref, other_ref, down_ref, router_ref,
    picked_ref, gm_ref, gch_ref, gmine_ref, gother_ref,
    all_s, gall_s, call_s, code_s, wu_s, wd_s, gm_s, gch_s, go_s, gpre_s, hid_s, slope_s, hidden_s, far, *refs,
):
    sems, gsems, csems, refs = refs[:3], refs[3:6], refs[6:9], refs[9:]
    group = 2
    rows, width = moe_ref.shape
    block = 2 * rows
    units = up_ref.shape[0]
    per = units // experts
    place = Place(nz)
    place.barrier(1)
    gather = Gather(place, moe_ref, all_s, *sems, group)
    gouts = Gather(place, gout_ref, gall_s, *gsems, group)
    codes = Gather(place, code_s, call_s, *csems, group)
    exchange = Exchange(place, down_ref, wd_s.at[pl.ds(units, units), :], far)
    grads = Scatter(place, gm_s, None, *refs[1:8], group)
    chosens = Scatter(place, gch_s, None, *refs[9:16], group)
    ids = ids_ref[...]
    code = jnp.where(lane_iota(ids.shape) < count_ref[0], ids, ids + experts).astype(F32)
    code_s[...] = jnp.broadcast_to(code, code_s.shape)
    codes.begin()
    gather.begin()
    for part in range(exchange.parts):
        exchange.start(part)
    wu_s[0:units, :] = up_ref[...]
    wu_s[units : 2 * units, :] = other_ref[...]
    wd_s[0:units, :] = down_ref[...]
    router = padded_router(router_ref)
    chips = [(fy, fx, far) for fy in (0, 1) for fx in (0, 1) for far in (0, 1)]
    own = {1: [(0, 0)], 2: [(1, 0), (0, 1)], 3: [(1, 0), (0, 1)], 6: [(1, 1)], 7: [(1, 1)]}
    zloc = place.z % group
    zfar = 1 - zloc

    def turn(fx, fy):
        return fx * (1 - place.c) + fy * place.c, fy * (1 - place.c) + fx * place.c

    def arrive(gathers, i):
        for j, (fy, fx, far) in enumerate(chips):
            @pl.when(i == j)
            def _():
                for g in gathers:
                    if j == 0:
                        g.own_wait()
                    for f2, f3 in own.get(j, []):
                        for dist in (-1, 1) if far else (0,):
                            g.handle(dist, f2, f3)
                for g in gathers:
                    g.wait_block(place.block(zfar if far else zloc, *turn(fx, fy), 1))

    def chip_of(i):
        far, fx, fy = i % 2, (i // 2) % 2, i // 4
        return place.block(zloc + far - 2 * far * zloc, *turn(fx, fy), place.c) // 2

    def masks(chip):
        parts = [column(call_s[pl.ds(pl.multiple_of(chip * 16 + 8 * c, 8), 8), :][0:1, :]) for c in range(2)]
        code = jnp.concatenate(parts, axis=0)
        expert = jnp.where(code < experts, code, code - experts)
        col = lane_iota((block, 2 * units))
        col = jnp.where(col >= units, col - units, col).astype(F32)
        return code, expert, (col >= expert * per) & (col < (expert + 1.0) * per)

    @pl.loop(0, len(chips))
    def _(i):
        arrive((codes, gather), i)

        @pl.when(i == LATE)
        def _():
            gouts.begin()

        chip = chip_of(i)
        at = pl.ds(pl.multiple_of(chip * block, block), block)
        _, _, mask = masks(chip)
        act, slope = gelu_parts(dot_nt(all_s[at, :], wu_s[...]))
        hidden = jnp.where(mask, act, 0.0).astype(LOW)
        hidden_s[at, :] = hidden
        slope_s[at, :] = jnp.where(mask, slope, 0.0)
        lanes = pl.ds(pl.multiple_of(chip * block, block), block)
        hid_s[:, lanes] = jnp.transpose(hidden)

    exchange.wait()

    @pl.loop(0, len(chips))
    def _(i):
        arrive((gouts,), i)
        chip = chip_of(i)
        at = pl.ds(pl.multiple_of(chip * block, block), block)
        code, expert, _ = masks(chip)
        hidden = hidden_s[at, :]
        picked_ref[at, :] = dot_nn(hidden, wd_s[...]).astype(LOW)
        _, _, chosen = route(all_s[at, :], router, expert, experts)
        scale = jnp.where(code < experts, chosen, 0.0)
        g = gall_s[at, :]
        back = dot_nt(g, wd_s[...])
        gch = jnp.sum(hidden.astype(F32) * back, axis=1, keepdims=True)
        gpre = (scale * back * slope_s[at, :]).astype(LOW)
        gm = dot_nn(gpre, wu_s[...]).astype(LOW)
        for c in range(2):
            gm_s[2 * chip + c] = gm[c * rows : (c + 1) * rows, :]
            turned = jnp.transpose(jnp.broadcast_to(gch[c * rows : (c + 1) * rows, :], (rows, LANES)))
            gch_s[2 * chip + c] = turned[0:8, :]
        go_s[at, :] = (scale * g.astype(F32)).astype(LOW)
        lanes = pl.ds(pl.multiple_of(chip * block, block), block)
        gpre_s[:, lanes] = jnp.transpose(gpre)
        for j, (fy, fx, far) in enumerate(chips):
            @pl.when(i == j)
            def _():
                grads.to_sib(1 - far, *turn(fx, fy)).start()
                chosens.to_sib(1 - far, *turn(fx, fy)).start()

    def weights(j):
        half = 3
        left, right, base = (gpre_s, all_s, 0) if j < half else (hid_s, go_s, units)
        step = width // half
        at = slice((j % half) * step, (j % half + 1) * step)
        part = dot_nn(left[...], right[:, at])
        gmine_ref[base : base + units, at] = part[0:units, :]
        gother_ref[base : base + units, at] = part[units : 2 * units, :].astype(LOW)

    for k in (0, 1):
        grads.step_a(k)
    for k in (0, 1):
        chosens.step_a(k)
    for j in (0, 1, 2):
        weights(j)
    grads.step_b(0)
    chosens.step_b(0)
    weights(3)
    grads.step_c(0)
    chosens.step_c(0)
    weights(4)
    grads.step_b(1)
    chosens.step_b(1)
    weights(5)
    grads.step_c(1)
    chosens.step_c(1)
    grads.result(gm_ref)
    chosens.result(gch_ref)
    grads.finish()
    chosens.finish()
    for g in (gather, gouts, codes):
        g.finish_sends()


LATE = 0


def expert_call(experts, nz, count, moe_in, gout, ids, up, other, down, router, collective_id):
    rows, width = moe_in.shape
    tokens = rows * 16
    units = 2 * up.shape[0]
    return pl.pallas_call(
        partial(expert_kernel, experts, nz),
        out_shape=(
            shape_of((tokens, width), LOW),
            shape_of((rows, width), F32),
            shape_of((8, LANES), F32),
            shape_of((units, width), F32),
            shape_of((units, width), LOW),
        ),
        in_specs=[SMEM_SPEC] + [ANY_SPEC] * 2 + [VMEM_SPEC] * 5,
        out_specs=(VMEM_SPEC,) * 5,
        scratch_shapes=[
            VMEM((tokens, width), LOW),
            VMEM((tokens, width), LOW),
            VMEM((16 * 8, LANES), F32),
            VMEM((8, LANES), F32),
            VMEM((units, width), LOW),
            VMEM((units, width), LOW),
            VMEM((16, rows, width), LOW),
            VMEM((16, 8, LANES), F32),
            VMEM((tokens, width), LOW),
            VMEM((units, tokens), LOW),
            VMEM((units, tokens), LOW),
            VMEM((tokens, units), F32),
            VMEM((tokens, units), LOW),
            pltpu.SemaphoreType.DMA((2, Exchange.parts)),
        ]
        + gather_scratch(2) * 3
        + Scatter.scratch(2, rows, width, LOW, True)
        + Scatter.scratch(2, 8, LANES, F32, True),
        compiler_params=pltpu.CompilerParams(collective_id=collective_id, has_side_effects=True, vmem_limit_bytes=63 << 20),
        name="experts",
    )(count, moe_in, gout, ids, up, other, down, router)


def mixer_backward(sm, experts, nz, lens, count, tokens, gain, small, gain2, saved, gm, gch, gout, ids, router, win, wout, picked, mine, collective_id):
    rows, width = tokens.shape
    inner = wout.shape[0]
    st = sm.states
    chunks = inner // CH
    here = inner // (8 * nz) if nz else 0
    return pl.pallas_call(
        partial(mixer_backward_kernel, sm, inner, experts, nz),
        out_shape=(
            shape_of((rows, width), LOW),
            shape_of((rows, width), F32),
            shape_of((flat_rows(width, experts), LANES), F32),
            shape_of((inner, 2 * LANES), LOW),
            shape_of((2 * inner, width), LOW),
            shape_of((inner, width), LOW),
        )
        + ((shape_of((here, width), F32), shape_of((mine.shape[0] // 2, width), mine.dtype)) if nz else ()),
        in_specs=[SMEM_SPEC] * 2 + [VMEM_SPEC] * 19 + [ANY_SPEC] * 2 + [ANY_SPEC if nz else VMEM_SPEC, ANY_SPEC],
        out_specs=(VMEM_SPEC,) * 4 + (ANY_SPEC,) * 2 + ((VMEM_SPEC, ANY_SPEC) if nz else ()),
        scratch_shapes=[
            VMEM((rows, width), F32),
            VMEM((rows, width), LOW),
            VMEM((rows, inner), LOW),
            VMEM((rows, inner), F32),
            VMEM((rows, inner), F32),
            VMEM((rows, CH), F32),
            VMEM((rows, CH), F32),
            VMEM((rows, CH), F32),
            VMEM((rows * st, LANES), F32),
            VMEM((rows * st, LANES), F32),
            VMEM(((rows + 1) * st, CH), F32),
            VMEM((rows * st, CH), F32),
            VMEM((rows * st, LANES), F32),
            VMEM((rows * st, LANES), F32),
            VMEM((CH // LANES, rows * 8, LANES), F32),
            VMEM((CH // LANES, rows * 8, LANES), F32),
            VMEM((rows, LANES), F32),
            VMEM((rows, width), F32),
            VMEM((rows, width), F32),
            VMEM((chunks, CH, width), LOW),
            VMEM((2, 2, CH, width), LOW),
            pltpu.SemaphoreType.DMA((chunks,)),
            pltpu.SemaphoreType.DMA((2, 2)),
        ]
        + (Scatter.scratch(nz, here, width, LOW) + Scatter.scratch(2, rows, width, LOW) + [pltpu.SemaphoreType.DMA((2, Exchange.parts))] if nz else []),
        compiler_params=pltpu.CompilerParams(
            collective_id=collective_id if nz else None, has_side_effects=bool(nz), vmem_limit_bytes=63 << 20
        ),
        name="mixer_backward",
    )(lens, count, tokens, gain, small, gain2, *saved, gm, gch, gout, ids, router, win, wout, picked, mine)


def last_kernel(nz, gwin_src, gsmall_src, flat_src, mine_ref, gwin_ref, gsmall_ref, total_ref, other_ref, flat_s, far, *refs):
    place = Place(nz)
    place.barrier(1)
    half = other_ref.shape[0]
    exchange = Exchange(place, mine_ref.at[pl.ds(half, half), :], other_ref, far)
    s_small = Scatter(place, gsmall_src, *refs[0:8], nz)
    s_win = Scatter(place, gwin_src, *refs[8:16], nz)
    g_flat = Gather(place, flat_src, flat_s, *refs[16:19], nz)
    s_small.begin()
    s_win.begin()
    g_flat.begin()
    for i in range(exchange.parts):
        exchange.start(i)
    steps = []
    for i, s in enumerate((s_small, s_win)):
        steps += [(t, i, step, k) for t, step, k in s.steps()]
    for i, (_, dist, f2, f3) in enumerate(g_flat.events()):
        steps.append((4 + i / 4, 2, lambda e: g_flat.handle(*e), (dist, f2, f3)))
    for _, _, step, k in sorted(steps, key=lambda e: e[:2]):
        step(k)
    g_flat.finish()
    count = flat_src.shape[0]
    total = flat_s[0:count, :]
    for i in range(1, 8 * nz):
        total = total + flat_s[i * count : (i + 1) * count, :]
    total_ref[...] = total
    s_small.result(gsmall_ref)
    s_win.result(gwin_ref)
    s_small.finish()
    s_win.finish()
    exchange.wait()


def last_call(nz, gwin, gsmall, flat, mine, collective_id):
    width = gwin.shape[1]
    devices = 8 * nz
    here = gsmall.shape[0] // devices
    rows = gwin.shape[0] // devices
    return pl.pallas_call(
        partial(last_kernel, nz),
        out_shape=(shape_of((rows, width), F32), shape_of((here, 2 * LANES), F32), shape_of(flat.shape, F32), shape_of((mine.shape[0] // 2, width), mine.dtype)),
        in_specs=[ANY_SPEC] * 4,
        out_specs=(VMEM_SPEC,) * 3 + (ANY_SPEC,),
        scratch_shapes=[VMEM((devices * flat.shape[0], LANES), F32), pltpu.SemaphoreType.DMA((2, Exchange.parts))]
        + Scatter.scratch(nz, here, 2 * LANES, LOW)
        + Scatter.scratch(nz, rows, width, LOW)
        + gather_scratch(nz),
        compiler_params=pltpu.CompilerParams(collective_id=collective_id, has_side_effects=True, vmem_limit_bytes=60 << 20),
        name="gradient_sums",
    )(gwin, gsmall, flat, mine)


def finish_kernel(
    sm, win_ref, small_ref, total_ref, mine_ref, oup_ref, odown_ref, res_ref, tok_ref, out_ref,
    gwin_ref, gwx_ref, gwdt_ref, galog_ref, gconvw_ref, gconvb_ref, grate_ref, gskip_ref, ggain_ref, ggain2_ref, grouter_ref, rms_ref,
    gup_ref, gdown_ref, result_ref, gtok_ref, gwout_ref,
):
    units = gup_ref.shape[0]
    here, width = out_ref.shape
    gup_ref[...] = mine_ref[0:units, :] + oup_ref[...].astype(F32)
    gdown_ref[...] = mine_ref[units : 2 * units, :] + odown_ref[...].astype(F32)
    result_ref[...] = res_ref[...]
    gtok_ref[...] = tok_ref[...]
    gwout_ref[...] = out_ref[...]
    gwin_ref[...] = win_ref[...]
    gwx_ref[...] = small_ref[:, 0 : gwx_ref.shape[1]]
    total = total_ref[...]
    pieces = width // LANES
    experts = grouter_ref.shape[0]
    row = lambda v, start: jnp.concatenate([v[start + i : start + i + 1, :] for i in range(pieces)], axis=1)
    ggain_ref[...] = row(total, 0).reshape(-1)
    ggain2_ref[...] = row(total, pieces).reshape(-1)
    for e in range(experts):
        grouter_ref[e : e + 1, :] = row(total, (2 + e) * pieces)
    at = (2 + experts) * pieces
    stats = total[at : at + 1, :]
    rms = jnp.sqrt(stats / (stats[:, 3:4] * width))
    lane = lane_iota(rms.shape)
    for i in range(3):
        rms_ref[i] = jnp.sum(jnp.where(lane == i, rms, 0.0))
    block = jnp.concatenate([small_ref[:, LANES : 2 * LANES], jnp.zeros((LANES - here, LANES), F32)], axis=0)
    turned = jnp.transpose(block)
    for at, ref in ((0, gwdt_ref), (sm.alog, galog_ref), (sm.conv, gconvw_ref), (sm.bias, gconvb_ref), (sm.rate, grate_ref), (sm.skip, gskip_ref)):
        ref[...] = turned[at : at + ref.shape[0], 0:here]


def finish_call(sm, experts, wx_cols, win, small, total, mine, oup, odown, result, gtok, gwout):
    here, width = gwout.shape
    half = mine.shape[0] // 2
    f = lambda *s: shape_of(s, F32)
    return pl.pallas_call(
        partial(finish_kernel, sm),
        out_shape=(
            f(*win.shape), f(here, wx_cols), f(sm.rank, here), f(sm.states, here), f(sm.taps, here), f(1, here), f(1, here),
            f(1, here), f(width), f(width), f(experts, width), f(3), f(half, width), f(half, width),
            shape_of(result.shape, result.dtype), f(*gtok.shape), f(*gwout.shape),
        ),
        in_specs=[VMEM_SPEC] * 9,
        out_specs=(VMEM_SPEC,) * 11 + (SMEM_SPEC,) + (VMEM_SPEC,) * 5,
        compiler_params=pltpu.CompilerParams(vmem_limit_bytes=60 << 20),
        name="finish",
    )(win, small, total, mine, oup, odown, result, gtok, gwout)


AXES = ("wide", "narrow")


def experts_local(moe_in, gout, ids, count, w_up, w_down, w_router, experts):
    rows = moe_in.shape[0]
    ups = lax.all_gather(w_up, AXES, axis=2, tiled=True)
    downs = lax.all_gather(w_down, AXES, axis=1, tiled=True)
    probs = jax.nn.softmax(jnp.dot(moe_in, w_router, preferred_element_type=F32), axis=-1)
    onehot = (ids[:, None] == jnp.arange(experts, dtype=jnp.int32)[None, :]).astype(F32)
    chosen = jnp.sum(probs * onehot, axis=-1, keepdims=True)
    live = jnp.arange(rows, dtype=jnp.int32)[:, None] < count[0]
    pre = jnp.einsum("td,edf->etf", moe_in, ups, preferred_element_type=F32)
    act, slope = gelu_parts(pre)
    hidden = act.astype(LOW)
    outs = jnp.einsum("etf,efd->etd", hidden, downs, preferred_element_type=F32)
    picked = jnp.sum(onehot.T[:, :, None] * outs, axis=0)
    scaled = (jnp.where(live, chosen, 0.0) * gout.astype(F32)).astype(LOW)
    grad_expert = onehot.T.astype(LOW)[:, :, None] * scaled[None]
    grad_down = jnp.einsum("etf,etd->fed", hidden, grad_expert, preferred_element_type=LOW)
    grad_act = jnp.einsum("etd,efd->etf", grad_expert, downs, preferred_element_type=F32)
    grad_pre = (grad_act * slope).astype(LOW)
    grad_up = jnp.einsum("td,etf->fed", moe_in, grad_pre, preferred_element_type=LOW)
    gm = jnp.einsum("etf,edf->td", grad_pre, ups, preferred_element_type=F32)
    scatter = partial(lax.psum_scatter, axis_name=AXES, scatter_dimension=0, tiled=True)
    gup = scatter(grad_up).astype(F32).transpose(1, 2, 0)
    gdown = scatter(grad_down).astype(F32).transpose(1, 0, 2)
    return picked, gm, gup, gdown


def per_device(
    nz, tokens, norm_gain, w_in, conv_w, conv_b, w_x, w_dt, dt_bias, a_log, d_skip, w_out, moe_gain, w_router, w_up,
    w_down, seq_lengths, valid_counts, expert_ids, out_grad,
):
    rows, width = tokens.shape
    sm = Small(w_dt.shape[0], a_log.shape[1], conv_w.shape[0])
    here = w_out.shape[0]
    experts, per = w_up.shape[0], w_up.shape[2]
    lens = seq_lengths[0]
    ids = expert_ids[None]
    router = w_router.T
    if nz:
        up = w_up.transpose(0, 2, 1).reshape(experts * per, width)
        down = w_down.reshape(experts * per, width)
        smalls = (w_x, w_dt, a_log.T, conv_w, conv_b[None], dt_bias[None], d_skip[None])
        *saved, win_all, small_all, wout_all, other = forward_gather(
            sm, nz, lens, valid_counts, tokens, norm_gain, moe_gain, w_in.T, w_out, up, smalls, 0
        )
        picked, gm, gch, gmine, gother = expert_call(
            experts, nz, valid_counts, saved[8], out_grad, ids, up, other, down, router, 1
        )
    else:
        small = jnp.concatenate(
            [
                w_x, jnp.zeros((here, LANES - w_x.shape[1]), LOW), w_dt.T, a_log, conv_w.T, conv_b[:, None],
                dt_bias[:, None], d_skip[:, None], jnp.zeros((here, LANES - sm.end), LOW),
            ],
            axis=1,
        )
        win_all = lax.all_gather(w_in.T, AXES, axis=0, tiled=True)
        rest_all = lax.all_gather(jnp.concatenate([w_out, small], axis=1), AXES, axis=0, tiled=True)
        wout_all, small_all = rest_all[:, :width], rest_all[:, width:]
        saved = mixer_forward(sm, lens, valid_counts, tokens, norm_gain, moe_gain, win_all, small_all, wout_all)
        picked, gm, gup, gdown = experts_local(saved[8], out_grad, expert_ids, valid_counts, w_up, w_down, w_router, experts)
        gch = jnp.zeros((8, LANES), F32)
        gother = gch
    result, gtok, flat, gsmall, gwin, gwout, *home = mixer_backward(
        sm, experts, nz, lens, valid_counts, tokens, norm_gain, small_all, moe_gain, saved, gm, gch, out_grad, ids, router,
        win_all, wout_all, picked, gother, 2,
    )
    if nz:
        gwin, gsmall, flat, odown = last_call(nz, gwin, gsmall, flat, gother, 3)
        (
            gwin, gwx, gwdt, galog, gconvw, gconvb, grate, gskip, ggain, ggain2, grouter, rms, gup, gdown, result, gtok, gwout,
        ) = finish_call(sm, experts, w_x.shape[1], gwin, gsmall, flat, gmine, home[1], odown, result, gtok, home[0])
        return (
            result, gtok, ggain, gwin.T, gconvw, gconvb[0], gwx, gwdt, grate[0], galog.T, gskip[0], gwout, ggain2,
            grouter.T, gup.reshape(experts, per, width).transpose(0, 2, 1), gdown.reshape(experts, per, width), rms,
        )
    scatter = partial(lax.psum_scatter, axis_name=AXES, scatter_dimension=0, tiled=True)
    gwin = scatter(gwin).astype(F32)
    gall = scatter(jnp.concatenate([gwout, gsmall], axis=1)).astype(F32)
    g1, g2 = gall[:, width : width + LANES], gall[:, width + LANES :]
    flat = lax.psum(flat, AXES).reshape(-1)
    ggain, ggain2, flat = flat[:width], flat[width : 2 * width], flat[2 * width :]
    grad_router, flat = flat[: width * experts].reshape(experts, width).T, flat[width * experts :]
    return (
        result, gtok, ggain, gwin.T, g2[:, sm.conv : sm.conv + sm.taps].T, g2[:, sm.bias], g1[:, : w_x.shape[1]],
        g2[:, : sm.rank].T, g2[:, sm.rate], g2[:, sm.alog : sm.alog + sm.states], g2[:, sm.skip], gall[:, :width],
        ggain2, grad_router, gup, gdown, jnp.sqrt(flat[:3] / (flat[3] * width)),
    )


def solution(mesh):
    wide, narrow = mesh.shape["wide"], mesh.shape["narrow"]
    nz = wide // 2 if narrow == 4 and wide == 8 else 0
    both = ("wide", "narrow")
    rows2, cols, one, rep = P(both, None), P(None, both), P(both), P()
    in_specs = (
        rows2, rep, cols, cols, one, rows2, cols, one, rows2, one, rows2, rep, rep, P(None, None, both),
        P(None, both, None), rows2, one, one, rows2,
    )
    out_specs = (
        rows2, rows2, rep, cols, cols, one, rows2, cols, one, rows2, one, rows2, rep, rep, P(None, None, both),
        P(None, both, None), rep,
    )
    return jax.shard_map(partial(per_device, nz), mesh=mesh, in_specs=in_specs, out_specs=out_specs, check_vma=False)
```

```python
from functools import partial

import jax
import jax.numpy as jnp
from jax import lax
from jax.experimental import pallas as pl
from jax.experimental.pallas import tpu as pltpu
from jax.sharding import PartitionSpec as P

EPS = 1e-05
LOW = jnp.bfloat16
F32 = jnp.float32
LANES = 128
CH = 384


def dot_nn(a, b):
    return lax.dot_general(a, b, (((1,), (0,)), ((), ())), preferred_element_type=F32)


def dot_nt(a, b):
    return lax.dot_general(a, b, (((1,), (1,)), ((), ())), preferred_element_type=F32)


def dot_tn(a, b):
    return lax.dot_general(a, b, (((0,), (0,)), ((), ())), preferred_element_type=F32)


def sigmoid(v):
    return 1.0 / (1.0 + jnp.exp(-v))


def softplus(v):
    return jnp.maximum(v, 0.0) + jnp.log1p(jnp.exp(-jnp.abs(v)))


class Small:
    def __init__(self, rank, states, taps):
        self.rank, self.states, self.taps = rank, states, taps
        self.alog = -(-rank // 8) * 8
        self.conv = self.alog + states
        self.bias = self.conv + taps
        self.rate = self.bias + 1
        self.skip = self.bias + 2
        self.end = self.bias + 3


def row_iota(shape):
    return lax.broadcasted_iota(jnp.int32, shape, 0)


def lane_iota(shape):
    return lax.broadcasted_iota(jnp.int32, shape, 1)


def segments(lens_ref, shape):
    first = lens_ref[0]
    second = first + lens_ref[1]
    t = row_iota(shape)
    seg = (t >= first).astype(jnp.int32) + (t >= second).astype(jnp.int32)
    opening = (t == 0) | (t == first) | (t == second)
    return t, seg, opening


def lag_masks(lens_ref, shape, taps):
    first = lens_ref[0]
    second = first + lens_ref[1]
    t = row_iota(shape)
    masks = [None]
    for lag in range(1, taps):
        e = t - lag
        same = ((t >= first) == (e >= first)) & ((t >= second) == (e >= second)) & (e >= 0)
        masks.append(same)
    return masks


def conv_pre(src, prm, sm, masks):
    taps = sm.taps
    total = prm[sm.bias : sm.bias + 1, :] + prm[sm.conv : sm.conv + 1, :] * src
    for lag in range(1, taps):
        moved = jnp.where(masks[lag], pltpu.roll(src, lag, 0), 0.0)
        total = total + prm[sm.conv + lag : sm.conv + lag + 1, :] * moved
    return total


def params_of(small_ref, k):
    blk = small_ref[pl.ds(pl.multiple_of(k * CH, CH), CH), LANES : 2 * LANES]
    return jnp.transpose(blk.astype(F32))


def lanes3(v):
    return jnp.concatenate([v] * (CH // LANES), axis=1)


def fold3(v):
    out = v[:, 0:LANES]
    for i in range(1, CH // LANES):
        out = out + v[:, i * LANES : (i + 1) * LANES]
    return out


def spread(expanded, start, states, out_ref):
    rows = expanded.shape[0]
    for s in range(states):
        col = jnp.broadcast_to(expanded[:, start + s : start + s + 1], (rows, LANES))
        out_ref[pl.ds(s, rows, stride=states), :] = col


def rows_sum8(ref, rows):
    planes = []
    for i in range(CH // LANES):
        out = ref[i, pl.ds(0, rows, stride=8), :]
        for j in range(1, 8):
            out = out + ref[i, pl.ds(j, rows, stride=8), :]
        planes.append(out)
    return jnp.concatenate(planes, axis=1)


def put_planes(ref, at, v):
    for i in range(CH // LANES):
        ref[i, at, :] = v[:, i * LANES : (i + 1) * LANES]


def lane_chunk(k, base=0):
    return pl.ds(pl.multiple_of(base + k * CH, LANES), CH)


def row_chunk(k, base=0):
    return pl.ds(pl.multiple_of(base + k * CH, LANES), CH)


def norm_of(x, gain):
    r = lax.rsqrt(jnp.mean(x * x, axis=-1, keepdims=True) + EPS)
    return x * r * gain


def forward_chunk_conv(k, sm, lens_ref, normed_ref, win_ref, small_ref, src_ref, gate_ref, exp_acc, inner):
    normed = normed_ref[...]
    src = dot_nt(normed, win_ref[row_chunk(k), :])
    src_ref[:, lane_chunk(k)] = src
    gate_ref[:, lane_chunk(k)] = dot_nt(normed, win_ref[row_chunk(k, inner), :])
    prm = params_of(small_ref, k)
    masks = lag_masks(lens_ref, src.shape, sm.taps)
    pre = conv_pre(src, prm, sm, masks)
    conved = pre * sigmoid(pre)
    exp_acc[...] += dot_nn(conved.astype(LOW), small_ref[row_chunk(k), 0:LANES])
    return conved


def scan_forward(rows, dl_ref, dx_ref, a, bb_ref, states, cc_ref=None, yp_ref=None, hist_ref=None, dec_ref=None):
    def block(tb, h):
        t0 = pl.multiple_of(tb * 8, 8)
        d8 = dl_ref[pl.ds(t0, 8), :]
        x8 = dx_ref[pl.ds(t0, 8), :]
        for j in range(8):
            d = jnp.broadcast_to(d8[j : j + 1, :], (states, CH))
            x = jnp.broadcast_to(x8[j : j + 1, :], (states, CH))
            dec = jnp.exp(d * a)
            at = pl.ds(pl.multiple_of(t0 * states, 8 * states) + j * states, states)
            h = h * dec + x * lanes3(bb_ref[at, :])
            if hist_ref is not None:
                hist_ref[at, :] = h
                dec_ref[at, :] = dec
            if yp_ref is not None:
                p = h * lanes3(cc_ref[at, :])
                ps = p[0:8]
                for i in range(1, states // 8):
                    ps = ps + p[8 * i : 8 * i + 8]
                put_planes(yp_ref, pl.ds(pl.multiple_of(t0 * 8, 64) + j * 8, 8), ps)
        return h

    lax.fori_loop(0, rows // 8, block, jnp.zeros((states, CH), F32))


def row_of(ref):
    return ref[...].reshape(1, -1)


class Forward:
    def __init__(self, sm, inner, lens_ref, count_ref, tok_ref, gain_ref, gain2_ref, win_ref, small_ref, wout_ref, outs, scratch):
        self.sm, self.inner = sm, inner
        self.lens, self.count, self.tok, self.gain, self.gain2 = lens_ref, count_ref, tok_ref, gain_ref, gain2_ref
        self.win, self.small, self.wout = win_ref, small_ref, wout_ref
        (self.normed, self.src, self.gate, self.lin, self.ym, self.exp, self.gated, self.middle, self.moe, self.sum) = outs
        self.conved, self.dl, self.dx, self.bb, self.cc, self.yp = scratch
        self.chunks = inner // CH
        self.rows = tok_ref.shape[0]

    def start(self):
        self.normed[...] = norm_of(self.tok[...].astype(F32), row_of(self.gain)).astype(LOW)
        self.exp[...] = jnp.zeros_like(self.exp)

    def project(self, k):
        self.conved[:, lane_chunk(k)] = forward_chunk_conv(
            k, self.sm, self.lens, self.normed, self.win, self.small, self.src, self.gate, self.exp, self.inner
        )

    def spread(self):
        sm = self.sm
        expanded = self.exp[...]
        spread(expanded, sm.rank, sm.states, self.bb)
        spread(expanded, sm.rank + sm.states, sm.states, self.cc)

    def scan(self, k):
        sm = self.sm
        expanded = self.exp[...]
        rate = jnp.where(lane_iota(expanded.shape) < sm.rank, expanded, 0.0).astype(LOW)
        prm = params_of(self.small, k)
        lin = dot_nt(rate, self.small[row_chunk(k), LANES : 2 * LANES]) + prm[sm.rate : sm.rate + 1, :]
        self.lin[:, lane_chunk(k)] = lin
        delta = softplus(lin)
        conved = self.conved[:, lane_chunk(k)]
        _, _, opening = segments(self.lens, lin.shape)
        self.dl[...] = jnp.where(opening, 1e30, delta)
        self.dx[...] = delta * conved
        a = -jnp.exp(prm[sm.alog : sm.alog + sm.states, :])
        scan_forward(self.rows, self.dl, self.dx, a, self.bb, sm.states, self.cc, self.yp)
        ym = rows_sum8(self.yp, self.rows) + prm[sm.skip : sm.skip + 1, :] * conved
        self.ym[:, lane_chunk(k)] = ym
        gate = self.gate[:, lane_chunk(k)]
        self.gated[:, lane_chunk(k)] = (ym * (gate * sigmoid(gate))).astype(LOW)

    def end(self):
        valid = row_iota((self.rows, 1)) < self.count[0]
        branch = jnp.where(valid, dot_nn(self.gated[...], self.wout[...]), 0.0)
        self.sum[...] = jnp.broadcast_to(jnp.sum(branch * branch), self.sum.shape)
        middle = self.tok[...].astype(F32) + branch
        self.middle[...] = middle
        self.moe[...] = norm_of(middle, row_of(self.gain2)).astype(LOW)


def mixer_forward_kernel(sm, inner, lens_ref, count_ref, tok_ref, gain_ref, gain2_ref, win_ref, small_ref, wout_ref, *refs):
    f = Forward(sm, inner, lens_ref, count_ref, tok_ref, gain_ref, gain2_ref, win_ref, small_ref, wout_ref, refs[:10], refs[10:])
    f.start()
    pl.loop(0, f.chunks)(f.project)
    f.spread()
    pl.loop(0, f.chunks)(f.scan)
    f.end()


def silu_grad(v, s):
    return s * (1.0 + v * (1.0 - s))


def norm_back(x, gain, grad):
    r = lax.rsqrt(jnp.mean(x * x, axis=-1, keepdims=True) + EPS)
    n = x * r
    q = grad * gain
    return r * (q - n * jnp.mean(q * n, axis=-1, keepdims=True)), grad * n


def scan_backward(rows, states, a, gs_ref, dx_ref, dt_ref, bb_ref, cc_ref, hist_ref, dec_ref, gcp_ref, gbp_ref, lbp_ref, amp_ref):
    blocks = rows // 8

    def fold8(p):
        out = p[0:8]
        for i in range(1, states // 8):
            out = out + p[8 * i : 8 * i + 8]
        return out

    def block(i, carry):
        back, total = carry
        tb = blocks - 1 - i
        t0 = pl.multiple_of(tb * 8, 8)
        g8 = gs_ref[pl.ds(t0, 8), :]
        x8 = dx_ref[pl.ds(t0, 8), :]
        d8 = dt_ref[pl.ds(t0, 8), :]
        for j in range(7, -1, -1):
            base = pl.multiple_of(t0 * states, 8 * states) + j * states
            at = pl.ds(base + states, states)
            prev = pl.ds(base, states)
            here = pl.ds(base, states)
            g = jnp.broadcast_to(g8[j : j + 1, :], (states, CH))
            x = jnp.broadcast_to(x8[j : j + 1, :], (states, CH))
            d = jnp.broadcast_to(d8[j : j + 1, :], (states, CH))
            adj = g * lanes3(cc_ref[here, :]) + back
            gcp_ref[here, :] += fold3(hist_ref[at, :] * g)
            gbp_ref[here, :] += fold3(adj * x)
            out8 = pl.ds(pl.multiple_of(t0 * 8, 64) + j * 8, 8)
            put_planes(lbp_ref, out8, fold8(adj * lanes3(bb_ref[here, :])))
            back = adj * dec_ref[here, :]
            m = back * hist_ref[prev, :]
            put_planes(amp_ref, out8, fold8(m * a))
            total = total + m * d
        return back, total

    zero = jnp.zeros((states, CH), F32)
    _, total = lax.fori_loop(0, blocks, block, (zero, zero))
    return total * a


def column(row):
    return jnp.transpose(jnp.broadcast_to(row, (LANES, LANES)))[:, 0:1]


def padded_router(ref):
    experts, width = ref.shape
    rows = jnp.concatenate([ref[...].astype(F32), jnp.zeros((LANES - experts, width), F32)], axis=0)
    return rows.astype(LOW)


def route(rows_in, router, expert, experts):
    logits = dot_nt(rows_in, router)
    lane = lane_iota(logits.shape)
    logits = jnp.where(lane < experts, logits, -1e30)
    e = jnp.exp(logits - jnp.max(logits, axis=-1, keepdims=True))
    probs = e / jnp.sum(e, axis=-1, keepdims=True)
    onehot = (lane.astype(F32) == expert).astype(F32)
    return probs, onehot, jnp.sum(probs * onehot, axis=-1, keepdims=True)


def some(work, k, chunks):
    per = -(-len(work) // chunks)
    for i in range(chunks):
        share = work[i * per : (i + 1) * per]
        if share:
            def run(share=share):
                for item in share:
                    item()

            pl.when(k == i)(run)


def mixer_backward_kernel(
    sm, inner, experts, nz,
    lens_ref, count_ref, tok_ref, gain_ref, small_ref, gain2_ref,
    normed_ref, src_ref, gate_ref, lin_ref, ym_ref, exp_ref, gated_ref, middle_ref, moe_ref, sum_ref,
    gm_ref, gch_ref, gout_ref, ids_ref, router_ref, win_ref, wout_ref, picked_ref, mine_ref,
    result_ref, gtok_ref, flat_ref, gsmall_ref, gwin_ref, gwout_ref, *refs,
):
    if nz:
        home_ref, other_ref, refs = refs[0], refs[1], refs[2:]
    (
        gmid_s, gmix_s, ggate_s, gconv_s, gs_s, dl_s, dx_s, dt_s, bb_s, cc_s, hist_s, dec_s, gcp_s, gbp_s, lbp_s, amp_s,
        grate_s, gnorm_s, pick_s, wbuf, outs, wsem, osem,
    ) = refs[:23]
    rows, width = tok_ref.shape
    states = sm.states
    chunks = inner // CH
    pieces = width // LANES

    def wout_in(k):
        return pltpu.make_async_copy(wout_ref.at[row_chunk(k), :], wbuf.at[k], wsem.at[k])

    for k in range(chunks):
        wout_in(k).start()
    todo = []
    if nz:
        place = Place(nz)
        place.barrier(1)
        exchange = Exchange(place, mine_ref.at[pl.ds(0, other_ref.shape[0]), :], other_ref, refs[39])
        for i in range(exchange.parts):
            exchange.start(i)
        s_out = Scatter(place, gwout_ref, *refs[23:31], nz)
        s_pick = Scatter(place, picked_ref, *refs[31:39], 2)
        todo = sorted(
            [(t, 0, step, k) for t, step, k in s_out.steps()] + [(t + 4, 1, step, k) for t, step, k in s_pick.steps()],
            key=lambda e: e[:2],
        )
        todo = [partial(step, k) for _, _, step, k in todo]
    early = todo[: 2 * chunks]
    late = todo[2 * chunks :]

    def put_flat(row, v):
        for i in range(pieces):
            flat_ref[row + i : row + i + 1, :] = v[:, i * LANES : (i + 1) * LANES]

    flat_ref[...] = jnp.zeros_like(flat_ref)
    gout = gout_ref[...].astype(F32)
    valid = row_iota((rows, 1)) < count_ref[0]
    expert = column(ids_ref[...].astype(F32))
    moe_in = moe_ref[...]
    router = padded_router(router_ref)
    probs, onehot, chosen = route(moe_in, router, expert, experts)
    if nz:
        gchosen = column(gch_ref[0:1, :])
    else:
        gchosen = jnp.sum(gout * picked_ref[...], axis=-1, keepdims=True)
    gchosen = jnp.where(valid, gchosen, 0.0)
    glogits = (probs * (onehot - chosen) * gchosen).astype(LOW)
    grouter = dot_tn(glogits, moe_in)
    for e in range(experts):
        put_flat((2 + e) * pieces, grouter[e : e + 1, :])
    gmoe = gm_ref[...] + dot_nn(glogits, router)
    gmid, prod = norm_back(middle_ref[...], row_of(gain2_ref), gmoe)
    put_flat(pieces, jnp.sum(prod, axis=0, keepdims=True))
    gmid = gmid + gout
    gmid_s[...] = gmid
    gmix_s[...] = jnp.where(valid, gmid, 0.0).astype(LOW)

    def out_copy(which, k, base):
        dst = (gwout_ref, gwin_ref)[which]
        return pltpu.make_async_copy(outs.at[which, k % 2], dst.at[row_chunk(k, base), :], osem.at[which, k % 2])

    def put_out(which, k, base, v):
        @pl.when(k >= 2)
        def _():
            out_copy(which, k - 2, base).wait()

        outs[which, k % 2] = v.astype(LOW)
        out_copy(which, k, base).start()

    def end_out(which, base):
        for k in (chunks - 2, chunks - 1):
            out_copy(which, k, base).wait()

    @pl.loop(0, chunks)
    def _(k):
        wout_in(k).wait()
        gmix = gmix_s[...]
        gg = dot_nt(gmix, wbuf[k])
        put_out(0, k, 0, dot_tn(gated_ref[:, lane_chunk(k)], gmix))
        gate = gate_ref[:, lane_chunk(k)]
        s = sigmoid(gate)
        gs_s[:, lane_chunk(k)] = gg * (gate * s)
        ggate = (gg * ym_ref[:, lane_chunk(k)] * silu_grad(gate, s)).astype(LOW)
        ggate_s[:, lane_chunk(k)] = ggate
        put_out(1, k, inner, dot_tn(ggate, normed_ref[...]))

    end_out(0, 0)
    if nz:
        s_out.begin()
        s_pick.begin()
    end_out(1, inner)

    slots = chunks // 2

    def win_in(k, half):
        slot = (k % slots) * 2 + half
        return pltpu.make_async_copy(win_ref.at[row_chunk(k, half * inner), :], wbuf.at[slot], wsem.at[slot])

    for k in range(slots):
        win_in(k, 0).start()
        win_in(k, 1).start()
    expanded = exp_ref[...]
    lane = lane_iota((rows, LANES))
    rate = jnp.where(lane < sm.rank, expanded, 0.0).astype(LOW)
    spread(expanded, sm.rank, states, bb_s)
    spread(expanded, sm.rank + states, states, cc_s)
    grate_s[...] = jnp.zeros_like(grate_s)
    gcp_s[...] = jnp.zeros_like(gcp_s)
    gbp_s[...] = jnp.zeros_like(gbp_s)
    gnorm_s[...] = jnp.zeros_like(gnorm_s)
    hist_s[0:states, :] = jnp.zeros((states, CH), F32)

    @pl.loop(0, chunks)
    def _(k):
        prm = params_of(small_ref, k)
        src = src_ref[:, lane_chunk(k)]
        masks = lag_masks(lens_ref, src.shape, sm.taps)
        pre = conv_pre(src, prm, sm, masks)
        conved = pre * sigmoid(pre)
        lin = lin_ref[:, lane_chunk(k)]
        delta = softplus(lin)
        _, _, opening = segments(lens_ref, lin.shape)
        dl_s[...] = jnp.where(opening, 1e30, delta)
        dt_s[...] = delta
        dx_s[...] = delta * conved
        a = -jnp.exp(prm[sm.alog : sm.alog + states, :])
        gs_ref = gs_s.at[:, lane_chunk(k)]
        scan_forward(rows, dl_s, dx_s, a, bb_s, states, hist_ref=hist_s.at[pl.ds(states, rows * states), :], dec_ref=dec_s)
        galog = scan_backward(rows, states, a, gs_ref, dx_s, dt_s, bb_s, cc_s, hist_s, dec_s, gcp_s, gbp_s, lbp_s, amp_s)
        gs = gs_ref[...]
        lb = rows_sum8(lbp_s, rows)
        gdelta = rows_sum8(amp_s, rows) + conved * lb
        glin = gdelta * sigmoid(lin)
        gconv_s[:, lane_chunk(k)] = prm[sm.skip : sm.skip + 1, :] * gs + delta * lb
        glin_low = glin.astype(LOW)
        grate_s[...] += dot_nn(glin_low, small_ref[row_chunk(k), LANES : 2 * LANES])
        part = dot_tn(glin_low, rate)
        grows = jnp.concatenate(
            [
                jnp.zeros((sm.alog, CH), F32),
                galog,
                jnp.zeros((sm.taps + 1, CH), F32),
                jnp.sum(glin, axis=0, keepdims=True),
                jnp.sum(gs * conved, axis=0, keepdims=True),
                jnp.zeros((LANES - sm.end, CH), F32),
            ],
            axis=0,
        )
        gsmall_ref[row_chunk(k), LANES : 2 * LANES] = (part + jnp.transpose(grows)).astype(LOW)
        some(early, k, chunks)

    gexp = jnp.where(lane < sm.rank, grate_s[...], 0.0)
    for s in range(states):
        gb = jnp.sum(gbp_s[pl.ds(s, rows, stride=states), :], axis=1, keepdims=True)
        gc = jnp.sum(gcp_s[pl.ds(s, rows, stride=states), :], axis=1, keepdims=True)
        gexp = jnp.where(lane == sm.rank + s, gb, gexp)
        gexp = jnp.where(lane == sm.rank + states + s, gc, gexp)
    gexp_low = gexp.astype(LOW)

    @pl.loop(0, chunks)
    def _(k):
        prm = params_of(small_ref, k)
        src = src_ref[:, lane_chunk(k)]
        masks = lag_masks(lens_ref, src.shape, sm.taps)
        pre = conv_pre(src, prm, sm, masks)
        s = sigmoid(pre)
        conved_low = (pre * s).astype(LOW)
        gsmall_ref[row_chunk(k), 0:LANES] = dot_tn(conved_low, gexp_low).astype(LOW)
        gconv = gconv_s[:, lane_chunk(k)] + dot_nt(gexp_low, small_ref[row_chunk(k), 0:LANES])
        p = gconv * silu_grad(pre, s)
        gsrc = prm[sm.conv : sm.conv + 1, :] * p
        taps = [jnp.sum(p * src, axis=0, keepdims=True)]
        for lag in range(1, sm.taps):
            pm = jnp.where(masks[lag], p, 0.0)
            taps.append(jnp.sum(pm * pltpu.roll(src, lag, 0), axis=0, keepdims=True))
            gsrc = gsrc + prm[sm.conv + lag : sm.conv + lag + 1, :] * pltpu.roll(pm, rows - lag, 0)
        grows = jnp.concatenate(
            [jnp.zeros((sm.conv, CH), F32)]
            + taps
            + [jnp.sum(p, axis=0, keepdims=True), jnp.zeros((LANES - sm.bias - 1, CH), F32)],
            axis=0,
        )
        old = gsmall_ref[row_chunk(k), LANES : 2 * LANES].astype(F32)
        gsmall_ref[row_chunk(k), LANES : 2 * LANES] = (old + jnp.transpose(grows)).astype(LOW)
        gsrc_low = gsrc.astype(LOW)
        put_out(1, k, 0, dot_tn(gsrc_low, normed_ref[...]))
        win_in(k, 0).wait()
        win_in(k, 1).wait()
        slot = (k % slots) * 2
        gnorm_s[...] += dot_nn(gsrc_low, wbuf[slot]) + dot_nn(ggate_s[:, lane_chunk(k)], wbuf[slot + 1])

        @pl.when(k + slots < chunks)
        def _():
            win_in(k + slots, 0).start()
            win_in(k + slots, 1).start()

        some(late, k, chunks)

    gtok, prod = norm_back(tok_ref[...].astype(F32), row_of(gain_ref), gnorm_s[...])
    put_flat(0, jnp.sum(prod, axis=0, keepdims=True))
    gtok_ref[...] = gtok + gmid_s[...]
    end_out(1, 0)
    if nz:
        s_pick.result(pick_s)
        picked = pick_s[...]
    else:
        picked = picked_ref[...]
    two = chosen * jnp.where(valid, picked, 0.0)
    result = middle_ref[...] + two
    result_ref[...] = result.astype(LOW)
    squares = jnp.where(valid, result * result, 0.0)
    lane1 = lane_iota((1, LANES))
    stats = jnp.where(lane1 == 0, jnp.sum(squares), 0.0)
    stats = jnp.where(lane1 == 1, sum_ref[0:1, :], stats)
    stats = jnp.where(lane1 == 2, jnp.sum(two * two), stats)
    stats = jnp.where(lane1 == 3, count_ref[0].astype(F32), stats)
    flat_ref[(2 + experts) * pieces : (2 + experts) * pieces + 1, :] = stats
    if nz:
        s_out.result(home_ref)
        s_out.finish()
        s_pick.finish()
        exchange.wait()


VMEM = pltpu.VMEM
SMEM_SPEC = pl.BlockSpec(memory_space=pltpu.SMEM)
VMEM_SPEC = pl.BlockSpec(memory_space=pltpu.VMEM)


def shape_of(shape, dtype):
    return jax.ShapeDtypeStruct(shape, dtype)


def forward_outs(sm, rows, width, inner):
    return (
        shape_of((rows, width), LOW),
        shape_of((rows, inner), F32),
        shape_of((rows, inner), F32),
        shape_of((rows, inner), F32),
        shape_of((rows, inner), F32),
        shape_of((rows, LANES), F32),
        shape_of((rows, inner), LOW),
        shape_of((rows, width), F32),
        shape_of((rows, width), LOW),
        shape_of((8, LANES), F32),
    )


def forward_scratch(sm, rows, inner):
    st = sm.states
    return [
        VMEM((rows, inner), F32),
        VMEM((rows, CH), F32),
        VMEM((rows, CH), F32),
        VMEM((rows * st, LANES), F32),
        VMEM((rows * st, LANES), F32),
        VMEM((CH // LANES, rows * 8, LANES), F32),
    ]


def mixer_forward(sm, lens, count, tokens, gain, gain2, win, small, wout):
    rows, width = tokens.shape
    inner = wout.shape[0]
    return pl.pallas_call(
        partial(mixer_forward_kernel, sm, inner),
        out_shape=forward_outs(sm, rows, width, inner),
        in_specs=[SMEM_SPEC] * 2 + [VMEM_SPEC] * 6,
        out_specs=(VMEM_SPEC,) * 10,
        scratch_shapes=forward_scratch(sm, rows, inner),
        compiler_params=pltpu.CompilerParams(vmem_limit_bytes=60 << 20),
        name="mixer_forward",
    )(lens, count, tokens, gain, gain2, win, small, wout)


def flat_rows(width, experts):
    return -(-((2 + experts) * (width // LANES) + 1) // 8) * 8


MESH = pl.DeviceIdType.MESH


class Place:
    def __init__(self, nz):
        self.nz = nz
        w, n = lax.axis_index("wide"), lax.axis_index("narrow")
        self.z, self.y, self.x, self.c = w // 2, w % 2, n // 2, n % 2

    def flips(self, f2, f3):
        fx = f2 * (1 - self.c) + f3 * self.c
        fy = f3 * (1 - self.c) + f2 * self.c
        return self.x + fx - 2 * self.x * fx, self.y + fy - 2 * self.y * fy

    def device(self, z, f2, f3, fc):
        x, y = self.flips(f2, f3)
        core = 1 - self.c if fc else self.c
        return (z * 2 + y, x * 2 + core)

    def target(self, kind):
        if kind == "sib":
            return self.device(self.z, 0, 0, 1)
        if kind == "d2":
            return self.device(self.z, 1, 0, 0)
        if kind == "d3":
            return self.device(self.z, 0, 1, 0)
        if kind == "far":
            return self.device((self.z + self.nz // 2) % self.nz, 0, 0, 0)
        return self.device(self.z + kind, 0, 0, 0)

    def block(self, zloc, f2, f3, fc):
        x, y = self.flips(f2, f3)
        return zloc * 8 + y * 4 + x * 2 + self.c + fc - 2 * fc * self.c

    def has(self, side, group):
        at = self.z % group + side
        return (at >= 0) & (at < group)

    def barrier(self, far=0):
        sem = pltpu.get_barrier_semaphore()
        for kind in ("sib", "d2", "d3") + (("far",) if far else ()):
            pl.semaphore_signal(sem, inc=1, device_id=self.target(kind), device_id_type=MESH)
        for side in (-1, 1):
            @pl.when(self.has(side, self.nz))
            def _():
                pl.semaphore_signal(sem, inc=1, device_id=self.target(side), device_id_type=MESH)
        below = (self.z + self.nz - 1) // self.nz
        above = (2 * self.nz - 2 - self.z) // self.nz
        pl.semaphore_wait(sem, 3 + far + below + above)


def when(cond, body):
    if cond is True:
        body()
    else:
        pl.when(cond)(body)


class Gather:
    def __init__(self, place, src, out, send, recv, local, group):
        self.place, self.src, self.out, self.send, self.recv, self.local, self.group = place, src, out, send, recv, local, group
        self.rows = src.shape[0]
        self.slots = 0
        self.sent = []

    def at(self, p):
        return self.out.at[pl.ds(pl.multiple_of(p * self.rows, 8), self.rows), :]

    def copy(self, src, p, kind, slot):
        return pltpu.make_async_remote_copy(
            src, self.at(p), self.send.at[slot], self.recv.at[p], device_id=self.place.target(kind), device_id_type=MESH
        )

    def push(self, rel, kinds):
        for kind in kinds:
            slot = self.slots
            self.slots += 1
            self.sent.append((rel, kind, slot))

            def go(kind=kind, slot=slot):
                p, src = self.source(rel)
                self.copy(src, p, kind, slot).start()

            when(self.extra(kind), go)

    def extra(self, kind):
        return True if isinstance(kind, str) else self.place.has(kind, self.group)

    def source(self, rel):
        zloc = self.place.z % self.group
        if rel is None:
            return self.place.block(zloc, 0, 0, 0), self.src
        p = self.place.block(zloc + rel[0], rel[1], rel[2], 0)
        return p, self.at(p)

    def begin(self):
        p, src = self.source(None)
        self.push(None, [-1, 1, "d2", "d3", "sib"])
        pltpu.make_async_copy(src, self.at(p), self.local).start()

    def begin_z(self):
        self.push(None, [-1, 1])

    def handle_z(self, dist):
        def body():
            self.wait_block(self.place.block(self.place.z % self.group + dist, 0, 0, 0))
            self.push((dist, 0, 0), [1 if dist < 0 else -1])

        when(self.place.has(dist, self.group), body)

    def begin_xy(self):
        p, src = self.source(None)
        self.push(None, ["d2", "d3", "sib"])
        pltpu.make_async_copy(src, self.at(p), self.local).start()

    def pass_on(self, dist):
        def body():
            self.push((dist, 0, 0), ["d2", "d3", "sib"])

        when(self.place.has(dist, self.group), body)

    def wait_block(self, p):
        self.copy(self.src, p, "sib", 0).wait_recv()

    def events(self):
        out = []
        for dist in range(-self.group + 1, self.group):
            for f2 in (0, 1):
                for f3 in (0, 1):
                    if dist or f2 or f3:
                        out.append((abs(dist) + f2 + 2 * f3, dist, f2, f3))
        return sorted(out)

    def handle(self, dist, f2, f3):
        zloc = self.place.z % self.group
        cond = True if dist == 0 else self.place.has(dist, self.group)
        kinds = ["sib"]
        if not f3:
            kinds = ["d3"] + kinds
            if not f2:
                kinds = [1 if dist < 0 else -1, "d2"] + kinds

        def body():
            self.wait_block(self.place.block(zloc + dist, f2, f3, 0))
            self.push((dist, f2, f3), kinds)

        when(cond, body)

    def own_wait(self):
        p, src = self.source(None)
        pltpu.make_async_copy(src, self.at(p), self.local).wait()

    def finish(self):
        self.own_wait()
        for f2 in (0, 1):
            for f3 in (0, 1):
                for z in range(self.group):
                    self.wait_block(self.place.block(z, f2, f3, 1))
        self.finish_sends()

    def finish_sends(self):
        for rel, kind, slot in self.sent:
            def end(rel=rel, kind=kind, slot=slot):
                def inner():
                    p, src = self.source(rel)
                    self.copy(src, p, kind, slot).wait_send()

                when(self.extra(kind), inner)

            when(True if rel is None or not rel[0] else self.place.has(rel[0], self.group), end)

    @staticmethod
    def sends(group):
        return 5 + sum(2 + (not f3) + 2 * ((not f3) and (not f2)) for d in range(-group + 1, group) for f2 in (0, 1) for f3 in (0, 1))


def run_gathers(gathers):
    for g in gathers:
        g.begin()
    events = []
    for i, g in enumerate(gathers):
        events += [(e[0], i) + e[1:] for e in g.events()]
    for _, i, dist, f2, f3 in sorted(events):
        gathers[i].handle(dist, f2, f3)
    for g in gathers:
        g.finish()


class Exchange:
    parts = 3

    def __init__(self, place, src, out, sems):
        rows = src.shape[0] // self.parts
        assert rows % 8 == 0
        self.copies = [
            pltpu.make_async_remote_copy(
                src.at[pl.ds(i * rows, rows), :], out.at[pl.ds(i * rows, rows), :], sems.at[0, i], sems.at[1, i],
                device_id=place.target("far"), device_id_type=MESH,
            )
            for i in range(self.parts)
        ]

    def start(self, i):
        self.copies[i].start()

    def wait(self):
        for copy in self.copies:
            copy.wait()


class Scatter:
    def __init__(self, place, src, acc, rsib, rd3, rd2, rz, send, recv, local, group):
        self.place, self.src, self.acc = place, src, acc
        self.rows = rsib.shape[1]
        self.rsib, self.rd3, self.rd2, self.rz = rsib, rd3, rd2, rz
        self.send, self.recv, self.local, self.group = send, recv, local, group
        z = place.z % group
        self.zloc = z
        if group == 2:
            self.order = [(1 - z, 1 - 2 * z)]
        else:
            h, low = z // 2, z % 2
            self.order = [(3 * (1 - h), 1 - 2 * h), (2 - h, 1 - 2 * h), (2 * h + 1 - low, 1 - 2 * low)]
        self.dests = [zz for zz, _ in self.order] + [z]

    def copy(self, src, dst, send, recv, target):
        return pltpu.make_async_remote_copy(
            src, dst, self.send.at[send], self.recv.at[recv], device_id=target, device_id_type=MESH
        )

    def part(self, p):
        if len(self.src.shape) == 3:
            return self.src.at[p]
        return self.src.at[pl.ds(pl.multiple_of(p * self.rows, 8), self.rows), :]

    def sum(self, zz, f2, f3):
        if self.acc is None:
            return self.part(self.place.block(zz, f2, f3, 0))
        return self.acc.at[zz * 4 + f2 * 2 + f3]

    def to_sib(self, k, f2, f3):
        at = self.dests[k] * 4 + f3 * 2 + f2
        src = self.part(self.place.block(self.dests[k], f2, f3, 1))
        return self.copy(src, self.rsib.at[at], k * 4 + f2 * 2 + f3, at, self.place.target("sib"))

    def to_d3(self, k, f2):
        zz, group = self.dests[k], self.group
        row = 4 * group + k * 2 + f2
        return self.copy(
            self.sum(zz, f2, 1), self.rd3.at[zz * 2 + f2], row, 4 * group + zz * 2 + f2, self.place.target("d3")
        )

    def to_d2(self, k):
        zz, group = self.dests[k], self.group
        return self.copy(self.sum(zz, 1, 0), self.rd2.at[zz], 6 * group + k, 6 * group + zz, self.place.target("d2"))

    def zrow(self, zz, side):
        return zz + self.group * (1 + side) // 2

    def to_z(self, k):
        zz, side = self.order[k]
        row = self.zrow(zz, side)
        return self.copy(self.sum(zz, 0, 0), self.rz.at[row], 7 * self.group + k, 7 * self.group + row, self.place.target(side))

    def received(self, ref, row):
        pltpu.make_async_remote_copy(
            ref, ref, self.send.at[0], self.recv.at[row], device_id=self.place.target("sib"), device_id_type=MESH
        ).wait_recv()
        return ref

    def from_z(self, zz, side):
        row = self.zrow(zz, side)
        return self.received(self.rz.at[row], 7 * self.group + row)

    def local_copy(self, k, f2, f3):
        return pltpu.make_async_copy(
            self.part(self.place.block(self.dests[k], f2, f3, 0)),
            self.sum(self.dests[k], f2, f3),
            self.local.at[k * 4 + f2 * 2 + f3],
        )

    def begin(self):
        for k in range(self.group):
            for f2, f3 in ((1, 1), (1, 0), (0, 1), (0, 0)):
                self.to_sib(k, f2, f3).start()
            if self.acc is not None:
                for f2, f3 in ((1, 1), (0, 1), (1, 0), (0, 0)):
                    self.local_copy(k, f2, f3).start()

    def add(self, acc, ref):
        @pl.loop(0, ref.shape[-1] // LANES)
        def _(i):
            lanes = pl.ds(pl.multiple_of(i * LANES, LANES), LANES)
            acc[:, lanes] = acc[:, lanes] + ref[:, lanes]

    def own(self, k, f2, f3):
        at = self.dests[k] * 4 + f2 * 2 + f3
        if self.acc is not None:
            self.local_copy(k, f2, f3).wait()
        acc = self.sum(self.dests[k], f2, f3)
        self.add(acc, self.received(self.rsib.at[at], at))
        return acc

    def step_a(self, k):
        for f2 in (1, 0):
            self.own(k, f2, 1)
            self.to_d3(k, f2).start()

    def add_d3(self, k, f2, at):
        row = self.dests[k] * 2 + f2
        self.add(at, self.received(self.rd3.at[row], 4 * self.group + row))

    def step_b(self, k):
        at = self.own(k, 1, 0)
        self.add_d3(k, 1, at)
        self.to_d2(k).start()

    def step_c(self, k):
        at = self.own(k, 0, 0)
        self.add_d3(k, 0, at)
        zz = self.dests[k]
        self.add(at, self.received(self.rd2.at[zz], 6 * self.group + zz))
        if k < self.group - 1:
            side = self.order[k][1]

            @pl.when(self.place.has(-side, self.group))
            def _():
                self.add(at, self.from_z(zz, side))

            self.to_z(k).start()

    def result(self, out):
        out[...] = self.sum(self.zloc, 0, 0)[...].astype(out.dtype)
        for side in (-1, 1):
            @pl.when(self.place.has(side, self.group))
            def _():
                out[...] += self.from_z(self.zloc, -side)[...].astype(out.dtype)

    def steps(self):
        out = []
        for k in range(self.group):
            out += [(3 * k, self.step_a, k), (3 * k + 4, self.step_b, k), (3 * k + 8, self.step_c, k)]
        return sorted(out, key=lambda e: e[0])

    def finish(self):
        for k in range(self.group):
            for f2 in (0, 1):
                for f3 in (0, 1):
                    self.to_sib(k, f2, f3).wait_send()
                self.to_d3(k, f2).wait_send()
            self.to_d2(k).wait_send()
            if k < self.group - 1:
                self.to_z(k).wait_send()

    @staticmethod
    def scratch(group, rows, cols, dtype, in_place=False):
        return [
            VMEM((8, LANES) if in_place else (4 * group, rows, cols), dtype),
            VMEM((4 * group, rows, cols), dtype),
            VMEM((2 * group, rows, cols), dtype),
            VMEM((group, rows, cols), dtype),
            VMEM((2 * group, rows, cols), dtype),
            pltpu.SemaphoreType.DMA((8 * group,)),
            pltpu.SemaphoreType.DMA((9 * group,)),
            pltpu.SemaphoreType.DMA((4 * group,)),
        ]


ORDERS = (("z", "x", "y"), ("x", "y", "z"), ("y", "z", "x"))


class Cube:
    def __init__(self, place, order):
        self.place, self.order = place, order

    def flip(self, rel):
        at = dict(zip(self.order, rel))
        return at["z"], at["x"], at["y"]

    def target(self, i):
        place = self.place
        if i == 3:
            return place.device(place.z, 0, 0, 1)
        fz, fx, fy = self.flip([int(i == j) for j in range(3)])
        z = place.z + fz * (1 - 2 * (place.z % 2))
        return (z * 2 + place.y + fy * (1 - 2 * place.y), (place.x + fx * (1 - 2 * place.x)) * 2 + place.c)

    def block(self, rel, fc):
        place = self.place
        fz, fx, fy = self.flip(rel)
        z = place.z % 2
        at = [v + f * (1 - 2 * v) for v, f in ((z, fz), (place.y, fy), (place.x, fx), (place.c, fc))]
        return at[0] * 8 + at[1] * 4 + at[2] * 2 + at[3]


RELS = [(f1, f2, f3) for f1 in (0, 1) for f2 in (0, 1) for f3 in (0, 1)]


class CubeGather(Cube):
    def __init__(self, place, order, src, out, cols, send, recv, local):
        super().__init__(place, order)
        self.src, self.out, self.cols = src, out, cols
        self.send, self.recv, self.local = send, recv, local
        self.rows = src.shape[0]
        self.slots = []

    def at(self, p):
        return self.out.at[pl.ds(pl.multiple_of(p * self.rows, 8), self.rows), self.cols]

    def copy(self, rel, i, slot):
        p = self.block(rel, 0)
        src = self.at(p) if any(rel) else self.src.at[:, self.cols]
        return pltpu.make_async_remote_copy(
            src, self.at(p), self.send.at[slot], self.recv.at[p], device_id=self.target(i), device_id_type=MESH
        )

    def push(self, rel):
        last = max([i for i in range(3) if rel[i]], default=-1)
        for i in list(range(last + 1, 3)) + [3]:
            self.copy(rel, i, len(self.slots)).start()
            self.slots.append((rel, i))

    def local_copy(self):
        return pltpu.make_async_copy(self.src.at[:, self.cols], self.at(self.block((0, 0, 0), 0)), self.local)

    def begin(self):
        self.push((0, 0, 0))
        self.local_copy().start()

    def wait_block(self, rel, fc):
        here = self.at(self.block(rel, fc))
        pltpu.make_async_remote_copy(
            here, here, self.send.at[0], self.recv.at[self.block(rel, fc)], device_id=self.target(3), device_id_type=MESH
        ).wait_recv()

    def handle(self, rel):
        self.wait_block(rel, 0)
        self.push(rel)

    def finish_sends(self):
        for slot, (rel, i) in enumerate(self.slots):
            self.copy(rel, i, slot).wait_send()

    @staticmethod
    def scratch():
        return [pltpu.SemaphoreType.DMA((15,)), pltpu.SemaphoreType.DMA((16,)), pltpu.SemaphoreType.DMA]


class CubeScatter(Cube):
    def __init__(self, place, order, src, cols, acc, rsib, r3, r2, r1, send, recv, local):
        super().__init__(place, order)
        self.src, self.cols, self.acc = src, cols, acc
        self.rsib, self.r3, self.r2, self.r1 = rsib, r3, r2, r1
        self.send, self.recv, self.local = send, recv, local
        self.rows = rsib.shape[1]

    def part(self, p):
        if len(self.src.shape) == 3:
            return self.src.at[p, :, self.cols]
        return self.src.at[pl.ds(pl.multiple_of(p * self.rows, 8), self.rows), self.cols]

    def sum(self, rel):
        if self.acc is None:
            return self.part(self.block(rel, 0))
        return self.acc.at[rel[0] * 4 + rel[1] * 2 + rel[2]]

    def copy(self, src, dst, slot, i):
        return pltpu.make_async_remote_copy(
            src, dst, self.send.at[slot], self.recv.at[slot], device_id=self.target(i), device_id_type=MESH
        )

    def to_sib(self, rel):
        at = rel[0] * 4 + rel[1] * 2 + rel[2]
        return self.copy(self.part(self.block(rel, 1)), self.rsib.at[at], at, 3)

    def onward(self, rel):
        if rel[2]:
            at = rel[0] * 2 + rel[1]
            return self.copy(self.sum(rel), self.r3.at[at], 8 + at, 2)
        if rel[1]:
            return self.copy(self.sum(rel), self.r2.at[rel[0]], 12 + rel[0], 1)
        return self.copy(self.sum(rel), self.r1.at[0], 14, 0)

    def local_copy(self, rel):
        at = rel[0] * 4 + rel[1] * 2 + rel[2]
        return pltpu.make_async_copy(self.part(self.block(rel, 0)), self.acc.at[at], self.local.at[at])

    def begin(self):
        for rel in reversed(RELS):
            self.to_sib(rel).start()
        if self.acc is not None:
            for rel in reversed(RELS):
                self.local_copy(rel).start()

    def received(self, ref, slot):
        pltpu.make_async_remote_copy(
            ref, ref, self.send.at[0], self.recv.at[slot], device_id=self.target(3), device_id_type=MESH
        ).wait_recv()
        return ref

    def add(self, acc, ref):
        @pl.loop(0, ref.shape[-1] // LANES)
        def _(i):
            lanes = pl.ds(pl.multiple_of(i * LANES, LANES), LANES)
            acc[:, lanes] = acc[:, lanes] + ref[:, lanes]

    def step(self, rel):
        at = rel[0] * 4 + rel[1] * 2 + rel[2]
        if self.acc is not None:
            self.local_copy(rel).wait()
        acc = self.sum(rel)
        self.add(acc, self.received(self.rsib.at[at], at))
        if not rel[2]:
            row = rel[0] * 2 + rel[1]
            self.add(acc, self.received(self.r3.at[row], 8 + row))
            if not rel[1]:
                self.add(acc, self.received(self.r2.at[rel[0]], 12 + rel[0]))
                if not rel[0]:
                    self.add(acc, self.received(self.r1.at[0], 14))
        if any(rel):
            self.onward(rel).start()

    def result(self, out):
        out[:, self.cols] = self.sum((0, 0, 0))[...].astype(out.dtype)

    def finish(self):
        for rel in RELS:
            self.to_sib(rel).wait_send()
            if any(rel):
                self.onward(rel).wait_send()

    @staticmethod
    def scratch(rows, cols, dtype, in_place):
        return [
            VMEM((8, LANES) if in_place else (8, rows, cols), dtype),
            VMEM((8, rows, cols), dtype),
            VMEM((4, rows, cols), dtype),
            VMEM((2, rows, cols), dtype),
            VMEM((1, rows, cols), dtype),
            pltpu.SemaphoreType.DMA((15,)),
            pltpu.SemaphoreType.DMA((15,)),
            pltpu.SemaphoreType.DMA((8,)),
        ]


def thirds(width):
    step = width // 3
    return [pl.ds(i * step, step) for i in range(3)]


def run_scatters(scatters, outs, gathers=()):
    for g in gathers:
        g.begin()
    for s in scatters:
        s.begin()
    steps = []
    for i, s in enumerate(scatters):
        steps += [(t, i, step, k) for t, step, k in s.steps()]
    for _, _, step, k in sorted(steps, key=lambda e: e[:2]):
        step(k)
    for g in gathers:
        for _, dist, f2, f3 in g.events():
            g.handle(dist, f2, f3)
    for s, out in zip(scatters, outs):
        s.result(out)
    for s in scatters:
        s.finish()
    for g in gathers:
        g.finish()


ANY_SPEC = pl.BlockSpec(memory_space=pl.ANY)


def gather_scratch(group):
    return [
        pltpu.SemaphoreType.DMA((Gather.sends(group),)),
        pltpu.SemaphoreType.DMA((group * 8,)),
        pltpu.SemaphoreType.DMA,
    ]


def gather_kernel(nz, groups, *refs):
    n = len(groups)
    srcs, outs, scr = refs[:n], refs[n : 2 * n], refs[2 * n :]
    place = Place(nz)
    place.barrier()
    run_gathers(
        [Gather(place, srcs[i], outs[i], *scr[3 * i : 3 * i + 3], groups[i]) for i in range(n)]
    )


def gather_call(nz, groups, arrays, collective_id):
    return pl.pallas_call(
        partial(gather_kernel, nz, groups),
        out_shape=tuple(shape_of((g * 8 * a.shape[0], a.shape[1]), a.dtype) for g, a in zip(groups, arrays)),
        in_specs=[ANY_SPEC] * len(arrays),
        out_specs=(ANY_SPEC,) * len(arrays),
        scratch_shapes=sum([gather_scratch(g) for g in groups], []),
        compiler_params=pltpu.CompilerParams(collective_id=collective_id, has_side_effects=True, vmem_limit_bytes=60 << 20),
        name="gather_blocks",
    )(*arrays)


def scatter_kernel(nz, groups, gathered, *refs):
    n = len(groups)
    g = len(gathered)
    srcs, gsrcs, outs, gouts, scr = refs[:n], refs[n : n + g], refs[n + g : 2 * n + g], refs[2 * n + g : 2 * n + 2 * g], refs[2 * n + 2 * g :]
    place = Place(nz)
    place.barrier()
    scatters = [Scatter(place, srcs[i], *scr[8 * i : 8 * i + 8], groups[i]) for i in range(n)]
    more = scr[8 * n :]
    gathers = [Gather(place, gsrcs[i], gouts[i], *more[3 * i : 3 * i + 3], gathered[i]) for i in range(g)]
    run_scatters(scatters, outs, gathers)


def scatter_call(nz, groups, arrays, gathered, garrays, collective_id):
    return pl.pallas_call(
        partial(scatter_kernel, nz, groups, gathered),
        out_shape=tuple(shape_of((a.shape[0] // (8 * g), a.shape[1]), F32) for g, a in zip(groups, arrays))
        + tuple(shape_of((g * 8 * a.shape[0], a.shape[1]), a.dtype) for g, a in zip(gathered, garrays)),
        in_specs=[ANY_SPEC] * (len(arrays) + len(garrays)),
        out_specs=(VMEM_SPEC,) * len(arrays) + (ANY_SPEC,) * len(garrays),
        scratch_shapes=sum([Scatter.scratch(g, a.shape[0] // (8 * g), a.shape[1], a.dtype) for g, a in zip(groups, arrays)], [])
        + sum([gather_scratch(g) for g in gathered], []),
        compiler_params=pltpu.CompilerParams(collective_id=collective_id, has_side_effects=True, vmem_limit_bytes=60 << 20),
        name="scatter_blocks",
    )(*arrays, *garrays)


FAR_AT = 5.0


def forward_gather_kernel(sm, inner, nz, lens_ref, count_ref, tok_ref, gain_ref, gain2_ref, *refs):
    (win_src, wout_src, up_ref, down_ref, wx_ref, wdt_ref, alog_ref, convw_ref, convb_ref, rate_ref, skip_ref) = refs[:11]
    outs, alls, other, odown, refs = refs[11:21], refs[21:24], refs[24], refs[25], refs[26:]
    win_v, small_v, wout_v, load, small_src, turned = refs[:6]
    fwd_scratch, far, far_down, sems = refs[6:12], refs[12], refs[13], refs[14:]
    here = small_src.shape[0]
    srcs = (win_src, small_src, wout_src)
    place = Place(nz)
    f = Forward(sm, inner, lens_ref, count_ref, tok_ref, gain_ref, gain2_ref, win_v, small_v, wout_v, outs, fwd_scratch)
    place.barrier(1)
    exchange = Exchange(place, up_ref, other, far)
    more = Exchange(place, down_ref.at[pl.ds(0, DOWN_FIRST), :], odown, far_down)
    g_win, g_small, g_wout = (Gather(place, srcs[i], alls[i], *sems[3 * i : 3 * i + 3], nz) for i in range(3))
    win_hbm, small_hbm, wout_hbm = alls
    g_win.begin()
    turned[...] = jnp.zeros_like(turned)
    for at, ref in ((0, wdt_ref), (sm.alog, alog_ref), (sm.conv, convw_ref), (sm.bias, convb_ref), (sm.rate, rate_ref), (sm.skip, skip_ref)):
        turned[at : at + ref.shape[0], 0:here] = ref[...].astype(F32)
    small_src[:, 0:LANES] = jnp.zeros((here, LANES), LOW)
    small_src[:, 0 : wx_ref.shape[1]] = wx_ref[...]
    small_src[:, LANES : 2 * LANES] = jnp.transpose(turned[...])[0:here, :].astype(LOW)
    g_small.begin()
    g_wout.begin_z()
    f.start()
    events = []
    for i, g in enumerate((g_small, g_win)):
        events += [(e[0], i, partial(g.handle, *e[1:])) for e in g.events()]
    span = nz - 1
    for dist in range(1, nz):
        for side in (-1, 1):
            events.append((span + dist / 2, 2, partial(g_wout.handle_z, side * dist)))
    for i in range(Exchange.parts):
        events.append((FAR_AT, 3, partial(exchange.start, i)))
        events.append((FAR_AT, 3.5, partial(more.start, i)))
    events.append((span + 2, 4, g_wout.begin_xy))
    for _, _, event in sorted(events, key=lambda e: e[:2]):
        event()
    g_small.finish()
    small_in = pltpu.make_async_copy(small_hbm, small_v, load.at[0])
    small_in.start()
    g_win.finish()

    def win_in(k, half):
        rows = row_chunk(k, half * inner)
        return pltpu.make_async_copy(win_hbm.at[rows, :], win_v.at[rows, :], load.at[2 + 2 * k + half])

    for k in range(f.chunks):
        win_in(k, 0).start()
        win_in(k, 1).start()
    small_in.wait()
    near = sorted(((abs(d), d) for d in range(1 - nz, nz) if d))
    todo = [partial(g_wout.pass_on, d) for _, d in near]
    todo += [partial(g_wout.handle, *e[1:]) for e in g_wout.events() if e[2] or e[3]]
    split = len(todo) // 2
    first, second = todo[:split], todo[split:]

    @pl.loop(0, f.chunks)
    def _(k):
        win_in(k, 0).wait()
        win_in(k, 1).wait()
        f.project(k)
        some(first, k, f.chunks)

    f.spread()

    @pl.loop(0, f.chunks)
    def _(k):
        f.scan(k)
        some(second, k, f.chunks)

    g_wout.finish()
    wout_in = pltpu.make_async_copy(wout_hbm, wout_v, load.at[1])
    wout_in.start()
    wout_in.wait()
    f.end()
    exchange.wait()
    more.wait()


def forward_gather(sm, nz, lens, count, tokens, gain, gain2, win, wout, up, down, smalls, collective_id):
    rows, width = tokens.shape
    devices = 8 * nz
    inner = wout.shape[0] * devices
    here = wout.shape[0]
    alls = (shape_of((2 * inner, width), LOW), shape_of((inner, 2 * LANES), LOW), shape_of((inner, width), LOW))
    return pl.pallas_call(
        partial(forward_gather_kernel, sm, inner, nz),
        out_shape=forward_outs(sm, rows, width, inner) + alls + (shape_of(up.shape, up.dtype), shape_of((DOWN_FIRST, width), LOW)),
        in_specs=[SMEM_SPEC] * 2 + [VMEM_SPEC] * 3 + [ANY_SPEC] * 4 + [VMEM_SPEC] * 7,
        out_specs=(VMEM_SPEC,) * 10 + (ANY_SPEC,) * 5,
        scratch_shapes=[VMEM(a.shape, a.dtype) for a in alls[:3]]
        + [pltpu.SemaphoreType.DMA((2 + 2 * (inner // CH),)), VMEM((here, 2 * LANES), LOW), VMEM((LANES, LANES), F32)]
        + forward_scratch(sm, rows, inner)
        + [pltpu.SemaphoreType.DMA((2, Exchange.parts))] * 2
        + sum([gather_scratch(g) for g in (nz, nz, nz)], []),
        compiler_params=pltpu.CompilerParams(collective_id=collective_id, has_side_effects=True, vmem_limit_bytes=62 << 20),
        name="forward_gather",
    )(lens, count, tokens, gain, gain2, win, wout, up, down, *smalls)


GELU_A = 0.7978845608028654
GELU_B = 0.044715


def gelu_parts(v):
    inside = GELU_A * (v + GELU_B * v * v * v)
    t = jnp.tanh(inside)
    slope = 0.5 * (1.0 + t) + 0.5 * v * (1.0 - t * t) * (GELU_A * (1.0 + 3.0 * GELU_B * v * v))
    return 0.5 * v * (1.0 + t), slope


DOWN_FIRST = 96


def expert_kernel(
    experts, nz, count_ref, moe_ref, gout_ref, ids_ref, up_ref, other_ref, down_ref, odown_ref, router_ref,
    picked_ref, gm_ref, gch_ref, gmine_ref, gother_ref,
    all_s, gall_s, call_s, code_s, wu_s, wd_s, gm_s, gch_s, go_s, gpre_s, hid_s, slope_s, hidden_s, far, *refs,
):
    group = 2
    rows, width = moe_ref.shape
    block = 2 * rows
    units = up_ref.shape[0]
    per = units // experts
    place = Place(nz)
    place.barrier(1)
    cuts = thirds(width)
    gather = [CubeGather(place, ORDERS[i], moe_ref, all_s, cuts[i], *refs[3 * i : 3 * i + 3]) for i in range(3)]
    refs = refs[9:]
    gouts = [CubeGather(place, ORDERS[i], gout_ref, gall_s, cuts[i], *refs[3 * i : 3 * i + 3]) for i in range(3)]
    refs = refs[9:]
    codes = [CubeGather(place, ORDERS[0], code_s, call_s, pl.ds(0, LANES), *refs[:3])]
    refs = refs[3:]
    left = units - DOWN_FIRST
    exchange = Exchange(place, down_ref.at[pl.ds(DOWN_FIRST, left), :], wd_s.at[pl.ds(units + DOWN_FIRST, left), :], far)
    grads = [CubeScatter(place, ORDERS[i], gm_s, cuts[i], None, *refs[8 * i + 1 : 8 * i + 8]) for i in range(3)]
    chosens = CubeScatter(place, ORDERS[0], gch_s, pl.ds(0, LANES), None, *refs[25:32])
    ids = ids_ref[...]
    code = jnp.where(lane_iota(ids.shape) < count_ref[0], ids, ids + experts).astype(F32)
    code_s[...] = jnp.broadcast_to(code, code_s.shape)
    for g in codes + gather + gouts:
        g.begin()
    for part in range(exchange.parts):
        exchange.start(part)
    wu_s[0:units, :] = up_ref[...]
    wu_s[units : 2 * units, :] = other_ref[...]
    wd_s[0:units, :] = down_ref[...]
    wd_s[units : units + DOWN_FIRST, :] = odown_ref[...]
    router = padded_router(router_ref)
    chips = [(i % 2, i // 2 % 2, i // 4) for i in range(8)]
    steps = {1: 1, 3: 2, 7: 3}
    zloc = place.z % group
    zfar = 1 - zloc

    def by_order(g, chip):
        at = dict(zip("zxy", chip))
        return tuple(at[d] for d in g.order)

    def arrive(gathers, i):
        for j, chip in enumerate(chips):
            @pl.when(i == j)
            def _():
                for g in gathers:
                    if j == 0:
                        g.local_copy().wait()
                if j in steps:
                    for near in chips:
                        if sum(near) == steps[j]:
                            for g in gathers:
                                g.handle(by_order(g, near))
                for g in gathers:
                    g.wait_block(by_order(g, chip), 1)

    def chip_of(i):
        fz, fx, fy = i % 2, (i // 2) % 2, i // 4
        at = [v + f * (1 - 2 * v) for v, f in ((zloc, fz), (place.y, fy), (place.x, fx))]
        return at[0] * 4 + at[1] * 2 + at[2]

    def masks(chip):
        parts = [column(call_s[pl.ds(pl.multiple_of(chip * 16 + 8 * c, 8), 8), :][0:1, :]) for c in range(2)]
        code = jnp.concatenate(parts, axis=0)
        expert = jnp.where(code < experts, code, code - experts)
        col = lane_iota((block, 2 * units))
        col = jnp.where(col >= units, col - units, col).astype(F32)
        return code, expert, (col >= expert * per) & (col < (expert + 1.0) * per)

    @pl.loop(0, len(chips))
    def _(i):
        arrive(codes + gather, i)

        chip = chip_of(i)
        at = pl.ds(pl.multiple_of(chip * block, block), block)
        _, _, mask = masks(chip)
        act, slope = gelu_parts(dot_nt(all_s[at, :], wu_s[...]))
        hidden = jnp.where(mask, act, 0.0).astype(LOW)
        hidden_s[at, :] = hidden
        slope_s[at, :] = jnp.where(mask, slope, 0.0)
        lanes = pl.ds(pl.multiple_of(chip * block, block), block)
        hid_s[:, lanes] = jnp.transpose(hidden)

    exchange.wait()

    @pl.loop(0, len(chips))
    def _(i):
        arrive(gouts, i)
        chip = chip_of(i)
        at = pl.ds(pl.multiple_of(chip * block, block), block)
        code, expert, _ = masks(chip)
        hidden = hidden_s[at, :]
        picked_ref[at, :] = dot_nn(hidden, wd_s[...]).astype(LOW)
        _, _, chosen = route(all_s[at, :], router, expert, experts)
        scale = jnp.where(code < experts, chosen, 0.0)
        g = gall_s[at, :]
        back = dot_nt(g, wd_s[...])
        gch = jnp.sum(hidden.astype(F32) * back, axis=1, keepdims=True)
        gpre = (scale * back * slope_s[at, :]).astype(LOW)
        gm = dot_nn(gpre, wu_s[...]).astype(LOW)
        for c in range(2):
            gm_s[2 * chip + c] = gm[c * rows : (c + 1) * rows, :]
            turned = jnp.transpose(jnp.broadcast_to(gch[c * rows : (c + 1) * rows, :], (rows, LANES)))
            gch_s[2 * chip + c] = turned[0:8, :]
        go_s[at, :] = (scale * g.astype(F32)).astype(LOW)
        lanes = pl.ds(pl.multiple_of(chip * block, block), block)
        gpre_s[:, lanes] = jnp.transpose(gpre)
        for j, at_chip in enumerate(chips):
            @pl.when(i == j)
            def _():
                for g in grads + [chosens]:
                    g.to_sib(by_order(g, at_chip)).start()

    def weights(j):
        half = 3
        left, right, base = (gpre_s, all_s, 0) if j < half else (hid_s, go_s, units)
        step = width // half
        at = slice((j % half) * step, (j % half + 1) * step)
        part = dot_nn(left[...], right[:, at])
        gmine_ref[base : base + units, at] = part[0:units, :]
        gother_ref[base : base + units, at] = part[units : 2 * units, :].astype(LOW)

    def sums(rels):
        for rel in rels:
            for g in grads + [chosens]:
                g.step(rel)

    sums([(1, 1, 1), (0, 1, 1), (1, 0, 1), (0, 0, 1)])
    for j in (0, 1, 2):
        weights(j)
    sums([(1, 1, 0)])
    weights(3)
    sums([(0, 1, 0)])
    weights(4)
    sums([(1, 0, 0)])
    weights(5)
    sums([(0, 0, 0)])
    for g in grads:
        g.result(gm_ref)
    chosens.result(gch_ref)
    for g in grads + [chosens]:
        g.finish()
    for g in codes + gather + gouts:
        g.finish_sends()


def expert_call(experts, nz, count, moe_in, gout, ids, up, other, down, odown, router, collective_id):
    rows, width = moe_in.shape
    tokens = rows * 16
    units = 2 * up.shape[0]
    return pl.pallas_call(
        partial(expert_kernel, experts, nz),
        out_shape=(
            shape_of((tokens, width), LOW),
            shape_of((rows, width), F32),
            shape_of((8, LANES), F32),
            shape_of((units, width), F32),
            shape_of((units, width), LOW),
        ),
        in_specs=[SMEM_SPEC] + [ANY_SPEC] * 2 + [VMEM_SPEC] * 6,
        out_specs=(VMEM_SPEC,) * 5,
        scratch_shapes=[
            VMEM((tokens, width), LOW),
            VMEM((tokens, width), LOW),
            VMEM((16 * 8, LANES), F32),
            VMEM((8, LANES), F32),
            VMEM((units, width), LOW),
            VMEM((units, width), LOW),
            VMEM((16, rows, width), LOW),
            VMEM((16, 8, LANES), F32),
            VMEM((tokens, width), LOW),
            VMEM((units, tokens), LOW),
            VMEM((units, tokens), LOW),
            VMEM((tokens, units), F32),
            VMEM((tokens, units), LOW),
            pltpu.SemaphoreType.DMA((2, Exchange.parts)),
        ]
        + CubeGather.scratch() * 7
        + CubeScatter.scratch(rows, width // 3, LOW, True) * 3
        + CubeScatter.scratch(8, LANES, F32, True),
        compiler_params=pltpu.CompilerParams(collective_id=collective_id, has_side_effects=True, vmem_limit_bytes=63 << 20),
        name="experts",
    )(count, moe_in, gout, ids, up, other, down, odown, router)


def mixer_backward(sm, experts, nz, lens, count, tokens, gain, small, gain2, saved, gm, gch, gout, ids, router, win, wout, picked, mine, collective_id):
    rows, width = tokens.shape
    inner = wout.shape[0]
    st = sm.states
    chunks = inner // CH
    here = inner // (8 * nz) if nz else 0
    return pl.pallas_call(
        partial(mixer_backward_kernel, sm, inner, experts, nz),
        out_shape=(
            shape_of((rows, width), LOW),
            shape_of((rows, width), F32),
            shape_of((flat_rows(width, experts), LANES), F32),
            shape_of((inner, 2 * LANES), LOW),
            shape_of((2 * inner, width), LOW),
            shape_of((inner, width), LOW),
        )
        + ((shape_of((here, width), F32), shape_of((mine.shape[0] // 2, width), mine.dtype)) if nz else ()),
        in_specs=[SMEM_SPEC] * 2 + [VMEM_SPEC] * 19 + [ANY_SPEC] * 2 + [ANY_SPEC if nz else VMEM_SPEC, ANY_SPEC],
        out_specs=(VMEM_SPEC,) * 4 + (ANY_SPEC,) * 2 + ((VMEM_SPEC, ANY_SPEC) if nz else ()),
        scratch_shapes=[
            VMEM((rows, width), F32),
            VMEM((rows, width), LOW),
            VMEM((rows, inner), LOW),
            VMEM((rows, inner), F32),
            VMEM((rows, inner), F32),
            VMEM((rows, CH), F32),
            VMEM((rows, CH), F32),
            VMEM((rows, CH), F32),
            VMEM((rows * st, LANES), F32),
            VMEM((rows * st, LANES), F32),
            VMEM(((rows + 1) * st, CH), F32),
            VMEM((rows * st, CH), F32),
            VMEM((rows * st, LANES), F32),
            VMEM((rows * st, LANES), F32),
            VMEM((CH // LANES, rows * 8, LANES), F32),
            VMEM((CH // LANES, rows * 8, LANES), F32),
            VMEM((rows, LANES), F32),
            VMEM((rows, width), F32),
            VMEM((rows, width), F32),
            VMEM((chunks, CH, width), LOW),
            VMEM((2, 2, CH, width), LOW),
            pltpu.SemaphoreType.DMA((chunks,)),
            pltpu.SemaphoreType.DMA((2, 2)),
        ]
        + (Scatter.scratch(nz, here, width, LOW) + Scatter.scratch(2, rows, width, LOW) + [pltpu.SemaphoreType.DMA((2, Exchange.parts))] if nz else []),
        compiler_params=pltpu.CompilerParams(
            collective_id=collective_id if nz else None, has_side_effects=bool(nz), vmem_limit_bytes=63 << 20
        ),
        name="mixer_backward",
    )(lens, count, tokens, gain, small, gain2, *saved, gm, gch, gout, ids, router, win, wout, picked, mine)


def last_kernel(nz, gwin_src, gsmall_src, flat_src, mine_ref, gwin_ref, gsmall_ref, total_ref, other_ref, flat_s, far, *refs):
    place = Place(nz)
    place.barrier(1)
    half = other_ref.shape[0]
    exchange = Exchange(place, mine_ref.at[pl.ds(half, half), :], other_ref, far)
    s_small = Scatter(place, gsmall_src, *refs[0:8], nz)
    s_win = Scatter(place, gwin_src, *refs[8:16], nz)
    g_flat = Gather(place, flat_src, flat_s, *refs[16:19], nz)
    s_win.begin()
    s_small.begin()
    g_flat.begin()
    for i in range(exchange.parts):
        exchange.start(i)
    steps = []
    for i, s in enumerate((s_win, s_small)):
        steps += [(t + i, i, step, k) for t, step, k in s.steps()]
    for i, (_, dist, f2, f3) in enumerate(g_flat.events()):
        steps.append((14 + i / 4, 2, lambda e: g_flat.handle(*e), (dist, f2, f3)))
    for _, _, step, k in sorted(steps, key=lambda e: e[:2]):
        step(k)
    g_flat.finish()
    count = flat_src.shape[0]
    total = flat_s[0:count, :]
    for i in range(1, 8 * nz):
        total = total + flat_s[i * count : (i + 1) * count, :]
    total_ref[...] = total
    s_small.result(gsmall_ref)
    s_win.result(gwin_ref)
    s_small.finish()
    s_win.finish()
    exchange.wait()


def last_call(nz, gwin, gsmall, flat, mine, collective_id):
    width = gwin.shape[1]
    devices = 8 * nz
    here = gsmall.shape[0] // devices
    rows = gwin.shape[0] // devices
    return pl.pallas_call(
        partial(last_kernel, nz),
        out_shape=(shape_of((rows, width), F32), shape_of((here, 2 * LANES), F32), shape_of(flat.shape, F32), shape_of((mine.shape[0] // 2, width), mine.dtype)),
        in_specs=[ANY_SPEC] * 4,
        out_specs=(VMEM_SPEC,) * 3 + (ANY_SPEC,),
        scratch_shapes=[VMEM((devices * flat.shape[0], LANES), F32), pltpu.SemaphoreType.DMA((2, Exchange.parts))]
        + Scatter.scratch(nz, here, 2 * LANES, LOW)
        + Scatter.scratch(nz, rows, width, LOW)
        + gather_scratch(nz),
        compiler_params=pltpu.CompilerParams(collective_id=collective_id, has_side_effects=True, vmem_limit_bytes=60 << 20),
        name="gradient_sums",
    )(gwin, gsmall, flat, mine)


def finish_kernel(
    sm, win_ref, small_ref, total_ref, mine_ref, oup_ref, odown_ref, res_ref, tok_ref, out_ref,
    gwin_ref, gwx_ref, gwdt_ref, galog_ref, gconvw_ref, gconvb_ref, grate_ref, gskip_ref, ggain_ref, ggain2_ref, grouter_ref, rms_ref,
    gup_ref, gdown_ref, result_ref, gtok_ref, gwout_ref,
):
    units = gup_ref.shape[0]
    here, width = out_ref.shape
    gup_ref[...] = mine_ref[0:units, :] + oup_ref[...].astype(F32)
    gdown_ref[...] = mine_ref[units : 2 * units, :] + odown_ref[...].astype(F32)
    result_ref[...] = res_ref[...]
    gtok_ref[...] = tok_ref[...]
    gwout_ref[...] = out_ref[...]
    gwin_ref[...] = win_ref[...]
    gwx_ref[...] = small_ref[:, 0 : gwx_ref.shape[1]]
    total = total_ref[...]
    pieces = width // LANES
    experts = grouter_ref.shape[0]
    row = lambda v, start: jnp.concatenate([v[start + i : start + i + 1, :] for i in range(pieces)], axis=1)
    ggain_ref[...] = row(total, 0).reshape(-1)
    ggain2_ref[...] = row(total, pieces).reshape(-1)
    for e in range(experts):
        grouter_ref[e : e + 1, :] = row(total, (2 + e) * pieces)
    at = (2 + experts) * pieces
    stats = total[at : at + 1, :]
    rms = jnp.sqrt(stats / (stats[:, 3:4] * width))
    lane = lane_iota(rms.shape)
    for i in range(3):
        rms_ref[i] = jnp.sum(jnp.where(lane == i, rms, 0.0))
    block = jnp.concatenate([small_ref[:, LANES : 2 * LANES], jnp.zeros((LANES - here, LANES), F32)], axis=0)
    turned = jnp.transpose(block)
    for at, ref in ((0, gwdt_ref), (sm.alog, galog_ref), (sm.conv, gconvw_ref), (sm.bias, gconvb_ref), (sm.rate, grate_ref), (sm.skip, gskip_ref)):
        ref[...] = turned[at : at + ref.shape[0], 0:here]


def finish_call(sm, experts, wx_cols, win, small, total, mine, oup, odown, result, gtok, gwout):
    here, width = gwout.shape
    half = mine.shape[0] // 2
    f = lambda *s: shape_of(s, F32)
    return pl.pallas_call(
        partial(finish_kernel, sm),
        out_shape=(
            f(*win.shape), f(here, wx_cols), f(sm.rank, here), f(sm.states, here), f(sm.taps, here), f(1, here), f(1, here),
            f(1, here), f(width), f(width), f(experts, width), f(3), f(half, width), f(half, width),
            shape_of(result.shape, result.dtype), f(*gtok.shape), f(*gwout.shape),
        ),
        in_specs=[VMEM_SPEC] * 9,
        out_specs=(VMEM_SPEC,) * 11 + (SMEM_SPEC,) + (VMEM_SPEC,) * 5,
        compiler_params=pltpu.CompilerParams(vmem_limit_bytes=60 << 20),
        name="finish",
    )(win, small, total, mine, oup, odown, result, gtok, gwout)


AXES = ("wide", "narrow")


def experts_local(moe_in, gout, ids, count, w_up, w_down, w_router, experts):
    rows = moe_in.shape[0]
    ups = lax.all_gather(w_up, AXES, axis=2, tiled=True)
    downs = lax.all_gather(w_down, AXES, axis=1, tiled=True)
    probs = jax.nn.softmax(jnp.dot(moe_in, w_router, preferred_element_type=F32), axis=-1)
    onehot = (ids[:, None] == jnp.arange(experts, dtype=jnp.int32)[None, :]).astype(F32)
    chosen = jnp.sum(probs * onehot, axis=-1, keepdims=True)
    live = jnp.arange(rows, dtype=jnp.int32)[:, None] < count[0]
    pre = jnp.einsum("td,edf->etf", moe_in, ups, preferred_element_type=F32)
    act, slope = gelu_parts(pre)
    hidden = act.astype(LOW)
    outs = jnp.einsum("etf,efd->etd", hidden, downs, preferred_element_type=F32)
    picked = jnp.sum(onehot.T[:, :, None] * outs, axis=0)
    scaled = (jnp.where(live, chosen, 0.0) * gout.astype(F32)).astype(LOW)
    grad_expert = onehot.T.astype(LOW)[:, :, None] * scaled[None]
    grad_down = jnp.einsum("etf,etd->fed", hidden, grad_expert, preferred_element_type=LOW)
    grad_act = jnp.einsum("etd,efd->etf", grad_expert, downs, preferred_element_type=F32)
    grad_pre = (grad_act * slope).astype(LOW)
    grad_up = jnp.einsum("td,etf->fed", moe_in, grad_pre, preferred_element_type=LOW)
    gm = jnp.einsum("etf,edf->td", grad_pre, ups, preferred_element_type=F32)
    scatter = partial(lax.psum_scatter, axis_name=AXES, scatter_dimension=0, tiled=True)
    gup = scatter(grad_up).astype(F32).transpose(1, 2, 0)
    gdown = scatter(grad_down).astype(F32).transpose(1, 0, 2)
    return picked, gm, gup, gdown


def per_device(
    nz, tokens, norm_gain, w_in, conv_w, conv_b, w_x, w_dt, dt_bias, a_log, d_skip, w_out, moe_gain, w_router, w_up,
    w_down, seq_lengths, valid_counts, expert_ids, out_grad,
):
    rows, width = tokens.shape
    sm = Small(w_dt.shape[0], a_log.shape[1], conv_w.shape[0])
    here = w_out.shape[0]
    experts, per = w_up.shape[0], w_up.shape[2]
    lens = seq_lengths[0]
    ids = expert_ids[None]
    router = w_router.T
    if nz:
        up = w_up.transpose(0, 2, 1).reshape(experts * per, width)
        down = w_down.reshape(experts * per, width)
        smalls = (w_x, w_dt, a_log.T, conv_w, conv_b[None], dt_bias[None], d_skip[None])
        *saved, win_all, small_all, wout_all, other, odown = forward_gather(
            sm, nz, lens, valid_counts, tokens, norm_gain, moe_gain, w_in.T, w_out, up, down, smalls, 0
        )
        picked, gm, gch, gmine, gother = expert_call(
            experts, nz, valid_counts, saved[8], out_grad, ids, up, other, down, odown, router, 1
        )
    else:
        small = jnp.concatenate(
            [
                w_x, jnp.zeros((here, LANES - w_x.shape[1]), LOW), w_dt.T, a_log, conv_w.T, conv_b[:, None],
                dt_bias[:, None], d_skip[:, None], jnp.zeros((here, LANES - sm.end), LOW),
            ],
            axis=1,
        )
        win_all = lax.all_gather(w_in.T, AXES, axis=0, tiled=True)
        rest_all = lax.all_gather(jnp.concatenate([w_out, small], axis=1), AXES, axis=0, tiled=True)
        wout_all, small_all = rest_all[:, :width], rest_all[:, width:]
        saved = mixer_forward(sm, lens, valid_counts, tokens, norm_gain, moe_gain, win_all, small_all, wout_all)
        picked, gm, gup, gdown = experts_local(saved[8], out_grad, expert_ids, valid_counts, w_up, w_down, w_router, experts)
        gch = jnp.zeros((8, LANES), F32)
        gother = gch
    result, gtok, flat, gsmall, gwin, gwout, *home = mixer_backward(
        sm, experts, nz, lens, valid_counts, tokens, norm_gain, small_all, moe_gain, saved, gm, gch, out_grad, ids, router,
        win_all, wout_all, picked, gother, 2,
    )
    if nz:
        gwin, gsmall, flat, gdown = last_call(nz, gwin, gsmall, flat, gother, 3)
        (
            gwin, gwx, gwdt, galog, gconvw, gconvb, grate, gskip, ggain, ggain2, grouter, rms, gup, gdown, result, gtok, gwout,
        ) = finish_call(sm, experts, w_x.shape[1], gwin, gsmall, flat, gmine, home[1], gdown, result, gtok, home[0])
        return (
            result, gtok, ggain, gwin.T, gconvw, gconvb[0], gwx, gwdt, grate[0], galog.T, gskip[0], gwout, ggain2,
            grouter.T, gup.reshape(experts, per, width).transpose(0, 2, 1), gdown.reshape(experts, per, width), rms,
        )
    scatter = partial(lax.psum_scatter, axis_name=AXES, scatter_dimension=0, tiled=True)
    gwin = scatter(gwin).astype(F32)
    gall = scatter(jnp.concatenate([gwout, gsmall], axis=1)).astype(F32)
    g1, g2 = gall[:, width : width + LANES], gall[:, width + LANES :]
    flat = lax.psum(flat, AXES).reshape(-1)
    ggain, ggain2, flat = flat[:width], flat[width : 2 * width], flat[2 * width :]
    grad_router, flat = flat[: width * experts].reshape(experts, width).T, flat[width * experts :]
    return (
        result, gtok, ggain, gwin.T, g2[:, sm.conv : sm.conv + sm.taps].T, g2[:, sm.bias], g1[:, : w_x.shape[1]],
        g2[:, : sm.rank].T, g2[:, sm.rate], g2[:, sm.alog : sm.alog + sm.states], g2[:, sm.skip], gall[:, :width],
        ggain2, grad_router, gup, gdown, jnp.sqrt(flat[:3] / (flat[3] * width)),
    )


def solution(mesh):
    wide, narrow = mesh.shape["wide"], mesh.shape["narrow"]
    nz = wide // 2 if narrow == 4 and wide == 8 else 0
    both = ("wide", "narrow")
    rows2, cols, one, rep = P(both, None), P(None, both), P(both), P()
    in_specs = (
        rows2, rep, cols, cols, one, rows2, cols, one, rows2, one, rows2, rep, rep, P(None, None, both),
        P(None, both, None), rows2, one, one, rows2,
    )
    out_specs = (
        rows2, rows2, rep, cols, cols, one, rows2, cols, one, rows2, one, rows2, rep, rep, P(None, None, both),
        P(None, both, None), rep,
    )
    return jax.shard_map(partial(per_device, nz), mesh=mesh, in_specs=in_specs, out_specs=out_specs, check_vma=False)
```

```python
from functools import partial

import jax
import jax.numpy as jnp
from jax import lax
from jax.experimental import pallas as pl
from jax.experimental.pallas import tpu as pltpu
from jax.sharding import PartitionSpec as P

EPS = 1e-05
LOW = jnp.bfloat16
F32 = jnp.float32
LANES = 128
CH = 384


def dot_nn(a, b):
    return lax.dot_general(a, b, (((1,), (0,)), ((), ())), preferred_element_type=F32)


def dot_nt(a, b):
    return lax.dot_general(a, b, (((1,), (1,)), ((), ())), preferred_element_type=F32)


def dot_tn(a, b):
    return lax.dot_general(a, b, (((0,), (0,)), ((), ())), preferred_element_type=F32)


def sigmoid(v):
    return 1.0 / (1.0 + jnp.exp(-v))


def softplus(v):
    return jnp.maximum(v, 0.0) + jnp.log1p(jnp.exp(-jnp.abs(v)))


class Small:
    def __init__(self, rank, states, taps):
        self.rank, self.states, self.taps = rank, states, taps
        self.alog = -(-rank // 8) * 8
        self.conv = self.alog + states
        self.bias = self.conv + taps
        self.rate = self.bias + 1
        self.skip = self.bias + 2
        self.end = self.bias + 3


def row_iota(shape):
    return lax.broadcasted_iota(jnp.int32, shape, 0)


def lane_iota(shape):
    return lax.broadcasted_iota(jnp.int32, shape, 1)


def segments(lens_ref, shape):
    first = lens_ref[0]
    second = first + lens_ref[1]
    t = row_iota(shape)
    seg = (t >= first).astype(jnp.int32) + (t >= second).astype(jnp.int32)
    opening = (t == 0) | (t == first) | (t == second)
    return t, seg, opening


def lag_masks(lens_ref, shape, taps):
    first = lens_ref[0]
    second = first + lens_ref[1]
    t = row_iota(shape)
    masks = [None]
    for lag in range(1, taps):
        e = t - lag
        same = ((t >= first) == (e >= first)) & ((t >= second) == (e >= second)) & (e >= 0)
        masks.append(same)
    return masks


def conv_pre(src, prm, sm, masks):
    taps = sm.taps
    total = prm[sm.bias : sm.bias + 1, :] + prm[sm.conv : sm.conv + 1, :] * src
    for lag in range(1, taps):
        moved = jnp.where(masks[lag], pltpu.roll(src, lag, 0), 0.0)
        total = total + prm[sm.conv + lag : sm.conv + lag + 1, :] * moved
    return total


def params_of(small_ref, k):
    blk = small_ref[pl.ds(pl.multiple_of(k * CH, CH), CH), LANES : 2 * LANES]
    return jnp.transpose(blk.astype(F32))


def lanes3(v):
    return jnp.concatenate([v] * (CH // LANES), axis=1)


def fold3(v):
    out = v[:, 0:LANES]
    for i in range(1, CH // LANES):
        out = out + v[:, i * LANES : (i + 1) * LANES]
    return out


def spread(expanded, start, states, out_ref):
    rows = expanded.shape[0]
    for s in range(states):
        col = jnp.broadcast_to(expanded[:, start + s : start + s + 1], (rows, LANES))
        out_ref[pl.ds(s, rows, stride=states), :] = col


def rows_sum8(ref, rows):
    planes = []
    for i in range(CH // LANES):
        out = ref[i, pl.ds(0, rows, stride=8), :]
        for j in range(1, 8):
            out = out + ref[i, pl.ds(j, rows, stride=8), :]
        planes.append(out)
    return jnp.concatenate(planes, axis=1)


def put_planes(ref, at, v):
    for i in range(CH // LANES):
        ref[i, at, :] = v[:, i * LANES : (i + 1) * LANES]


def lane_chunk(k, base=0):
    return pl.ds(pl.multiple_of(base + k * CH, LANES), CH)


def row_chunk(k, base=0):
    return pl.ds(pl.multiple_of(base + k * CH, LANES), CH)


def norm_of(x, gain):
    r = lax.rsqrt(jnp.mean(x * x, axis=-1, keepdims=True) + EPS)
    return x * r * gain


def forward_chunk_conv(k, sm, lens_ref, normed_ref, win_ref, small_ref, src_ref, gate_ref, exp_acc, inner):
    normed = normed_ref[...]
    src = dot_nt(normed, win_ref[row_chunk(k), :])
    src_ref[:, lane_chunk(k)] = src
    gate_ref[:, lane_chunk(k)] = dot_nt(normed, win_ref[row_chunk(k, inner), :])
    prm = params_of(small_ref, k)
    masks = lag_masks(lens_ref, src.shape, sm.taps)
    pre = conv_pre(src, prm, sm, masks)
    conved = pre * sigmoid(pre)
    exp_acc[...] += dot_nn(conved.astype(LOW), small_ref[row_chunk(k), 0:LANES])
    return conved


def scan_forward(rows, dl_ref, dx_ref, a, bb_ref, states, cc_ref=None, yp_ref=None, hist_ref=None, dec_ref=None):
    def block(tb, h):
        t0 = pl.multiple_of(tb * 8, 8)
        d8 = dl_ref[pl.ds(t0, 8), :]
        x8 = dx_ref[pl.ds(t0, 8), :]
        for j in range(8):
            d = jnp.broadcast_to(d8[j : j + 1, :], (states, CH))
            x = jnp.broadcast_to(x8[j : j + 1, :], (states, CH))
            dec = jnp.exp(d * a)
            at = pl.ds(pl.multiple_of(t0 * states, 8 * states) + j * states, states)
            h = h * dec + x * lanes3(bb_ref[at, :])
            if hist_ref is not None:
                hist_ref[at, :] = h
                dec_ref[at, :] = dec
            if yp_ref is not None:
                p = h * lanes3(cc_ref[at, :])
                ps = p[0:8]
                for i in range(1, states // 8):
                    ps = ps + p[8 * i : 8 * i + 8]
                put_planes(yp_ref, pl.ds(pl.multiple_of(t0 * 8, 64) + j * 8, 8), ps)
        return h

    lax.fori_loop(0, rows // 8, block, jnp.zeros((states, CH), F32))


def row_of(ref):
    return ref[...].reshape(1, -1)


class Forward:
    def __init__(self, sm, inner, lens_ref, count_ref, tok_ref, gain_ref, gain2_ref, win_ref, small_ref, wout_ref, outs, scratch):
        self.sm, self.inner = sm, inner
        self.lens, self.count, self.tok, self.gain, self.gain2 = lens_ref, count_ref, tok_ref, gain_ref, gain2_ref
        self.win, self.small, self.wout = win_ref, small_ref, wout_ref
        (self.normed, self.src, self.gate, self.lin, self.ym, self.exp, self.gated, self.middle, self.moe, self.sum) = outs
        self.conved, self.dl, self.dx, self.bb, self.cc, self.yp = scratch
        self.chunks = inner // CH
        self.rows = tok_ref.shape[0]

    def start(self):
        self.normed[...] = norm_of(self.tok[...].astype(F32), row_of(self.gain)).astype(LOW)
        self.exp[...] = jnp.zeros_like(self.exp)

    def project(self, k):
        self.conved[:, lane_chunk(k)] = forward_chunk_conv(
            k, self.sm, self.lens, self.normed, self.win, self.small, self.src, self.gate, self.exp, self.inner
        )

    def spread(self):
        sm = self.sm
        expanded = self.exp[...]
        spread(expanded, sm.rank, sm.states, self.bb)
        spread(expanded, sm.rank + sm.states, sm.states, self.cc)

    def scan(self, k):
        sm = self.sm
        expanded = self.exp[...]
        rate = jnp.where(lane_iota(expanded.shape) < sm.rank, expanded, 0.0).astype(LOW)
        prm = params_of(self.small, k)
        lin = dot_nt(rate, self.small[row_chunk(k), LANES : 2 * LANES]) + prm[sm.rate : sm.rate + 1, :]
        self.lin[:, lane_chunk(k)] = lin
        delta = softplus(lin)
        conved = self.conved[:, lane_chunk(k)]
        _, _, opening = segments(self.lens, lin.shape)
        self.dl[...] = jnp.where(opening, 1e30, delta)
        self.dx[...] = delta * conved
        a = -jnp.exp(prm[sm.alog : sm.alog + sm.states, :])
        scan_forward(self.rows, self.dl, self.dx, a, self.bb, sm.states, self.cc, self.yp)
        ym = rows_sum8(self.yp, self.rows) + prm[sm.skip : sm.skip + 1, :] * conved
        self.ym[:, lane_chunk(k)] = ym
        gate = self.gate[:, lane_chunk(k)]
        self.gated[:, lane_chunk(k)] = (ym * (gate * sigmoid(gate))).astype(LOW)

    def end(self):
        valid = row_iota((self.rows, 1)) < self.count[0]
        branch = jnp.where(valid, dot_nn(self.gated[...], self.wout[...]), 0.0)
        self.sum[...] = jnp.broadcast_to(jnp.sum(branch * branch), self.sum.shape)
        middle = self.tok[...].astype(F32) + branch
        self.middle[...] = middle
        self.moe[...] = norm_of(middle, row_of(self.gain2)).astype(LOW)


def mixer_forward_kernel(sm, inner, lens_ref, count_ref, tok_ref, gain_ref, gain2_ref, win_ref, small_ref, wout_ref, *refs):
    f = Forward(sm, inner, lens_ref, count_ref, tok_ref, gain_ref, gain2_ref, win_ref, small_ref, wout_ref, refs[:10], refs[10:])
    f.start()
    pl.loop(0, f.chunks)(f.project)
    f.spread()
    pl.loop(0, f.chunks)(f.scan)
    f.end()


def silu_grad(v, s):
    return s * (1.0 + v * (1.0 - s))


def norm_back(x, gain, grad):
    r = lax.rsqrt(jnp.mean(x * x, axis=-1, keepdims=True) + EPS)
    n = x * r
    q = grad * gain
    return r * (q - n * jnp.mean(q * n, axis=-1, keepdims=True)), grad * n


def scan_backward(rows, states, a, gs_ref, dx_ref, dt_ref, bb_ref, cc_ref, hist_ref, dec_ref, gcp_ref, gbp_ref, lbp_ref, amp_ref):
    blocks = rows // 8

    def fold8(p):
        out = p[0:8]
        for i in range(1, states // 8):
            out = out + p[8 * i : 8 * i + 8]
        return out

    def block(i, carry):
        back, total = carry
        tb = blocks - 1 - i
        t0 = pl.multiple_of(tb * 8, 8)
        g8 = gs_ref[pl.ds(t0, 8), :]
        x8 = dx_ref[pl.ds(t0, 8), :]
        d8 = dt_ref[pl.ds(t0, 8), :]
        for j in range(7, -1, -1):
            base = pl.multiple_of(t0 * states, 8 * states) + j * states
            at = pl.ds(base + states, states)
            prev = pl.ds(base, states)
            here = pl.ds(base, states)
            g = jnp.broadcast_to(g8[j : j + 1, :], (states, CH))
            x = jnp.broadcast_to(x8[j : j + 1, :], (states, CH))
            d = jnp.broadcast_to(d8[j : j + 1, :], (states, CH))
            adj = g * lanes3(cc_ref[here, :]) + back
            gcp_ref[here, :] += fold3(hist_ref[at, :] * g)
            gbp_ref[here, :] += fold3(adj * x)
            out8 = pl.ds(pl.multiple_of(t0 * 8, 64) + j * 8, 8)
            put_planes(lbp_ref, out8, fold8(adj * lanes3(bb_ref[here, :])))
            back = adj * dec_ref[here, :]
            m = back * hist_ref[prev, :]
            put_planes(amp_ref, out8, fold8(m * a))
            total = total + m * d
        return back, total

    zero = jnp.zeros((states, CH), F32)
    _, total = lax.fori_loop(0, blocks, block, (zero, zero))
    return total * a


def column(row):
    return jnp.transpose(jnp.broadcast_to(row, (LANES, LANES)))[:, 0:1]


def padded_router(ref):
    experts, width = ref.shape
    rows = jnp.concatenate([ref[...].astype(F32), jnp.zeros((LANES - experts, width), F32)], axis=0)
    return rows.astype(LOW)


def route(rows_in, router, expert, experts):
    logits = dot_nt(rows_in, router)
    lane = lane_iota(logits.shape)
    logits = jnp.where(lane < experts, logits, -1e30)
    e = jnp.exp(logits - jnp.max(logits, axis=-1, keepdims=True))
    probs = e / jnp.sum(e, axis=-1, keepdims=True)
    onehot = (lane.astype(F32) == expert).astype(F32)
    return probs, onehot, jnp.sum(probs * onehot, axis=-1, keepdims=True)


def some(work, k, chunks):
    per = -(-len(work) // chunks)
    for i in range(chunks):
        share = work[i * per : (i + 1) * per]
        if share:
            def run(share=share):
                for item in share:
                    item()

            pl.when(k == i)(run)


def mixer_backward_kernel(
    sm, inner, experts, nz,
    lens_ref, count_ref, tok_ref, gain_ref, small_ref, gain2_ref,
    normed_ref, src_ref, gate_ref, lin_ref, ym_ref, exp_ref, gated_ref, middle_ref, moe_ref, sum_ref,
    gm_ref, gch_ref, gout_ref, ids_ref, router_ref, win_ref, wout_ref, picked_ref, mine_ref,
    result_ref, gtok_ref, flat_ref, gsmall_ref, gwin_ref, gwout_ref, *refs,
):
    if nz:
        home_ref, other_ref, refs = refs[0], refs[1], refs[2:]
    (
        gmid_s, gmix_s, ggate_s, gconv_s, gs_s, dl_s, dx_s, dt_s, bb_s, cc_s, hist_s, dec_s, gcp_s, gbp_s, lbp_s, amp_s,
        grate_s, gnorm_s, pick_s, wbuf, outs, wsem, osem,
    ) = refs[:23]
    rows, width = tok_ref.shape
    states = sm.states
    chunks = inner // CH
    pieces = width // LANES

    def wout_in(k):
        return pltpu.make_async_copy(wout_ref.at[row_chunk(k), :], wbuf.at[k], wsem.at[k])

    for k in range(chunks):
        wout_in(k).start()
    todo = []
    if nz:
        place = Place(nz)
        place.barrier(1)
        exchange = Exchange(place, mine_ref.at[pl.ds(0, other_ref.shape[0]), :], other_ref, refs[39])
        for i in range(exchange.parts):
            exchange.start(i)
        s_out = Scatter(place, gwout_ref, *refs[23:31], nz)
        s_pick = Scatter(place, picked_ref, *refs[31:39], 2)
        todo = sorted(
            [(t, 0, step, k) for t, step, k in s_out.steps()] + [(t + 4, 1, step, k) for t, step, k in s_pick.steps()],
            key=lambda e: e[:2],
        )
        todo = [partial(step, k) for _, _, step, k in todo]
    early = todo[: 2 * chunks]
    late = todo[2 * chunks :]

    def put_flat(row, v):
        for i in range(pieces):
            flat_ref[row + i : row + i + 1, :] = v[:, i * LANES : (i + 1) * LANES]

    flat_ref[...] = jnp.zeros_like(flat_ref)
    gout = gout_ref[...].astype(F32)
    valid = row_iota((rows, 1)) < count_ref[0]
    expert = column(ids_ref[...].astype(F32))
    moe_in = moe_ref[...]
    router = padded_router(router_ref)
    probs, onehot, chosen = route(moe_in, router, expert, experts)
    if nz:
        gchosen = column(gch_ref[0:1, :])
    else:
        gchosen = jnp.sum(gout * picked_ref[...], axis=-1, keepdims=True)
    gchosen = jnp.where(valid, gchosen, 0.0)
    glogits = (probs * (onehot - chosen) * gchosen).astype(LOW)
    grouter = dot_tn(glogits, moe_in)
    for e in range(experts):
        put_flat((2 + e) * pieces, grouter[e : e + 1, :])
    gmoe = gm_ref[...] + dot_nn(glogits, router)
    gmid, prod = norm_back(middle_ref[...], row_of(gain2_ref), gmoe)
    put_flat(pieces, jnp.sum(prod, axis=0, keepdims=True))
    gmid = gmid + gout
    gmid_s[...] = gmid
    gmix_s[...] = jnp.where(valid, gmid, 0.0).astype(LOW)

    def out_copy(which, k, base):
        dst = (gwout_ref, gwin_ref)[which]
        return pltpu.make_async_copy(outs.at[which, k % 2], dst.at[row_chunk(k, base), :], osem.at[which, k % 2])

    def put_out(which, k, base, v):
        @pl.when(k >= 2)
        def _():
            out_copy(which, k - 2, base).wait()

        outs[which, k % 2] = v.astype(LOW)
        out_copy(which, k, base).start()

    def end_out(which, base):
        for k in (chunks - 2, chunks - 1):
            out_copy(which, k, base).wait()

    @pl.loop(0, chunks)
    def _(k):
        wout_in(k).wait()
        gmix = gmix_s[...]
        gg = dot_nt(gmix, wbuf[k])
        put_out(0, k, 0, dot_tn(gated_ref[:, lane_chunk(k)], gmix))
        gate = gate_ref[:, lane_chunk(k)]
        s = sigmoid(gate)
        gs_s[:, lane_chunk(k)] = gg * (gate * s)
        ggate = (gg * ym_ref[:, lane_chunk(k)] * silu_grad(gate, s)).astype(LOW)
        ggate_s[:, lane_chunk(k)] = ggate
        put_out(1, k, inner, dot_tn(ggate, normed_ref[...]))

    end_out(0, 0)
    if nz:
        s_out.begin()
        s_pick.begin()
    end_out(1, inner)

    slots = chunks // 2

    def win_in(k, half):
        slot = (k % slots) * 2 + half
        return pltpu.make_async_copy(win_ref.at[row_chunk(k, half * inner), :], wbuf.at[slot], wsem.at[slot])

    for k in range(slots):
        win_in(k, 0).start()
        win_in(k, 1).start()
    expanded = exp_ref[...]
    lane = lane_iota((rows, LANES))
    rate = jnp.where(lane < sm.rank, expanded, 0.0).astype(LOW)
    spread(expanded, sm.rank, states, bb_s)
    spread(expanded, sm.rank + states, states, cc_s)
    grate_s[...] = jnp.zeros_like(grate_s)
    gcp_s[...] = jnp.zeros_like(gcp_s)
    gbp_s[...] = jnp.zeros_like(gbp_s)
    gnorm_s[...] = jnp.zeros_like(gnorm_s)
    hist_s[0:states, :] = jnp.zeros((states, CH), F32)

    @pl.loop(0, chunks)
    def _(k):
        prm = params_of(small_ref, k)
        src = src_ref[:, lane_chunk(k)]
        masks = lag_masks(lens_ref, src.shape, sm.taps)
        pre = conv_pre(src, prm, sm, masks)
        conved = pre * sigmoid(pre)
        lin = lin_ref[:, lane_chunk(k)]
        delta = softplus(lin)
        _, _, opening = segments(lens_ref, lin.shape)
        dl_s[...] = jnp.where(opening, 1e30, delta)
        dt_s[...] = delta
        dx_s[...] = delta * conved
        a = -jnp.exp(prm[sm.alog : sm.alog + states, :])
        gs_ref = gs_s.at[:, lane_chunk(k)]
        scan_forward(rows, dl_s, dx_s, a, bb_s, states, hist_ref=hist_s.at[pl.ds(states, rows * states), :], dec_ref=dec_s)
        galog = scan_backward(rows, states, a, gs_ref, dx_s, dt_s, bb_s, cc_s, hist_s, dec_s, gcp_s, gbp_s, lbp_s, amp_s)
        gs = gs_ref[...]
        lb = rows_sum8(lbp_s, rows)
        gdelta = rows_sum8(amp_s, rows) + conved * lb
        glin = gdelta * sigmoid(lin)
        gconv_s[:, lane_chunk(k)] = prm[sm.skip : sm.skip + 1, :] * gs + delta * lb
        glin_low = glin.astype(LOW)
        grate_s[...] += dot_nn(glin_low, small_ref[row_chunk(k), LANES : 2 * LANES])
        part = dot_tn(glin_low, rate)
        grows = jnp.concatenate(
            [
                jnp.zeros((sm.alog, CH), F32),
                galog,
                jnp.zeros((sm.taps + 1, CH), F32),
                jnp.sum(glin, axis=0, keepdims=True),
                jnp.sum(gs * conved, axis=0, keepdims=True),
                jnp.zeros((LANES - sm.end, CH), F32),
            ],
            axis=0,
        )
        gsmall_ref[row_chunk(k), LANES : 2 * LANES] = (part + jnp.transpose(grows)).astype(LOW)
        some(early, k, chunks)

    gexp = jnp.where(lane < sm.rank, grate_s[...], 0.0)
    for s in range(states):
        gb = jnp.sum(gbp_s[pl.ds(s, rows, stride=states), :], axis=1, keepdims=True)
        gc = jnp.sum(gcp_s[pl.ds(s, rows, stride=states), :], axis=1, keepdims=True)
        gexp = jnp.where(lane == sm.rank + s, gb, gexp)
        gexp = jnp.where(lane == sm.rank + states + s, gc, gexp)
    gexp_low = gexp.astype(LOW)

    @pl.loop(0, chunks)
    def _(k):
        prm = params_of(small_ref, k)
        src = src_ref[:, lane_chunk(k)]
        masks = lag_masks(lens_ref, src.shape, sm.taps)
        pre = conv_pre(src, prm, sm, masks)
        s = sigmoid(pre)
        conved_low = (pre * s).astype(LOW)
        gsmall_ref[row_chunk(k), 0:LANES] = dot_tn(conved_low, gexp_low).astype(LOW)
        gconv = gconv_s[:, lane_chunk(k)] + dot_nt(gexp_low, small_ref[row_chunk(k), 0:LANES])
        p = gconv * silu_grad(pre, s)
        gsrc = prm[sm.conv : sm.conv + 1, :] * p
        taps = [jnp.sum(p * src, axis=0, keepdims=True)]
        for lag in range(1, sm.taps):
            pm = jnp.where(masks[lag], p, 0.0)
            taps.append(jnp.sum(pm * pltpu.roll(src, lag, 0), axis=0, keepdims=True))
            gsrc = gsrc + prm[sm.conv + lag : sm.conv + lag + 1, :] * pltpu.roll(pm, rows - lag, 0)
        grows = jnp.concatenate(
            [jnp.zeros((sm.conv, CH), F32)]
            + taps
            + [jnp.sum(p, axis=0, keepdims=True), jnp.zeros((LANES - sm.bias - 1, CH), F32)],
            axis=0,
        )
        old = gsmall_ref[row_chunk(k), LANES : 2 * LANES].astype(F32)
        gsmall_ref[row_chunk(k), LANES : 2 * LANES] = (old + jnp.transpose(grows)).astype(LOW)
        gsrc_low = gsrc.astype(LOW)
        put_out(1, k, 0, dot_tn(gsrc_low, normed_ref[...]))
        win_in(k, 0).wait()
        win_in(k, 1).wait()
        slot = (k % slots) * 2
        gnorm_s[...] += dot_nn(gsrc_low, wbuf[slot]) + dot_nn(ggate_s[:, lane_chunk(k)], wbuf[slot + 1])

        @pl.when(k + slots < chunks)
        def _():
            win_in(k + slots, 0).start()
            win_in(k + slots, 1).start()

        some(late, k, chunks)

    gtok, prod = norm_back(tok_ref[...].astype(F32), row_of(gain_ref), gnorm_s[...])
    put_flat(0, jnp.sum(prod, axis=0, keepdims=True))
    gtok_ref[...] = gtok + gmid_s[...]
    end_out(1, 0)
    if nz:
        s_pick.result(pick_s)
        picked = pick_s[...]
    else:
        picked = picked_ref[...]
    two = chosen * jnp.where(valid, picked, 0.0)
    result = middle_ref[...] + two
    result_ref[...] = result.astype(LOW)
    squares = jnp.where(valid, result * result, 0.0)
    lane1 = lane_iota((1, LANES))
    stats = jnp.where(lane1 == 0, jnp.sum(squares), 0.0)
    stats = jnp.where(lane1 == 1, sum_ref[0:1, :], stats)
    stats = jnp.where(lane1 == 2, jnp.sum(two * two), stats)
    stats = jnp.where(lane1 == 3, count_ref[0].astype(F32), stats)
    flat_ref[(2 + experts) * pieces : (2 + experts) * pieces + 1, :] = stats
    if nz:
        s_out.result(home_ref)
        s_out.finish()
        s_pick.finish()
        exchange.wait()


VMEM = pltpu.VMEM
SMEM_SPEC = pl.BlockSpec(memory_space=pltpu.SMEM)
VMEM_SPEC = pl.BlockSpec(memory_space=pltpu.VMEM)


def shape_of(shape, dtype):
    return jax.ShapeDtypeStruct(shape, dtype)


def forward_outs(sm, rows, width, inner):
    return (
        shape_of((rows, width), LOW),
        shape_of((rows, inner), F32),
        shape_of((rows, inner), F32),
        shape_of((rows, inner), F32),
        shape_of((rows, inner), F32),
        shape_of((rows, LANES), F32),
        shape_of((rows, inner), LOW),
        shape_of((rows, width), F32),
        shape_of((rows, width), LOW),
        shape_of((8, LANES), F32),
    )


def forward_scratch(sm, rows, inner):
    st = sm.states
    return [
        VMEM((rows, inner), F32),
        VMEM((rows, CH), F32),
        VMEM((rows, CH), F32),
        VMEM((rows * st, LANES), F32),
        VMEM((rows * st, LANES), F32),
        VMEM((CH // LANES, rows * 8, LANES), F32),
    ]


def mixer_forward(sm, lens, count, tokens, gain, gain2, win, small, wout):
    rows, width = tokens.shape
    inner = wout.shape[0]
    return pl.pallas_call(
        partial(mixer_forward_kernel, sm, inner),
        out_shape=forward_outs(sm, rows, width, inner),
        in_specs=[SMEM_SPEC] * 2 + [VMEM_SPEC] * 6,
        out_specs=(VMEM_SPEC,) * 10,
        scratch_shapes=forward_scratch(sm, rows, inner),
        compiler_params=pltpu.CompilerParams(vmem_limit_bytes=60 << 20),
        name="mixer_forward",
    )(lens, count, tokens, gain, gain2, win, small, wout)


def flat_rows(width, experts):
    return -(-((2 + experts) * (width // LANES) + 1) // 8) * 8


MESH = pl.DeviceIdType.MESH


class Place:
    def __init__(self, nz):
        self.nz = nz
        w, n = lax.axis_index("wide"), lax.axis_index("narrow")
        self.z, self.y, self.x, self.c = w // 2, w % 2, n // 2, n % 2

    def flips(self, f2, f3):
        fx = f2 * (1 - self.c) + f3 * self.c
        fy = f3 * (1 - self.c) + f2 * self.c
        return self.x + fx - 2 * self.x * fx, self.y + fy - 2 * self.y * fy

    def device(self, z, f2, f3, fc):
        x, y = self.flips(f2, f3)
        core = 1 - self.c if fc else self.c
        return (z * 2 + y, x * 2 + core)

    def target(self, kind):
        if kind == "sib":
            return self.device(self.z, 0, 0, 1)
        if kind == "d2":
            return self.device(self.z, 1, 0, 0)
        if kind == "d3":
            return self.device(self.z, 0, 1, 0)
        if kind == "far":
            return self.device((self.z + self.nz // 2) % self.nz, 0, 0, 0)
        return self.device(self.z + kind, 0, 0, 0)

    def block(self, zloc, f2, f3, fc):
        x, y = self.flips(f2, f3)
        return zloc * 8 + y * 4 + x * 2 + self.c + fc - 2 * fc * self.c

    def has(self, side, group):
        at = self.z % group + side
        return (at >= 0) & (at < group)

    def barrier(self, far=0):
        sem = pltpu.get_barrier_semaphore()
        for kind in ("sib", "d2", "d3") + (("far",) if far else ()):
            pl.semaphore_signal(sem, inc=1, device_id=self.target(kind), device_id_type=MESH)
        for side in (-1, 1):
            @pl.when(self.has(side, self.nz))
            def _():
                pl.semaphore_signal(sem, inc=1, device_id=self.target(side), device_id_type=MESH)
        below = (self.z + self.nz - 1) // self.nz
        above = (2 * self.nz - 2 - self.z) // self.nz
        pl.semaphore_wait(sem, 3 + far + below + above)


def when(cond, body):
    if cond is True:
        body()
    else:
        pl.when(cond)(body)


class Gather:
    def __init__(self, place, src, out, send, recv, local, group):
        self.place, self.src, self.out, self.send, self.recv, self.local, self.group = place, src, out, send, recv, local, group
        self.rows = src.shape[0]
        self.slots = 0
        self.sent = []

    def at(self, p):
        return self.out.at[pl.ds(pl.multiple_of(p * self.rows, 8), self.rows), :]

    def copy(self, src, p, kind, slot):
        return pltpu.make_async_remote_copy(
            src, self.at(p), self.send.at[slot], self.recv.at[p], device_id=self.place.target(kind), device_id_type=MESH
        )

    def push(self, rel, kinds):
        for kind in kinds:
            slot = self.slots
            self.slots += 1
            self.sent.append((rel, kind, slot))

            def go(kind=kind, slot=slot):
                p, src = self.source(rel)
                self.copy(src, p, kind, slot).start()

            when(self.extra(kind), go)

    def extra(self, kind):
        return True if isinstance(kind, str) else self.place.has(kind, self.group)

    def source(self, rel):
        zloc = self.place.z % self.group
        if rel is None:
            return self.place.block(zloc, 0, 0, 0), self.src
        p = self.place.block(zloc + rel[0], rel[1], rel[2], 0)
        return p, self.at(p)

    def begin(self):
        p, src = self.source(None)
        self.push(None, [-1, 1, "d2", "d3", "sib"])
        pltpu.make_async_copy(src, self.at(p), self.local).start()

    def begin_z(self):
        self.push(None, [-1, 1])

    def handle_z(self, dist):
        def body():
            self.wait_block(self.place.block(self.place.z % self.group + dist, 0, 0, 0))
            self.push((dist, 0, 0), [1 if dist < 0 else -1])

        when(self.place.has(dist, self.group), body)

    def begin_xy(self):
        p, src = self.source(None)
        self.push(None, ["d2", "d3", "sib"])
        pltpu.make_async_copy(src, self.at(p), self.local).start()

    def pass_on(self, dist):
        def body():
            self.push((dist, 0, 0), ["d2", "d3", "sib"])

        when(self.place.has(dist, self.group), body)

    def wait_block(self, p):
        self.copy(self.src, p, "sib", 0).wait_recv()

    def events(self):
        out = []
        for dist in range(-self.group + 1, self.group):
            for f2 in (0, 1):
                for f3 in (0, 1):
                    if dist or f2 or f3:
                        out.append((abs(dist) + f2 + 2 * f3, dist, f2, f3))
        return sorted(out)

    def handle(self, dist, f2, f3):
        zloc = self.place.z % self.group
        cond = True if dist == 0 else self.place.has(dist, self.group)
        kinds = ["sib"]
        if not f3:
            kinds = ["d3"] + kinds
            if not f2:
                kinds = [1 if dist < 0 else -1, "d2"] + kinds

        def body():
            self.wait_block(self.place.block(zloc + dist, f2, f3, 0))
            self.push((dist, f2, f3), kinds)

        when(cond, body)

    def own_wait(self):
        p, src = self.source(None)
        pltpu.make_async_copy(src, self.at(p), self.local).wait()

    def finish(self):
        self.own_wait()
        for f2 in (0, 1):
            for f3 in (0, 1):
                for z in range(self.group):
                    self.wait_block(self.place.block(z, f2, f3, 1))
        self.finish_sends()

    def finish_sends(self):
        for rel, kind, slot in self.sent:
            def end(rel=rel, kind=kind, slot=slot):
                def inner():
                    p, src = self.source(rel)
                    self.copy(src, p, kind, slot).wait_send()

                when(self.extra(kind), inner)

            when(True if rel is None or not rel[0] else self.place.has(rel[0], self.group), end)

    @staticmethod
    def sends(group):
        return 5 + sum(2 + (not f3) + 2 * ((not f3) and (not f2)) for d in range(-group + 1, group) for f2 in (0, 1) for f3 in (0, 1))


def run_gathers(gathers):
    for g in gathers:
        g.begin()
    events = []
    for i, g in enumerate(gathers):
        events += [(e[0], i) + e[1:] for e in g.events()]
    for _, i, dist, f2, f3 in sorted(events):
        gathers[i].handle(dist, f2, f3)
    for g in gathers:
        g.finish()


class Exchange:
    parts = 3

    def __init__(self, place, src, out, sems):
        rows = src.shape[0] // self.parts
        assert rows % 8 == 0
        self.copies = [
            pltpu.make_async_remote_copy(
                src.at[pl.ds(i * rows, rows), :], out.at[pl.ds(i * rows, rows), :], sems.at[0, i], sems.at[1, i],
                device_id=place.target("far"), device_id_type=MESH,
            )
            for i in range(self.parts)
        ]

    def start(self, i):
        self.copies[i].start()

    def wait(self):
        for copy in self.copies:
            copy.wait()


class Scatter:
    def __init__(self, place, src, acc, rsib, rd3, rd2, rz, send, recv, local, group):
        self.place, self.src, self.acc = place, src, acc
        self.rows = rsib.shape[1]
        self.rsib, self.rd3, self.rd2, self.rz = rsib, rd3, rd2, rz
        self.send, self.recv, self.local, self.group = send, recv, local, group
        z = place.z % group
        self.zloc = z
        if group == 2:
            self.order = [(1 - z, 1 - 2 * z)]
        else:
            h, low = z // 2, z % 2
            self.order = [(3 * (1 - h), 1 - 2 * h), (2 - h, 1 - 2 * h), (2 * h + 1 - low, 1 - 2 * low)]
        self.dests = [zz for zz, _ in self.order] + [z]

    def copy(self, src, dst, send, recv, target):
        return pltpu.make_async_remote_copy(
            src, dst, self.send.at[send], self.recv.at[recv], device_id=target, device_id_type=MESH
        )

    def part(self, p):
        if len(self.src.shape) == 3:
            return self.src.at[p]
        return self.src.at[pl.ds(pl.multiple_of(p * self.rows, 8), self.rows), :]

    def sum(self, zz, f2, f3):
        if self.acc is None:
            return self.part(self.place.block(zz, f2, f3, 0))
        return self.acc.at[zz * 4 + f2 * 2 + f3]

    def to_sib(self, k, f2, f3):
        at = self.dests[k] * 4 + f3 * 2 + f2
        src = self.part(self.place.block(self.dests[k], f2, f3, 1))
        return self.copy(src, self.rsib.at[at], k * 4 + f2 * 2 + f3, at, self.place.target("sib"))

    def to_d3(self, k, f2):
        zz, group = self.dests[k], self.group
        row = 4 * group + k * 2 + f2
        return self.copy(
            self.sum(zz, f2, 1), self.rd3.at[zz * 2 + f2], row, 4 * group + zz * 2 + f2, self.place.target("d3")
        )

    def to_d2(self, k):
        zz, group = self.dests[k], self.group
        return self.copy(self.sum(zz, 1, 0), self.rd2.at[zz], 6 * group + k, 6 * group + zz, self.place.target("d2"))

    def zrow(self, zz, side):
        return zz + self.group * (1 + side) // 2

    def to_z(self, k):
        zz, side = self.order[k]
        row = self.zrow(zz, side)
        return self.copy(self.sum(zz, 0, 0), self.rz.at[row], 7 * self.group + k, 7 * self.group + row, self.place.target(side))

    def received(self, ref, row):
        pltpu.make_async_remote_copy(
            ref, ref, self.send.at[0], self.recv.at[row], device_id=self.place.target("sib"), device_id_type=MESH
        ).wait_recv()
        return ref

    def from_z(self, zz, side):
        row = self.zrow(zz, side)
        return self.received(self.rz.at[row], 7 * self.group + row)

    def local_copy(self, k, f2, f3):
        return pltpu.make_async_copy(
            self.part(self.place.block(self.dests[k], f2, f3, 0)),
            self.sum(self.dests[k], f2, f3),
            self.local.at[k * 4 + f2 * 2 + f3],
        )

    def begin(self):
        for k in range(self.group):
            for f2, f3 in ((1, 1), (1, 0), (0, 1), (0, 0)):
                self.to_sib(k, f2, f3).start()
            if self.acc is not None:
                for f2, f3 in ((1, 1), (0, 1), (1, 0), (0, 0)):
                    self.local_copy(k, f2, f3).start()

    def add(self, acc, ref):
        @pl.loop(0, ref.shape[-1] // LANES)
        def _(i):
            lanes = pl.ds(pl.multiple_of(i * LANES, LANES), LANES)
            acc[:, lanes] = acc[:, lanes] + ref[:, lanes]

    def own(self, k, f2, f3):
        at = self.dests[k] * 4 + f2 * 2 + f3
        if self.acc is not None:
            self.local_copy(k, f2, f3).wait()
        acc = self.sum(self.dests[k], f2, f3)
        self.add(acc, self.received(self.rsib.at[at], at))
        return acc

    def step_a(self, k):
        for f2 in (1, 0):
            self.own(k, f2, 1)
            self.to_d3(k, f2).start()

    def add_d3(self, k, f2, at):
        row = self.dests[k] * 2 + f2
        self.add(at, self.received(self.rd3.at[row], 4 * self.group + row))

    def step_b(self, k):
        at = self.own(k, 1, 0)
        self.add_d3(k, 1, at)
        self.to_d2(k).start()

    def step_c(self, k):
        at = self.own(k, 0, 0)
        self.add_d3(k, 0, at)
        zz = self.dests[k]
        self.add(at, self.received(self.rd2.at[zz], 6 * self.group + zz))
        if k < self.group - 1:
            side = self.order[k][1]

            @pl.when(self.place.has(-side, self.group))
            def _():
                self.add(at, self.from_z(zz, side))

            self.to_z(k).start()

    def result(self, out):
        out[...] = self.sum(self.zloc, 0, 0)[...].astype(out.dtype)
        for side in (-1, 1):
            @pl.when(self.place.has(side, self.group))
            def _():
                out[...] += self.from_z(self.zloc, -side)[...].astype(out.dtype)

    def steps(self):
        out = []
        for k in range(self.group):
            out += [(3 * k, self.step_a, k), (3 * k + 4, self.step_b, k), (3 * k + 8, self.step_c, k)]
        return sorted(out, key=lambda e: e[0])

    def finish(self):
        for k in range(self.group):
            for f2 in (0, 1):
                for f3 in (0, 1):
                    self.to_sib(k, f2, f3).wait_send()
                self.to_d3(k, f2).wait_send()
            self.to_d2(k).wait_send()
            if k < self.group - 1:
                self.to_z(k).wait_send()

    @staticmethod
    def scratch(group, rows, cols, dtype, in_place=False):
        return [
            VMEM((8, LANES) if in_place else (4 * group, rows, cols), dtype),
            VMEM((4 * group, rows, cols), dtype),
            VMEM((2 * group, rows, cols), dtype),
            VMEM((group, rows, cols), dtype),
            VMEM((2 * group, rows, cols), dtype),
            pltpu.SemaphoreType.DMA((8 * group,)),
            pltpu.SemaphoreType.DMA((9 * group,)),
            pltpu.SemaphoreType.DMA((4 * group,)),
        ]


ORDERS = (("z", "x", "y"), ("x", "y", "z"), ("y", "z", "x"))


class Cube:
    def __init__(self, place, order):
        self.place, self.order = place, order

    def flip(self, rel):
        at = dict(zip(self.order, rel))
        return at["z"], at["x"], at["y"]

    def target(self, i):
        place = self.place
        if i == 3:
            return place.device(place.z, 0, 0, 1)
        fz, fx, fy = self.flip([int(i == j) for j in range(3)])
        z = place.z + fz * (1 - 2 * (place.z % 2))
        return (z * 2 + place.y + fy * (1 - 2 * place.y), (place.x + fx * (1 - 2 * place.x)) * 2 + place.c)

    def block(self, rel, fc):
        place = self.place
        fz, fx, fy = self.flip(rel)
        z = place.z % 2
        at = [v + f * (1 - 2 * v) for v, f in ((z, fz), (place.y, fy), (place.x, fx), (place.c, fc))]
        return at[0] * 8 + at[1] * 4 + at[2] * 2 + at[3]


RELS = [(f1, f2, f3) for f1 in (0, 1) for f2 in (0, 1) for f3 in (0, 1)]


class CubeGather(Cube):
    def __init__(self, place, order, src, out, cols, send, recv, local):
        super().__init__(place, order)
        self.src, self.out, self.cols = src, out, cols
        self.send, self.recv, self.local = send, recv, local
        self.rows = src.shape[0]
        self.slots = []

    def at(self, p):
        return self.out.at[pl.ds(pl.multiple_of(p * self.rows, 8), self.rows), self.cols]

    def copy(self, rel, i, slot):
        p = self.block(rel, 0)
        src = self.at(p) if any(rel) else self.src.at[:, self.cols]
        return pltpu.make_async_remote_copy(
            src, self.at(p), self.send.at[slot], self.recv.at[p], device_id=self.target(i), device_id_type=MESH
        )

    def push(self, rel):
        last = max([i for i in range(3) if rel[i]], default=-1)
        for i in list(range(last + 1, 3)) + [3]:
            self.copy(rel, i, len(self.slots)).start()
            self.slots.append((rel, i))

    def local_copy(self):
        return pltpu.make_async_copy(self.src.at[:, self.cols], self.at(self.block((0, 0, 0), 0)), self.local)

    def begin(self):
        self.push((0, 0, 0))
        self.local_copy().start()

    def wait_block(self, rel, fc):
        here = self.at(self.block(rel, fc))
        pltpu.make_async_remote_copy(
            here, here, self.send.at[0], self.recv.at[self.block(rel, fc)], device_id=self.target(3), device_id_type=MESH
        ).wait_recv()

    def handle(self, rel):
        self.wait_block(rel, 0)
        self.push(rel)

    def finish_sends(self):
        for slot, (rel, i) in enumerate(self.slots):
            self.copy(rel, i, slot).wait_send()

    @staticmethod
    def scratch():
        return [pltpu.SemaphoreType.DMA((15,)), pltpu.SemaphoreType.DMA((16,)), pltpu.SemaphoreType.DMA]


class CubeScatter(Cube):
    def __init__(self, place, order, src, cols, acc, rsib, r3, r2, r1, send, recv, local):
        super().__init__(place, order)
        self.src, self.cols, self.acc = src, cols, acc
        self.rsib, self.r3, self.r2, self.r1 = rsib, r3, r2, r1
        self.send, self.recv, self.local = send, recv, local
        self.rows = rsib.shape[1]

    def part(self, p):
        if len(self.src.shape) == 3:
            return self.src.at[p, :, self.cols]
        return self.src.at[pl.ds(pl.multiple_of(p * self.rows, 8), self.rows), self.cols]

    def sum(self, rel):
        if self.acc is None:
            return self.part(self.block(rel, 0))
        return self.acc.at[rel[0] * 4 + rel[1] * 2 + rel[2]]

    def copy(self, src, dst, slot, i):
        return pltpu.make_async_remote_copy(
            src, dst, self.send.at[slot], self.recv.at[slot], device_id=self.target(i), device_id_type=MESH
        )

    def to_sib(self, rel):
        at = rel[0] * 4 + rel[1] * 2 + rel[2]
        return self.copy(self.part(self.block(rel, 1)), self.rsib.at[at], at, 3)

    def onward(self, rel):
        if rel[2]:
            at = rel[0] * 2 + rel[1]
            return self.copy(self.sum(rel), self.r3.at[at], 8 + at, 2)
        if rel[1]:
            return self.copy(self.sum(rel), self.r2.at[rel[0]], 12 + rel[0], 1)
        return self.copy(self.sum(rel), self.r1.at[0], 14, 0)

    def local_copy(self, rel):
        at = rel[0] * 4 + rel[1] * 2 + rel[2]
        return pltpu.make_async_copy(self.part(self.block(rel, 0)), self.acc.at[at], self.local.at[at])

    def begin(self):
        for rel in reversed(RELS):
            self.to_sib(rel).start()
        if self.acc is not None:
            for rel in reversed(RELS):
                self.local_copy(rel).start()

    def received(self, ref, slot):
        pltpu.make_async_remote_copy(
            ref, ref, self.send.at[0], self.recv.at[slot], device_id=self.target(3), device_id_type=MESH
        ).wait_recv()
        return ref

    def add(self, acc, ref):
        @pl.loop(0, ref.shape[-1] // LANES)
        def _(i):
            lanes = pl.ds(pl.multiple_of(i * LANES, LANES), LANES)
            acc[:, lanes] = acc[:, lanes] + ref[:, lanes]

    def step(self, rel):
        at = rel[0] * 4 + rel[1] * 2 + rel[2]
        if self.acc is not None:
            self.local_copy(rel).wait()
        acc = self.sum(rel)
        self.add(acc, self.received(self.rsib.at[at], at))
        if not rel[2]:
            row = rel[0] * 2 + rel[1]
            self.add(acc, self.received(self.r3.at[row], 8 + row))
            if not rel[1]:
                self.add(acc, self.received(self.r2.at[rel[0]], 12 + rel[0]))
                if not rel[0]:
                    self.add(acc, self.received(self.r1.at[0], 14))
        if any(rel):
            self.onward(rel).start()

    def result(self, out):
        out[:, self.cols] = self.sum((0, 0, 0))[...].astype(out.dtype)

    def finish(self):
        for rel in RELS:
            self.to_sib(rel).wait_send()
            if any(rel):
                self.onward(rel).wait_send()

    @staticmethod
    def scratch(rows, cols, dtype, in_place):
        return [
            VMEM((8, LANES) if in_place else (8, rows, cols), dtype),
            VMEM((8, rows, cols), dtype),
            VMEM((4, rows, cols), dtype),
            VMEM((2, rows, cols), dtype),
            VMEM((1, rows, cols), dtype),
            pltpu.SemaphoreType.DMA((15,)),
            pltpu.SemaphoreType.DMA((15,)),
            pltpu.SemaphoreType.DMA((8,)),
        ]


def thirds(width):
    step = width // 3
    return [pl.ds(i * step, step) for i in range(3)]


def run_scatters(scatters, outs, gathers=()):
    for g in gathers:
        g.begin()
    for s in scatters:
        s.begin()
    steps = []
    for i, s in enumerate(scatters):
        steps += [(t, i, step, k) for t, step, k in s.steps()]
    for _, _, step, k in sorted(steps, key=lambda e: e[:2]):
        step(k)
    for g in gathers:
        for _, dist, f2, f3 in g.events():
            g.handle(dist, f2, f3)
    for s, out in zip(scatters, outs):
        s.result(out)
    for s in scatters:
        s.finish()
    for g in gathers:
        g.finish()


ANY_SPEC = pl.BlockSpec(memory_space=pl.ANY)


def gather_scratch(group):
    return [
        pltpu.SemaphoreType.DMA((Gather.sends(group),)),
        pltpu.SemaphoreType.DMA((group * 8,)),
        pltpu.SemaphoreType.DMA,
    ]


def gather_kernel(nz, groups, *refs):
    n = len(groups)
    srcs, outs, scr = refs[:n], refs[n : 2 * n], refs[2 * n :]
    place = Place(nz)
    place.barrier()
    run_gathers(
        [Gather(place, srcs[i], outs[i], *scr[3 * i : 3 * i + 3], groups[i]) for i in range(n)]
    )


def gather_call(nz, groups, arrays, collective_id):
    return pl.pallas_call(
        partial(gather_kernel, nz, groups),
        out_shape=tuple(shape_of((g * 8 * a.shape[0], a.shape[1]), a.dtype) for g, a in zip(groups, arrays)),
        in_specs=[ANY_SPEC] * len(arrays),
        out_specs=(ANY_SPEC,) * len(arrays),
        scratch_shapes=sum([gather_scratch(g) for g in groups], []),
        compiler_params=pltpu.CompilerParams(collective_id=collective_id, has_side_effects=True, vmem_limit_bytes=60 << 20),
        name="gather_blocks",
    )(*arrays)


def scatter_kernel(nz, groups, gathered, *refs):
    n = len(groups)
    g = len(gathered)
    srcs, gsrcs, outs, gouts, scr = refs[:n], refs[n : n + g], refs[n + g : 2 * n + g], refs[2 * n + g : 2 * n + 2 * g], refs[2 * n + 2 * g :]
    place = Place(nz)
    place.barrier()
    scatters = [Scatter(place, srcs[i], *scr[8 * i : 8 * i + 8], groups[i]) for i in range(n)]
    more = scr[8 * n :]
    gathers = [Gather(place, gsrcs[i], gouts[i], *more[3 * i : 3 * i + 3], gathered[i]) for i in range(g)]
    run_scatters(scatters, outs, gathers)


def scatter_call(nz, groups, arrays, gathered, garrays, collective_id):
    return pl.pallas_call(
        partial(scatter_kernel, nz, groups, gathered),
        out_shape=tuple(shape_of((a.shape[0] // (8 * g), a.shape[1]), F32) for g, a in zip(groups, arrays))
        + tuple(shape_of((g * 8 * a.shape[0], a.shape[1]), a.dtype) for g, a in zip(gathered, garrays)),
        in_specs=[ANY_SPEC] * (len(arrays) + len(garrays)),
        out_specs=(VMEM_SPEC,) * len(arrays) + (ANY_SPEC,) * len(garrays),
        scratch_shapes=sum([Scatter.scratch(g, a.shape[0] // (8 * g), a.shape[1], a.dtype) for g, a in zip(groups, arrays)], [])
        + sum([gather_scratch(g) for g in gathered], []),
        compiler_params=pltpu.CompilerParams(collective_id=collective_id, has_side_effects=True, vmem_limit_bytes=60 << 20),
        name="scatter_blocks",
    )(*arrays, *garrays)


FAR_AT = 5.0


def forward_gather_kernel(sm, inner, nz, lens_ref, count_ref, tok_ref, gain_ref, gain2_ref, *refs):
    (win_src, wout_src, up_ref, down_ref, wx_ref, wdt_ref, alog_ref, convw_ref, convb_ref, rate_ref, skip_ref) = refs[:11]
    outs, alls, other, odown, refs = refs[11:21], refs[21:24], refs[24], refs[25], refs[26:]
    win_v, small_v, wout_v, load, small_src, turned = refs[:6]
    fwd_scratch, far, far_down, sems = refs[6:12], refs[12], refs[13], refs[14:]
    here = small_src.shape[0]
    srcs = (win_src, small_src, wout_src)
    place = Place(nz)
    f = Forward(sm, inner, lens_ref, count_ref, tok_ref, gain_ref, gain2_ref, win_v, small_v, wout_v, outs, fwd_scratch)
    place.barrier(1)
    exchange = Exchange(place, up_ref, other, far)
    more = Exchange(place, down_ref.at[pl.ds(0, DOWN_FIRST), :], odown, far_down)
    g_win, g_small, g_wout = (Gather(place, srcs[i], alls[i], *sems[3 * i : 3 * i + 3], nz) for i in range(3))
    win_hbm, small_hbm, wout_hbm = alls
    g_win.begin()
    turned[...] = jnp.zeros_like(turned)
    for at, ref in ((0, wdt_ref), (sm.alog, alog_ref), (sm.conv, convw_ref), (sm.bias, convb_ref), (sm.rate, rate_ref), (sm.skip, skip_ref)):
        turned[at : at + ref.shape[0], 0:here] = ref[...].astype(F32)
    small_src[:, 0:LANES] = jnp.zeros((here, LANES), LOW)
    small_src[:, 0 : wx_ref.shape[1]] = wx_ref[...]
    small_src[:, LANES : 2 * LANES] = jnp.transpose(turned[...])[0:here, :].astype(LOW)
    g_small.begin()
    g_wout.begin_z()
    f.start()
    events = []
    for i, g in enumerate((g_small, g_win)):
        events += [(e[0], i, partial(g.handle, *e[1:])) for e in g.events()]
    span = nz - 1
    for dist in range(1, nz):
        for side in (-1, 1):
            events.append((span + dist / 2, 2, partial(g_wout.handle_z, side * dist)))
    for i in range(Exchange.parts):
        events.append((FAR_AT, 3, partial(exchange.start, i)))
        events.append((FAR_AT, 3.5, partial(more.start, i)))
    events.append((span + 2, 4, g_wout.begin_xy))
    for _, _, event in sorted(events, key=lambda e: e[:2]):
        event()
    g_small.finish()
    small_in = pltpu.make_async_copy(small_hbm, small_v, load.at[0])
    small_in.start()
    g_win.finish()

    def win_in(k, half):
        rows = row_chunk(k, half * inner)
        return pltpu.make_async_copy(win_hbm.at[rows, :], win_v.at[rows, :], load.at[2 + 2 * k + half])

    for k in range(f.chunks):
        win_in(k, 0).start()
        win_in(k, 1).start()
    small_in.wait()
    near = sorted(((abs(d), d) for d in range(1 - nz, nz) if d))
    todo = [partial(g_wout.pass_on, d) for _, d in near]
    todo += [partial(g_wout.handle, *e[1:]) for e in g_wout.events() if e[2] or e[3]]
    split = len(todo) // 2
    first, second = todo[:split], todo[split:]

    @pl.loop(0, f.chunks)
    def _(k):
        win_in(k, 0).wait()
        win_in(k, 1).wait()
        f.project(k)
        some(first, k, f.chunks)

    f.spread()

    @pl.loop(0, f.chunks)
    def _(k):
        f.scan(k)
        some(second, k, f.chunks)

    g_wout.finish()
    wout_in = pltpu.make_async_copy(wout_hbm, wout_v, load.at[1])
    wout_in.start()
    wout_in.wait()
    f.end()
    exchange.wait()
    more.wait()


def forward_gather(sm, nz, lens, count, tokens, gain, gain2, win, wout, up, down, smalls, collective_id):
    rows, width = tokens.shape
    devices = 8 * nz
    inner = wout.shape[0] * devices
    here = wout.shape[0]
    alls = (shape_of((2 * inner, width), LOW), shape_of((inner, 2 * LANES), LOW), shape_of((inner, width), LOW))
    return pl.pallas_call(
        partial(forward_gather_kernel, sm, inner, nz),
        out_shape=forward_outs(sm, rows, width, inner) + alls + (shape_of(up.shape, up.dtype), shape_of((DOWN_FIRST, width), LOW)),
        in_specs=[SMEM_SPEC] * 2 + [VMEM_SPEC] * 3 + [ANY_SPEC] * 4 + [VMEM_SPEC] * 7,
        out_specs=(VMEM_SPEC,) * 10 + (ANY_SPEC,) * 5,
        scratch_shapes=[VMEM(a.shape, a.dtype) for a in alls[:3]]
        + [pltpu.SemaphoreType.DMA((2 + 2 * (inner // CH),)), VMEM((here, 2 * LANES), LOW), VMEM((LANES, LANES), F32)]
        + forward_scratch(sm, rows, inner)
        + [pltpu.SemaphoreType.DMA((2, Exchange.parts))] * 2
        + sum([gather_scratch(g) for g in (nz, nz, nz)], []),
        compiler_params=pltpu.CompilerParams(collective_id=collective_id, has_side_effects=True, vmem_limit_bytes=62 << 20),
        name="forward_gather",
    )(lens, count, tokens, gain, gain2, win, wout, up, down, *smalls)


GELU_A = 0.7978845608028654
GELU_B = 0.044715


def gelu_parts(v):
    inside = GELU_A * (v + GELU_B * v * v * v)
    t = jnp.tanh(inside)
    slope = 0.5 * (1.0 + t) + 0.5 * v * (1.0 - t * t) * (GELU_A * (1.0 + 3.0 * GELU_B * v * v))
    return 0.5 * v * (1.0 + t), slope


DOWN_FIRST = 96


def expert_kernel(
    experts, nz, count_ref, moe_ref, gout_ref, ids_ref, up_ref, other_ref, down_ref, odown_ref, router_ref,
    picked_ref, gm_ref, gch_ref, gmine_ref, gother_ref,
    all_s, gall_s, call_s, code_s, wu_s, wd_s, gm_s, gch_s, go_s, gpre_s, hid_s, slope_s, hidden_s, far, *refs,
):
    group = 2
    rows, width = moe_ref.shape
    block = 2 * rows
    units = up_ref.shape[0]
    per = units // experts
    place = Place(nz)
    place.barrier(1)
    cuts = thirds(width)
    gather = [CubeGather(place, ORDERS[i], moe_ref, all_s, cuts[i], *refs[3 * i : 3 * i + 3]) for i in range(3)]
    refs = refs[9:]
    gouts = [CubeGather(place, ORDERS[i], gout_ref, gall_s, cuts[i], *refs[3 * i : 3 * i + 3]) for i in range(3)]
    refs = refs[9:]
    codes = [CubeGather(place, ORDERS[0], code_s, call_s, pl.ds(0, LANES), *refs[:3])]
    refs = refs[3:]
    left = units - DOWN_FIRST
    exchange = Exchange(place, down_ref.at[pl.ds(DOWN_FIRST, left), :], wd_s.at[pl.ds(units + DOWN_FIRST, left), :], far)
    grads = [CubeScatter(place, ORDERS[i], gm_s, cuts[i], None, *refs[8 * i + 1 : 8 * i + 8]) for i in range(3)]
    chosens = CubeScatter(place, ORDERS[0], gch_s, pl.ds(0, LANES), None, *refs[25:32])
    ids = ids_ref[...]
    code = jnp.where(lane_iota(ids.shape) < count_ref[0], ids, ids + experts).astype(F32)
    code_s[...] = jnp.broadcast_to(code, code_s.shape)
    for g in codes + gather + gouts:
        g.begin()
    for part in range(exchange.parts):
        exchange.start(part)
    wu_s[0:units, :] = up_ref[...]
    wu_s[units : 2 * units, :] = other_ref[...]
    wd_s[0:units, :] = down_ref[...]
    wd_s[units : units + DOWN_FIRST, :] = odown_ref[...]
    router = padded_router(router_ref)
    chips = [(i % 2, i // 2 % 2, i // 4) for i in range(8)]
    steps = {1: 1, 3: 2, 7: 3}
    zloc = place.z % group
    zfar = 1 - zloc

    def by_order(g, chip):
        at = dict(zip("zxy", chip))
        return tuple(at[d] for d in g.order)

    def arrive(gathers, i):
        for j, chip in enumerate(chips):
            @pl.when(i == j)
            def _():
                for g in gathers:
                    if j == 0:
                        g.local_copy().wait()
                if j in steps:
                    for near in chips:
                        if sum(near) == steps[j]:
                            for g in gathers:
                                g.handle(by_order(g, near))
                for g in gathers:
                    g.wait_block(by_order(g, chip), 1)

    def chip_of(i):
        fz, fx, fy = i % 2, (i // 2) % 2, i // 4
        at = [v + f * (1 - 2 * v) for v, f in ((zloc, fz), (place.y, fy), (place.x, fx))]
        return at[0] * 4 + at[1] * 2 + at[2]

    def masks(chip):
        parts = [column(call_s[pl.ds(pl.multiple_of(chip * 16 + 8 * c, 8), 8), :][0:1, :]) for c in range(2)]
        code = jnp.concatenate(parts, axis=0)
        expert = jnp.where(code < experts, code, code - experts)
        col = lane_iota((block, 2 * units))
        col = jnp.where(col >= units, col - units, col).astype(F32)
        return code, expert, (col >= expert * per) & (col < (expert + 1.0) * per)

    @pl.loop(0, len(chips))
    def _(i):
        arrive(codes + gather, i)

        chip = chip_of(i)
        at = pl.ds(pl.multiple_of(chip * block, block), block)
        _, _, mask = masks(chip)
        act, slope = gelu_parts(dot_nt(all_s[at, :], wu_s[...]))
        hidden = jnp.where(mask, act, 0.0).astype(LOW)
        hidden_s[at, :] = hidden
        slope_s[at, :] = jnp.where(mask, slope, 0.0)
        lanes = pl.ds(pl.multiple_of(chip * block, block), block)
        hid_s[:, lanes] = jnp.transpose(hidden)

    exchange.wait()

    @pl.loop(0, len(chips))
    def _(i):
        arrive(gouts, i)
        chip = chip_of(i)
        at = pl.ds(pl.multiple_of(chip * block, block), block)
        code, expert, _ = masks(chip)
        hidden = hidden_s[at, :]
        picked_ref[at, :] = dot_nn(hidden, wd_s[...]).astype(LOW)
        _, _, chosen = route(all_s[at, :], router, expert, experts)
        scale = jnp.where(code < experts, chosen, 0.0)
        g = gall_s[at, :]
        back = dot_nt(g, wd_s[...])
        gch = jnp.sum(hidden.astype(F32) * back, axis=1, keepdims=True)
        gpre = (scale * back * slope_s[at, :]).astype(LOW)
        gm = dot_nn(gpre, wu_s[...]).astype(LOW)
        for c in range(2):
            gm_s[2 * chip + c] = gm[c * rows : (c + 1) * rows, :]
            turned = jnp.transpose(jnp.broadcast_to(gch[c * rows : (c + 1) * rows, :], (rows, LANES)))
            gch_s[2 * chip + c] = turned[0:8, :]
        go_s[at, :] = (scale * g.astype(F32)).astype(LOW)
        lanes = pl.ds(pl.multiple_of(chip * block, block), block)
        gpre_s[:, lanes] = jnp.transpose(gpre)
        for j, at_chip in enumerate(chips):
            @pl.when(i == j)
            def _():
                for g in grads + [chosens]:
                    g.to_sib(by_order(g, at_chip)).start()

    def weights(j):
        half = 3
        left, right, base = (gpre_s, all_s, 0) if j < half else (hid_s, go_s, units)
        step = width // half
        at = slice((j % half) * step, (j % half + 1) * step)
        part = dot_nn(left[...], right[:, at])
        gmine_ref[base : base + units, at] = part[0:units, :]
        gother_ref[base : base + units, at] = part[units : 2 * units, :].astype(LOW)

    def sums(rels):
        for rel in rels:
            for g in grads:
                g.step(rel)

    first = [(1, 1, 1), (0, 1, 1), (1, 0, 1), (0, 0, 1)]
    sums(first)
    weights(0)
    for rel in first:
        chosens.step(rel)
    weights(1)
    weights(2)
    sums([(1, 1, 0)])
    weights(3)
    sums([(0, 1, 0)])
    chosens.step((1, 1, 0))
    chosens.step((0, 1, 0))
    weights(4)
    sums([(1, 0, 0)])
    chosens.step((1, 0, 0))
    weights(5)
    sums([(0, 0, 0)])
    chosens.step((0, 0, 0))
    for g in grads:
        g.result(gm_ref)
    chosens.result(gch_ref)
    for g in grads + [chosens]:
        g.finish()
    for g in codes + gather + gouts:
        g.finish_sends()


def expert_call(experts, nz, count, moe_in, gout, ids, up, other, down, odown, router, collective_id):
    rows, width = moe_in.shape
    tokens = rows * 16
    units = 2 * up.shape[0]
    return pl.pallas_call(
        partial(expert_kernel, experts, nz),
        out_shape=(
            shape_of((tokens, width), LOW),
            shape_of((rows, width), F32),
            shape_of((8, LANES), F32),
            shape_of((units, width), F32),
            shape_of((units, width), LOW),
        ),
        in_specs=[SMEM_SPEC] + [ANY_SPEC] * 2 + [VMEM_SPEC] * 6,
        out_specs=(VMEM_SPEC,) * 5,
        scratch_shapes=[
            VMEM((tokens, width), LOW),
            VMEM((tokens, width), LOW),
            VMEM((16 * 8, LANES), F32),
            VMEM((8, LANES), F32),
            VMEM((units, width), LOW),
            VMEM((units, width), LOW),
            VMEM((16, rows, width), LOW),
            VMEM((16, 8, LANES), F32),
            VMEM((tokens, width), LOW),
            VMEM((units, tokens), LOW),
            VMEM((units, tokens), LOW),
            VMEM((tokens, units), F32),
            VMEM((tokens, units), LOW),
            pltpu.SemaphoreType.DMA((2, Exchange.parts)),
        ]
        + CubeGather.scratch() * 7
        + CubeScatter.scratch(rows, width // 3, LOW, True) * 3
        + CubeScatter.scratch(8, LANES, F32, True),
        compiler_params=pltpu.CompilerParams(collective_id=collective_id, has_side_effects=True, vmem_limit_bytes=63 << 20),
        name="experts",
    )(count, moe_in, gout, ids, up, other, down, odown, router)


def mixer_backward(sm, experts, nz, lens, count, tokens, gain, small, gain2, saved, gm, gch, gout, ids, router, win, wout, picked, mine, collective_id):
    rows, width = tokens.shape
    inner = wout.shape[0]
    st = sm.states
    chunks = inner // CH
    here = inner // (8 * nz) if nz else 0
    return pl.pallas_call(
        partial(mixer_backward_kernel, sm, inner, experts, nz),
        out_shape=(
            shape_of((rows, width), LOW),
            shape_of((rows, width), F32),
            shape_of((flat_rows(width, experts), LANES), F32),
            shape_of((inner, 2 * LANES), LOW),
            shape_of((2 * inner, width), LOW),
            shape_of((inner, width), LOW),
        )
        + ((shape_of((here, width), F32), shape_of((mine.shape[0] // 2, width), mine.dtype)) if nz else ()),
        in_specs=[SMEM_SPEC] * 2 + [VMEM_SPEC] * 19 + [ANY_SPEC] * 2 + [ANY_SPEC if nz else VMEM_SPEC, ANY_SPEC],
        out_specs=(VMEM_SPEC,) * 4 + (ANY_SPEC,) * 2 + ((VMEM_SPEC, ANY_SPEC) if nz else ()),
        scratch_shapes=[
            VMEM((rows, width), F32),
            VMEM((rows, width), LOW),
            VMEM((rows, inner), LOW),
            VMEM((rows, inner), F32),
            VMEM((rows, inner), F32),
            VMEM((rows, CH), F32),
            VMEM((rows, CH), F32),
            VMEM((rows, CH), F32),
            VMEM((rows * st, LANES), F32),
            VMEM((rows * st, LANES), F32),
            VMEM(((rows + 1) * st, CH), F32),
            VMEM((rows * st, CH), F32),
            VMEM((rows * st, LANES), F32),
            VMEM((rows * st, LANES), F32),
            VMEM((CH // LANES, rows * 8, LANES), F32),
            VMEM((CH // LANES, rows * 8, LANES), F32),
            VMEM((rows, LANES), F32),
            VMEM((rows, width), F32),
            VMEM((rows, width), F32),
            VMEM((chunks, CH, width), LOW),
            VMEM((2, 2, CH, width), LOW),
            pltpu.SemaphoreType.DMA((chunks,)),
            pltpu.SemaphoreType.DMA((2, 2)),
        ]
        + (Scatter.scratch(nz, here, width, LOW) + Scatter.scratch(2, rows, width, LOW) + [pltpu.SemaphoreType.DMA((2, Exchange.parts))] if nz else []),
        compiler_params=pltpu.CompilerParams(
            collective_id=collective_id if nz else None, has_side_effects=bool(nz), vmem_limit_bytes=63 << 20
        ),
        name="mixer_backward",
    )(lens, count, tokens, gain, small, gain2, *saved, gm, gch, gout, ids, router, win, wout, picked, mine)


def last_kernel(nz, gwin_src, gsmall_src, flat_src, mine_ref, gwin_ref, gsmall_ref, total_ref, other_ref, flat_s, far, *refs):
    place = Place(nz)
    place.barrier(1)
    half = other_ref.shape[0]
    exchange = Exchange(place, mine_ref.at[pl.ds(half, half), :], other_ref, far)
    s_small = Scatter(place, gsmall_src, *refs[0:8], nz)
    s_win = Scatter(place, gwin_src, *refs[8:16], nz)
    g_flat = Gather(place, flat_src, flat_s, *refs[16:19], nz)
    s_win.begin()
    s_small.begin()
    g_flat.begin()
    for i in range(exchange.parts):
        exchange.start(i)
    steps = []
    for i, s in enumerate((s_win, s_small)):
        steps += [(t + i, i, step, k) for t, step, k in s.steps()]
    for i, (_, dist, f2, f3) in enumerate(g_flat.events()):
        steps.append((14 + i / 4, 2, lambda e: g_flat.handle(*e), (dist, f2, f3)))
    for _, _, step, k in sorted(steps, key=lambda e: e[:2]):
        step(k)
    g_flat.finish()
    count = flat_src.shape[0]
    total = flat_s[0:count, :]
    for i in range(1, 8 * nz):
        total = total + flat_s[i * count : (i + 1) * count, :]
    total_ref[...] = total
    s_small.result(gsmall_ref)
    s_win.result(gwin_ref)
    s_small.finish()
    s_win.finish()
    exchange.wait()


def last_call(nz, gwin, gsmall, flat, mine, collective_id):
    width = gwin.shape[1]
    devices = 8 * nz
    here = gsmall.shape[0] // devices
    rows = gwin.shape[0] // devices
    return pl.pallas_call(
        partial(last_kernel, nz),
        out_shape=(shape_of((rows, width), F32), shape_of((here, 2 * LANES), F32), shape_of(flat.shape, F32), shape_of((mine.shape[0] // 2, width), mine.dtype)),
        in_specs=[ANY_SPEC] * 4,
        out_specs=(VMEM_SPEC,) * 3 + (ANY_SPEC,),
        scratch_shapes=[VMEM((devices * flat.shape[0], LANES), F32), pltpu.SemaphoreType.DMA((2, Exchange.parts))]
        + Scatter.scratch(nz, here, 2 * LANES, LOW)
        + Scatter.scratch(nz, rows, width, LOW)
        + gather_scratch(nz),
        compiler_params=pltpu.CompilerParams(collective_id=collective_id, has_side_effects=True, vmem_limit_bytes=60 << 20),
        name="gradient_sums",
    )(gwin, gsmall, flat, mine)


def finish_kernel(
    sm, win_ref, small_ref, total_ref, mine_ref, oup_ref, odown_ref, res_ref, tok_ref, out_ref,
    gwin_ref, gwx_ref, gwdt_ref, galog_ref, gconvw_ref, gconvb_ref, grate_ref, gskip_ref, ggain_ref, ggain2_ref, grouter_ref, rms_ref,
    gup_ref, gdown_ref, result_ref, gtok_ref, gwout_ref,
):
    units = gup_ref.shape[0]
    here, width = out_ref.shape
    gup_ref[...] = mine_ref[0:units, :] + oup_ref[...].astype(F32)
    gdown_ref[...] = mine_ref[units : 2 * units, :] + odown_ref[...].astype(F32)
    result_ref[...] = res_ref[...]
    gtok_ref[...] = tok_ref[...]
    gwout_ref[...] = out_ref[...]
    gwin_ref[...] = win_ref[...]
    gwx_ref[...] = small_ref[:, 0 : gwx_ref.shape[1]]
    total = total_ref[...]
    pieces = width // LANES
    experts = grouter_ref.shape[0]
    row = lambda v, start: jnp.concatenate([v[start + i : start + i + 1, :] for i in range(pieces)], axis=1)
    ggain_ref[...] = row(total, 0).reshape(-1)
    ggain2_ref[...] = row(total, pieces).reshape(-1)
    for e in range(experts):
        grouter_ref[e : e + 1, :] = row(total, (2 + e) * pieces)
    at = (2 + experts) * pieces
    stats = total[at : at + 1, :]
    rms = jnp.sqrt(stats / (stats[:, 3:4] * width))
    lane = lane_iota(rms.shape)
    for i in range(3):
        rms_ref[i] = jnp.sum(jnp.where(lane == i, rms, 0.0))
    block = jnp.concatenate([small_ref[:, LANES : 2 * LANES], jnp.zeros((LANES - here, LANES), F32)], axis=0)
    turned = jnp.transpose(block)
    for at, ref in ((0, gwdt_ref), (sm.alog, galog_ref), (sm.conv, gconvw_ref), (sm.bias, gconvb_ref), (sm.rate, grate_ref), (sm.skip, gskip_ref)):
        ref[...] = turned[at : at + ref.shape[0], 0:here]


def finish_call(sm, experts, wx_cols, win, small, total, mine, oup, odown, result, gtok, gwout):
    here, width = gwout.shape
    half = mine.shape[0] // 2
    f = lambda *s: shape_of(s, F32)
    return pl.pallas_call(
        partial(finish_kernel, sm),
        out_shape=(
            f(*win.shape), f(here, wx_cols), f(sm.rank, here), f(sm.states, here), f(sm.taps, here), f(1, here), f(1, here),
            f(1, here), f(width), f(width), f(experts, width), f(3), f(half, width), f(half, width),
            shape_of(result.shape, result.dtype), f(*gtok.shape), f(*gwout.shape),
        ),
        in_specs=[VMEM_SPEC] * 9,
        out_specs=(VMEM_SPEC,) * 11 + (SMEM_SPEC,) + (VMEM_SPEC,) * 5,
        compiler_params=pltpu.CompilerParams(vmem_limit_bytes=60 << 20),
        name="finish",
    )(win, small, total, mine, oup, odown, result, gtok, gwout)


AXES = ("wide", "narrow")


def experts_local(moe_in, gout, ids, count, w_up, w_down, w_router, experts):
    rows = moe_in.shape[0]
    ups = lax.all_gather(w_up, AXES, axis=2, tiled=True)
    downs = lax.all_gather(w_down, AXES, axis=1, tiled=True)
    probs = jax.nn.softmax(jnp.dot(moe_in, w_router, preferred_element_type=F32), axis=-1)
    onehot = (ids[:, None] == jnp.arange(experts, dtype=jnp.int32)[None, :]).astype(F32)
    chosen = jnp.sum(probs * onehot, axis=-1, keepdims=True)
    live = jnp.arange(rows, dtype=jnp.int32)[:, None] < count[0]
    pre = jnp.einsum("td,edf->etf", moe_in, ups, preferred_element_type=F32)
    act, slope = gelu_parts(pre)
    hidden = act.astype(LOW)
    outs = jnp.einsum("etf,efd->etd", hidden, downs, preferred_element_type=F32)
    picked = jnp.sum(onehot.T[:, :, None] * outs, axis=0)
    scaled = (jnp.where(live, chosen, 0.0) * gout.astype(F32)).astype(LOW)
    grad_expert = onehot.T.astype(LOW)[:, :, None] * scaled[None]
    grad_down = jnp.einsum("etf,etd->fed", hidden, grad_expert, preferred_element_type=LOW)
    grad_act = jnp.einsum("etd,efd->etf", grad_expert, downs, preferred_element_type=F32)
    grad_pre = (grad_act * slope).astype(LOW)
    grad_up = jnp.einsum("td,etf->fed", moe_in, grad_pre, preferred_element_type=LOW)
    gm = jnp.einsum("etf,edf->td", grad_pre, ups, preferred_element_type=F32)
    scatter = partial(lax.psum_scatter, axis_name=AXES, scatter_dimension=0, tiled=True)
    gup = scatter(grad_up).astype(F32).transpose(1, 2, 0)
    gdown = scatter(grad_down).astype(F32).transpose(1, 0, 2)
    return picked, gm, gup, gdown


def per_device(
    nz, tokens, norm_gain, w_in, conv_w, conv_b, w_x, w_dt, dt_bias, a_log, d_skip, w_out, moe_gain, w_router, w_up,
    w_down, seq_lengths, valid_counts, expert_ids, out_grad,
):
    rows, width = tokens.shape
    sm = Small(w_dt.shape[0], a_log.shape[1], conv_w.shape[0])
    here = w_out.shape[0]
    experts, per = w_up.shape[0], w_up.shape[2]
    lens = seq_lengths[0]
    ids = expert_ids[None]
    router = w_router.T
    if nz:
        up = w_up.transpose(0, 2, 1).reshape(experts * per, width)
        down = w_down.reshape(experts * per, width)
        smalls = (w_x, w_dt, a_log.T, conv_w, conv_b[None], dt_bias[None], d_skip[None])
        *saved, win_all, small_all, wout_all, other, odown = forward_gather(
            sm, nz, lens, valid_counts, tokens, norm_gain, moe_gain, w_in.T, w_out, up, down, smalls, 0
        )
        picked, gm, gch, gmine, gother = expert_call(
            experts, nz, valid_counts, saved[8], out_grad, ids, up, other, down, odown, router, 1
        )
    else:
        small = jnp.concatenate(
            [
                w_x, jnp.zeros((here, LANES - w_x.shape[1]), LOW), w_dt.T, a_log, conv_w.T, conv_b[:, None],
                dt_bias[:, None], d_skip[:, None], jnp.zeros((here, LANES - sm.end), LOW),
            ],
            axis=1,
        )
        win_all = lax.all_gather(w_in.T, AXES, axis=0, tiled=True)
        rest_all = lax.all_gather(jnp.concatenate([w_out, small], axis=1), AXES, axis=0, tiled=True)
        wout_all, small_all = rest_all[:, :width], rest_all[:, width:]
        saved = mixer_forward(sm, lens, valid_counts, tokens, norm_gain, moe_gain, win_all, small_all, wout_all)
        picked, gm, gup, gdown = experts_local(saved[8], out_grad, expert_ids, valid_counts, w_up, w_down, w_router, experts)
        gch = jnp.zeros((8, LANES), F32)
        gother = gch
    result, gtok, flat, gsmall, gwin, gwout, *home = mixer_backward(
        sm, experts, nz, lens, valid_counts, tokens, norm_gain, small_all, moe_gain, saved, gm, gch, out_grad, ids, router,
        win_all, wout_all, picked, gother, 2,
    )
    if nz:
        gwin, gsmall, flat, gdown = last_call(nz, gwin, gsmall, flat, gother, 3)
        (
            gwin, gwx, gwdt, galog, gconvw, gconvb, grate, gskip, ggain, ggain2, grouter, rms, gup, gdown, result, gtok, gwout,
        ) = finish_call(sm, experts, w_x.shape[1], gwin, gsmall, flat, gmine, home[1], gdown, result, gtok, home[0])
        return (
            result, gtok, ggain, gwin.T, gconvw, gconvb[0], gwx, gwdt, grate[0], galog.T, gskip[0], gwout, ggain2,
            grouter.T, gup.reshape(experts, per, width).transpose(0, 2, 1), gdown.reshape(experts, per, width), rms,
        )
    scatter = partial(lax.psum_scatter, axis_name=AXES, scatter_dimension=0, tiled=True)
    gwin = scatter(gwin).astype(F32)
    gall = scatter(jnp.concatenate([gwout, gsmall], axis=1)).astype(F32)
    g1, g2 = gall[:, width : width + LANES], gall[:, width + LANES :]
    flat = lax.psum(flat, AXES).reshape(-1)
    ggain, ggain2, flat = flat[:width], flat[width : 2 * width], flat[2 * width :]
    grad_router, flat = flat[: width * experts].reshape(experts, width).T, flat[width * experts :]
    return (
        result, gtok, ggain, gwin.T, g2[:, sm.conv : sm.conv + sm.taps].T, g2[:, sm.bias], g1[:, : w_x.shape[1]],
        g2[:, : sm.rank].T, g2[:, sm.rate], g2[:, sm.alog : sm.alog + sm.states], g2[:, sm.skip], gall[:, :width],
        ggain2, grad_router, gup, gdown, jnp.sqrt(flat[:3] / (flat[3] * width)),
    )


def solution(mesh):
    wide, narrow = mesh.shape["wide"], mesh.shape["narrow"]
    nz = wide // 2 if narrow == 4 and wide == 8 else 0
    both = ("wide", "narrow")
    rows2, cols, one, rep = P(both, None), P(None, both), P(both), P()
    in_specs = (
        rows2, rep, cols, cols, one, rows2, cols, one, rows2, one, rows2, rep, rep, P(None, None, both),
        P(None, both, None), rows2, one, one, rows2,
    )
    out_specs = (
        rows2, rows2, rep, cols, cols, one, rows2, cols, one, rows2, one, rows2, rep, rep, P(None, None, both),
        P(None, both, None), rep,
    )
    return jax.shard_map(partial(per_device, nz), mesh=mesh, in_specs=in_specs, out_specs=out_specs, check_vma=False)
```
